32 devices in a mesh: dom: 4 (over y, x), edge: 8 (over z, core).
Axes of the slice: x: 2, y: 2, z: 4, core: 2. Of those that a mesh axis runs over, the one named last changes fastest.
Arguments:
- src_table: float32 [400, 16384], P(None, ('dom', 'edge')), may hold values from -2.5 to 2.5
- src_state: float32 [16384], P(('dom', 'edge')), may hold values from 0.001 to 1
- dst_table: float32 [400, 16384], P(None, ('dom', 'edge')), may hold values from -2.5 to 2.5
- dst_state: float32 [16384], P(('dom', 'edge')), may hold values from 0.001 to 1
- relation: float32 [400, 16], replicated, may hold values from -4 to 4
- edge_src: int32 [131072], P(('dom', 'edge')), may hold values from 0 to 511
- edge_dst: int32 [131072], P(('dom', 'edge')), may hold values from 0 to 511
- edge_rel: int32 [131072], P(('dom', 'edge')), may hold values from 0 to 15
- matching: int32 [4], replicated, may hold values from 0 to 3, as said below
- neg_rows: int32 [32, 8, 256], P(('dom', 'edge')), may hold values from 0 to 511
- quotas: int32 [32, 8], P(('dom', 'edge')), may hold values from 0 to 2, as said below
Outputs:
- src_out: float32 [400, 16384], P(None, ('dom', 'edge'))
- src_state_out: float32 [16384], P(('dom', 'edge'))
- dst_out: float32 [400, 16384], P(None, ('dom', 'edge'))
- dst_state_out: float32 [16384], P(('dom', 'edge'))
- relation_out: float32 [400, 16], replicated
The draws below stay inside these ranges and needn't reach their ends.
Inputs may be any that keep to these rules, and one draw needn't show every extreme that they name: matching names every partition exactly once. `quotas`: each device's 8 entries sum to exactly 12; for each index of dom, one index of edge is given 2 blocks by every device of that index of dom.
All inputs are finite; a program needn't handle non-finite values.
Results may differ from the reference program's by a relative error of at most 0.0011.
Values may be sent and summed in bfloat16 or wider, within the bound.
No kernel may reach another device: no remote copies, remote signals or barrier semaphores. Data moves between devices by JAX's collectives and lax.ppermute only.
A program may use at most 128 MiB of HBM per device.

```python
import math
import jax
import jax.numpy as jnp
import numpy as np
from jax import lax

DIM = 400
NREL = 16
ROWS_DEV = 512
E_DEV = 4096
BLOCK = 128
QMAX = 2
QTOTAL = 12
NNEG = 1536
SLOTS = 256
ROWS_ALL = 16384
EDGES_ALL = 131072
N_DOM = 4
N_EDGE = 8


def draw_matching(key, part):
    base_key = jax.random.fold_in(key, 11)
    shuffled = jax.random.permutation(jax.random.fold_in(base_key, 1), N_DOM).astype(jnp.int32)
    chosen = jax.random.randint(jax.random.fold_in(base_key, 2), (), 0, N_DOM, dtype=jnp.int32)
    target = ((chosen + N_DOM // 2) % N_DOM).astype(jnp.int32)
    places = jnp.arange(N_DOM, dtype=jnp.int32)
    where_target = jnp.sum(jnp.where(shuffled == target, places, 0)).astype(jnp.int32)
    held_value = jnp.sum(jnp.where(places == chosen, shuffled, 0)).astype(jnp.int32)
    result = jnp.where(places == chosen, target, jnp.where(places == where_target, held_value, shuffled))
    return result.astype(jnp.int32)


def draw_quotas(key, part):
    base_key = jax.random.fold_in(key, 23)
    heavy = jax.random.randint(jax.random.fold_in(base_key, 1), (N_DOM,), 0, N_EDGE, dtype=jnp.int32)
    row_keys = jax.random.split(jax.random.fold_in(base_key, 2), N_DOM * N_EDGE)
    shard_ids = jnp.arange(N_EDGE, dtype=jnp.int32)

    def one_device(row_key, dom_heavy):
        shuffled = jax.random.permutation(row_key, QMAX * (N_EDGE - 1)).astype(jnp.int32)
        chosen = shuffled[:QTOTAL - QMAX] // QMAX
        target = chosen + (chosen >= dom_heavy).astype(jnp.int32)
        counts = jnp.sum((target[:, None] == shard_ids[None, :]).astype(jnp.int32), axis=0)
        return (counts + QMAX * (shard_ids == dom_heavy).astype(jnp.int32)).astype(jnp.int32)
    return jax.vmap(one_device)(row_keys, jnp.repeat(heavy, N_EDGE)).astype(jnp.int32)


def plant(array, own_key, least, high):
    extent = array.shape
    place = [jax.random.randint(jax.random.fold_in(own_key, axis), (), 0, extent[axis]) for axis in range(len(extent))]
    array = array.at[tuple(place)].set(least)
    longest = extent.index(max(extent))
    place[longest] = (place[longest] + 1) % extent[longest]
    return array.at[tuple(place)].set(high)


def level_of(rng, shape, shards, low, largest):
    gain = 1.0
    for axis_at, shards_of in shards:
        steps = jax.random.uniform(jax.random.fold_in(jax.random.fold_in(rng, 6), axis_at), (shards_of,), jnp.float32, low / len(shards), largest / len(shards))
        gain = gain * jnp.repeat(jnp.exp(steps), shape[axis_at] // shards_of).reshape((-1,) + (1,) * (len(shape) - 1 - axis_at))
    return gain


def rank_bounds(amount, slope):
    weights = [(1 << 20) // math.isqrt(grade ** slope) + 1 for grade in range(1, amount + 1)]
    scale = 1 + sum(weights) // (1 << 30)
    return np.cumsum(np.array([max(1, weight // scale) for weight in weights]))


def ranked_ids(key, dims, amount, skew):
    listing = rank_bounds(amount, skew)
    ticket = jax.random.randint(jax.random.fold_in(key, 1), dims, 0, int(listing[amount - 1]))
    rank = jnp.searchsorted(jnp.asarray(listing, jnp.int32), ticket, side="right")
    return jax.random.permutation(jax.random.fold_in(key, 2), amount)[rank].astype(jnp.int32)


def normal_values(stream_key, shape, scale, limit, cuts=(), kind=jnp.bfloat16):
    loudness = level_of(stream_key, shape, cuts, -0.22, 0.18) if cuts else 1.0
    drawn = jax.random.normal(stream_key, shape, jnp.float32) * scale * loudness
    return jnp.minimum(jnp.maximum(drawn, -limit), limit).astype(kind)


def setup_inputs(seed: int = 0) -> dict:
    arg_keys = jax.random.split(jax.random.key(seed), 12)
    src_table = normal_values(arg_keys[0], (DIM, ROWS_ALL), 0.4, 2.5, ((1, 32),), jnp.float32)
    src_state = jnp.clip(jnp.exp(math.log(1.0) - 6.9077552 * jax.random.uniform(arg_keys[1], (ROWS_ALL,), jnp.float32) ** level_of(arg_keys[1], (ROWS_ALL,), ((0, 32),), -0.2, 0.2)), 0.001, 1.0)
    dst_table = normal_values(arg_keys[2], (DIM, ROWS_ALL), 0.4, 2.5, ((1, 32),), jnp.float32)
    dst_state = jnp.clip(jnp.exp(math.log(1.0) - 6.9077552 * jax.random.uniform(arg_keys[3], (ROWS_ALL,), jnp.float32) ** level_of(arg_keys[3], (ROWS_ALL,), ((0, 32),), -0.2, 0.2)), 0.001, 1.0)
    relation = normal_values(arg_keys[4], (DIM, NREL), 0.7, 4.0, (), jnp.float32)
    edge_src = plant(jax.random.randint(arg_keys[5], (EDGES_ALL,), 0, ROWS_DEV), jax.random.fold_in(arg_keys[5], 1), 0, ROWS_DEV - 1).astype(jnp.int32)
    edge_dst = plant(ranked_ids(arg_keys[6], (EDGES_ALL,), ROWS_DEV, 2), jax.random.fold_in(arg_keys[6], 3), 0, ROWS_DEV - 1).astype(jnp.int32)
    edge_rel = plant(ranked_ids(arg_keys[7], (EDGES_ALL,), NREL, 1), jax.random.fold_in(arg_keys[7], 3), 0, NREL - 1).astype(jnp.int32)
    matching = draw_matching(jax.random.fold_in(arg_keys[11], 71), 0)
    neg_rows = plant(ranked_ids(arg_keys[9], (N_DOM * N_EDGE, N_EDGE, SLOTS), ROWS_DEV, 2), jax.random.fold_in(arg_keys[9], 3), 0, ROWS_DEV - 1).astype(jnp.int32)
    quotas = draw_quotas(jax.random.fold_in(arg_keys[11], 71), 0)
    return dict(src_table=src_table, src_state=src_state, dst_table=dst_table, dst_state=dst_state, relation=relation, edge_src=edge_src, edge_dst=edge_dst, edge_rel=edge_rel, matching=matching, neg_rows=neg_rows, quotas=quotas)


learn_rate = 0.1
rel_rate = 0.02

def complex_product(one_side, other_side):
    half_dim = one_side.shape[0] // 2
    real_part = one_side[:half_dim] * other_side[:half_dim] - one_side[half_dim:] * other_side[half_dim:]
    imag_part = one_side[:half_dim] * other_side[half_dim:] + one_side[half_dim:] * other_side[:half_dim]
    return jnp.concatenate([real_part, imag_part], axis=0)

def conj_product(gradient, operand):
    half_dim = gradient.shape[0] // 2
    real_part = gradient[:half_dim] * operand[:half_dim] + gradient[half_dim:] * operand[half_dim:]
    imag_part = gradient[half_dim:] * operand[:half_dim] - gradient[:half_dim] * operand[half_dim:]
    return jnp.concatenate([real_part, imag_part], axis=0)

def block_plan(quota_row, edge_count):
    block_ends = jnp.cumsum(quota_row).astype(jnp.int32)
    starts = (block_ends - quota_row).astype(jnp.int32)
    positions = jnp.arange(QTOTAL, dtype=jnp.int32)
    owner_of = lax.optimization_barrier(jnp.sum((block_ends[None, :] <= positions[:, None]).astype(jnp.int32), axis=1)).astype(jnp.int32)
    matches = owner_of[:, None] == jnp.arange(edge_count, dtype=jnp.int32)[None, :]
    first_block = lax.optimization_barrier(jnp.sum(jnp.where(matches, starts[None, :], 0), axis=1)).astype(jnp.int32)
    return (owner_of, (owner_of * QMAX + positions - first_block).astype(jnp.int32))

def adagrad(table_in, state_in, gradient):
    new_state = state_in + lax.optimization_barrier(jnp.mean(gradient * gradient, axis=-2))
    return (table_in - learn_rate * gradient / jnp.sqrt(new_state)[..., None, :], new_state)

def reference(src_table, src_state, dst_table, dst_state, relation, edge_src, edge_dst, edge_rel, matching, neg_rows, quotas):

    def as_blocks(table_in):
        return jnp.transpose(table_in.reshape(DIM, N_DOM, N_EDGE, ROWS_DEV), (1, 2, 0, 3))
    src_blocks = as_blocks(src_table)
    dst_blocks = as_blocks(dst_table)[matching]
    src_states = src_state.reshape(N_DOM, N_EDGE, ROWS_DEV)
    dst_states = dst_state.reshape(N_DOM, N_EDGE, ROWS_DEV)[matching]
    src_all = edge_src.reshape(N_DOM, N_EDGE, E_DEV)
    dst_all = edge_dst.reshape(N_DOM, N_EDGE, E_DEV)
    rel_all = edge_rel.reshape(N_DOM, N_EDGE, E_DEV)
    neg_all = neg_rows.reshape(N_DOM, N_EDGE, N_EDGE * QMAX, BLOCK)
    quota_all = quotas.reshape(N_DOM, N_EDGE, N_EDGE)
    weight = 1.0 / math.sqrt(NNEG)
    labels = jnp.arange(NREL, dtype=jnp.int32)

    def dom_row(inputs):
        src_tabs, part_tabs, src_sts, part_sts, src_ids, dst_ids, rel_ids, neg_ids, quota_rows = inputs

        def requester(totals, item_set):
            dst_grad, rel_grad = totals
            own_shard, src_tab, src_e, dst_e, rel_e, neg_e, quota_e = item_set
            onehot = (rel_e[None, :] == labels[:, None]).astype(jnp.float32)
            rel_edges = jnp.dot(relation, onehot, precision=lax.Precision.HIGHEST)
            src_rows = src_tab[:, src_e]
            dst_rows = part_tabs[own_shard][:, dst_e]
            queries = complex_product(src_rows, rel_edges)
            positive = lax.optimization_barrier(jnp.sum(queries * dst_rows, axis=0))
            pos_coef = -jax.nn.sigmoid(-positive)
            owner_of, block_at = block_plan(quota_e, N_EDGE)
            row_ids = neg_e[block_at]
            picked = part_tabs[owner_of[:, None], :, row_ids].astype(jnp.bfloat16)
            negatives = jnp.transpose(picked, (2, 0, 1)).reshape(DIM, NNEG)
            query_b = queries.astype(jnp.bfloat16)
            scores = jnp.dot(query_b.T, negatives, preferred_element_type=jnp.float32)
            neg_coef = (weight * jax.nn.sigmoid(scores)).astype(jnp.bfloat16)
            neg_grad = jnp.dot(query_b, neg_coef, preferred_element_type=jnp.float32)
            query_grad = pos_coef[None, :] * dst_rows + jnp.dot(negatives, neg_coef.T, preferred_element_type=jnp.float32)
            src_grad = jnp.zeros((DIM, ROWS_DEV), jnp.float32).at[:, src_e].add(conj_product(query_grad, rel_edges))
            own_grad = jnp.zeros((DIM, ROWS_DEV), jnp.float32).at[:, dst_e].add(pos_coef[None, :] * queries)
            dst_grad = dst_grad.at[own_shard].add(own_grad)
            spread = jnp.transpose(neg_grad.reshape(DIM, QTOTAL, BLOCK), (1, 2, 0))
            dst_grad = dst_grad.at[owner_of[:, None], :, row_ids].add(spread)
            rel_grad = rel_grad + jnp.dot(conj_product(query_grad, src_rows), onehot.T, precision=lax.Precision.HIGHEST)
            return ((dst_grad, rel_grad), src_grad)
        shard_ids = jnp.arange(N_EDGE, dtype=jnp.int32)
        start_totals = (jnp.zeros((N_EDGE, DIM, ROWS_DEV), jnp.float32), jnp.zeros((DIM, NREL), jnp.float32))
        summed, src_grads = lax.scan(requester, start_totals, (shard_ids, src_tabs, src_ids, dst_ids, rel_ids, neg_ids, quota_rows))
        dst_grads, rel_grad = summed
        src_new, src_st_new = adagrad(src_tabs, src_sts, src_grads)
        dst_new, dst_st_new = adagrad(part_tabs, part_sts, dst_grads)
        return (src_new, src_st_new, dst_new, dst_st_new, rel_grad)
    src_new, src_st_new, dst_new, dst_st_new, rel_grads = lax.map(dom_row, (src_blocks, dst_blocks, src_states, dst_states, src_all, dst_all, rel_all, neg_all, quota_all))
    relation_grad = lax.optimization_barrier(jnp.sum(rel_grads, axis=0))
    src_out = jnp.transpose(src_new, (2, 0, 1, 3)).reshape(DIM, ROWS_ALL)
    dst_out = jnp.transpose(dst_new, (2, 0, 1, 3)).reshape(DIM, ROWS_ALL)
    relation_out = relation - rel_rate * relation_grad
    return (src_out, src_st_new.reshape(ROWS_ALL), dst_out, dst_st_new.reshape(ROWS_ALL), relation_out)
```

```python
import math

import jax
import jax.numpy as jnp
from jax import lax
from jax.experimental import pallas as pl
from jax.experimental.pallas import tpu as pltpu
from jax.sharding import PartitionSpec as P

BLOCK = 128
QMAX = 2
QTOTAL = 12
NNEG = QTOTAL * BLOCK
CORES = 2
LEARN_RATE = 0.1
REL_RATE = 0.02

bf16 = jnp.bfloat16
f32 = jnp.float32
MIB = 2**20


def dot_nn(lhs, rhs):
    return lax.dot_general(lhs, rhs, (((1,), (0,)), ((), ())), preferred_element_type=f32)


def dot_nt(lhs, rhs):
    return lax.dot_general(lhs, rhs, (((1,), (1,)), ((), ())), preferred_element_type=f32)


def split2(value):
    high = value.astype(bf16)
    return high, (value - high.astype(f32)).astype(bf16)


def select_rows(ids, rows):
    places = lax.broadcasted_iota(jnp.int32, (rows, ids.shape[1]), 0)
    return jnp.where(places == ids, 1.0, 0.0).astype(bf16)


def product(one, other):
    half = one.shape[0] // 2
    a, b, c, d = one[:half], one[half:], other[:half], other[half:]
    return jnp.concatenate([a * c - b * d, a * d + b * c], axis=0)


def back(grad, value):
    half = grad.shape[0] // 2
    a, b, c, d = grad[:half], grad[half:], value[:half], value[half:]
    return jnp.concatenate([a * c + b * d, b * c - a * d], axis=0)


def whole(shape):
    return pl.BlockSpec(shape, lambda *_: (0,) * len(shape))


def lanes(rows, width):
    return pl.BlockSpec((rows, width), lambda i, *_: (0, i))


def params(mib):
    return pltpu.CompilerParams(
        vmem_limit_bytes=mib * MIB, dimension_semantics=("arbitrary",)
    )


def cost(flops, moved):
    return pl.CostEstimate(flops=int(flops), bytes_accessed=int(moved), transcendentals=0)


def split_relation(relation):
    high = lax.reduce_precision(relation, 8, 7)
    rest = relation - high
    mid = lax.reduce_precision(rest, 8, 7)
    low = rest - mid
    parts = jnp.concatenate([high, mid, low], axis=1).astype(bf16)
    return jnp.pad(parts, ((0, 0), (0, (-parts.shape[1]) % 128)))


def relation_rows(rel_parts, ids, count):
    width = rel_parts.shape[1]
    places = lax.broadcasted_iota(jnp.int32, (width, ids.shape[1]), 0)
    hit = jnp.logical_and(places % count == ids, places < 3 * count)
    return dot_nn(rel_parts, jnp.where(hit, 1.0, 0.0).astype(bf16))


def make_queries(src_table, rel_parts, src_ids, rel_ids, rel_count, chunk):
    dim, rows = src_table.shape
    edges = src_ids.shape[1]

    def body(table, parts, src, rel, query, query_b, high, low):
        @pl.when(pl.program_id(0) == 0)
        def _():
            high[...], low[...] = split2(table[...])

        pick = select_rows(src[...], rows)
        src_rows = dot_nn(high[...], pick) + dot_nn(low[...], pick)
        value = product(src_rows, relation_rows(parts[...], rel[...], rel_count))
        query[...] = value
        query_b[...] = value.astype(bf16)

    return pl.pallas_call(
        body,
        name="make_queries",
        grid=(edges // chunk,),
        in_specs=[whole((dim, rows)), whole(rel_parts.shape), lanes(1, chunk), lanes(1, chunk)],
        out_specs=[lanes(dim, chunk), lanes(dim, chunk)],
        out_shape=[
            jax.ShapeDtypeStruct((dim, edges), f32),
            jax.ShapeDtypeStruct((dim, edges), bf16),
        ],
        scratch_shapes=[pltpu.VMEM((dim, rows), bf16)] * 2,
        compiler_params=params(40),
        cost_estimate=cost(4 * dim * rows * edges, 6 * dim * edges),
    )(src_table, rel_parts, src_ids, rel_ids)


def positives(part_high, query, dst_ids, chunk):
    dim, rows = part_high.shape
    edges = dst_ids.shape[1]

    def body(table, query_in, dst, query_grad, dst_grad):
        @pl.when(pl.program_id(0) == 0)
        def _():
            dst_grad[...] = jnp.zeros_like(dst_grad)

        pick = select_rows(dst[...], rows)
        dst_rows = dot_nn(table[...], pick)
        value = query_in[...]
        positive = jnp.sum(value * dst_rows, axis=0, keepdims=True)
        coef = -jax.nn.sigmoid(-positive)
        query_grad[...] = coef * dst_rows
        high, low = split2(coef * value)
        dst_grad[...] += dot_nt(high, pick) + dot_nt(low, pick)

    return pl.pallas_call(
        body,
        name="positives",
        grid=(edges // chunk,),
        in_specs=[whole((dim, rows)), lanes(dim, chunk), lanes(1, chunk)],
        out_specs=[lanes(dim, chunk), whole((dim, rows))],
        out_shape=[
            jax.ShapeDtypeStruct((dim, edges), f32),
            jax.ShapeDtypeStruct((dim, rows), f32),
        ],
        compiler_params=params(40),
        cost_estimate=cost(6 * dim * rows * edges, 8 * dim * edges),
    )(part_high, query, dst_ids)


def negative_wave(plan, tables, neg_ids, query_b, query_grad, chunk):
    count = len(tables)
    dim, rows = tables[0].shape
    edges = query_b.shape[1]
    half_weight = 0.5 / math.sqrt(NNEG)

    def body(plan_ref, *refs):
        table_refs = refs[:count]
        ids, query_ref, grad_in = refs[count : count + 3]
        grad_out = refs[count + 3]
        shard_grads = refs[count + 4 : 2 * count + 4]
        neg, neg_t, neg_grad = refs[2 * count + 4 :]
        step = pl.program_id(0)

        @pl.when(step == 0)
        def _():
            base = jnp.int32(0)
            for s in range(count):
                for b in range(QMAX):

                    @pl.when(plan_ref[s] > b)
                    def _(s=s, b=b, base=base):
                        pick = select_rows(ids[plan_ref[count + s], b : b + 1, :], rows)
                        value = dot_nn(table_refs[s][...], pick)
                        neg[base + b] = value.astype(bf16)
                        neg_t[base + b] = value.T.astype(bf16)

                base = base + plan_ref[s]

            @pl.when(base % 2 == 1)
            def _():
                neg[base] = jnp.zeros((dim, BLOCK), bf16)
                neg_t[base] = jnp.zeros((BLOCK, dim), bf16)

            def clear(j, carry):
                neg_grad[j] = jnp.zeros((dim, BLOCK), f32)
                return carry

            lax.fori_loop(0, base + base % 2, clear, 0)

        total = plan_ref[0]
        for s in range(1, count):
            total = total + plan_ref[s]
        grad_out[...] = grad_in[...]

        def pair(p, carry):
            left, right = 2 * p, 2 * p + 1
            columns = jnp.concatenate([neg[left], neg[right]], axis=1)
            columns_t = jnp.concatenate([neg_t[left], neg_t[right]], axis=0)
            scores = dot_nn(columns_t, query_ref[...])
            coef = (half_weight * jnp.tanh(0.5 * scores) + half_weight).astype(bf16)
            grad_out[...] += dot_nn(columns, coef)
            added = dot_nt(query_ref[...], coef)
            neg_grad[left] += added[:, :BLOCK]
            neg_grad[right] += added[:, BLOCK:]
            return carry

        lax.fori_loop(0, (total + 1) // 2, pair, 0)

        @pl.when(step == pl.num_programs(0) - 1)
        def _():
            base = jnp.int32(0)
            for s in range(count):
                shard_grads[s][...] = jnp.zeros((dim, rows), bf16)
                for b in range(QMAX):

                    @pl.when(plan_ref[s] > b)
                    def _(s=s, b=b, base=base):
                        pick = select_rows(ids[plan_ref[count + s], b : b + 1, :], rows)
                        high, low = split2(neg_grad[base + b])
                        value = dot_nt(high, pick) + dot_nt(low, pick)
                        if b:
                            value = value + shard_grads[s][...].astype(f32)
                        shard_grads[s][...] = value.astype(bf16)

                base = base + plan_ref[s]

    slots = QMAX * count
    return pl.pallas_call(
        body,
        name="negative_wave",
        grid_spec=pltpu.PrefetchScalarGridSpec(
            num_scalar_prefetch=1,
            grid=(edges // chunk,),
            in_specs=[whole((dim, rows))] * count
            + [whole(neg_ids.shape), lanes(dim, chunk), lanes(dim, chunk)],
            out_specs=[lanes(dim, chunk)] + [whole((dim, rows))] * count,
            scratch_shapes=[
                pltpu.VMEM((slots, dim, BLOCK), bf16),
                pltpu.VMEM((slots, BLOCK, dim), bf16),
                pltpu.VMEM((slots, dim, BLOCK), f32),
            ],
        ),
        out_shape=[jax.ShapeDtypeStruct((dim, edges), f32)]
        + [jax.ShapeDtypeStruct((dim, rows), bf16)] * count,
        input_output_aliases={count + 3: 0},
        compiler_params=params(40),
        cost_estimate=cost(6 * dim * 1.5 * count * BLOCK * edges, 10 * dim * edges),
    )(plan, *tables, neg_ids, query_b, query_grad)


def source_side(src_table, src_state, rel_parts, src_ids, rel_ids, query_grad, rel_count, chunk):
    dim, rows = src_table.shape
    edges = src_ids.shape[1]

    def body(table, state, parts, src, rel, grad_in, out, state_out, rel_out, high, low, acc):
        step = pl.program_id(0)

        @pl.when(step == 0)
        def _():
            high[...], low[...] = split2(table[...])
            acc[...] = jnp.zeros_like(acc)
            rel_out[...] = jnp.zeros_like(rel_out)

        pick = select_rows(src[...], rows)
        src_rows = dot_nn(high[...], pick) + dot_nn(low[...], pick)
        grad = grad_in[...]
        upper, lower = split2(back(grad, relation_rows(parts[...], rel[...], rel_count)))
        acc[...] += dot_nt(upper, pick) + dot_nt(lower, pick)
        kinds = select_rows(rel[...], rel_count)
        upper, lower = split2(back(grad, src_rows))
        rel_out[...] += dot_nt(kinds, upper) + dot_nt(kinds, lower)

        @pl.when(step == pl.num_programs(0) - 1)
        def _():
            total = acc[...]
            new_state = state[...] + jnp.sum(total * total, axis=0, keepdims=True) / dim
            state_out[...] = new_state
            out[...] = table[...] - LEARN_RATE * total / jnp.sqrt(new_state)

    return pl.pallas_call(
        body,
        name="source_side",
        grid=(edges // chunk,),
        in_specs=[
            whole((dim, rows)),
            whole((1, rows)),
            whole(rel_parts.shape),
            lanes(1, chunk),
            lanes(1, chunk),
            lanes(dim, chunk),
        ],
        out_specs=[whole((dim, rows)), whole((1, rows)), whole((rel_count, dim))],
        out_shape=[
            jax.ShapeDtypeStruct((dim, rows), f32),
            jax.ShapeDtypeStruct((1, rows), f32),
            jax.ShapeDtypeStruct((rel_count, dim), f32),
        ],
        scratch_shapes=[pltpu.VMEM((dim, rows), bf16)] * 2 + [pltpu.VMEM((dim, rows), f32)],
        compiler_params=params(40),
        cost_estimate=cost(8 * dim * rows * edges, 4 * dim * edges),
    )(src_table, src_state, rel_parts, src_ids, rel_ids, query_grad)


def destination_side(high, low, state, own_grad, grads):
    dim, rows = own_grad.shape
    count = len(grads)

    def body(*refs):
        high_ref, low_ref, state_ref, own_ref = refs[:4]
        out, state_out = refs[4 + count :]
        total = own_ref[...]
        for ref in refs[4 : 4 + count]:
            total = total + ref[...].astype(f32)
        new_state = state_ref[...] + jnp.sum(total * total, axis=0, keepdims=True) / dim
        state_out[...] = new_state
        table = high_ref[...].astype(f32) + low_ref[...].astype(f32)
        out[...] = table - LEARN_RATE * total / jnp.sqrt(new_state)

    width = min(rows, 128)
    return pl.pallas_call(
        body,
        name="destination_side",
        grid=(rows // width,),
        in_specs=[lanes(dim, width)] * 2
        + [lanes(1, width)]
        + [lanes(dim, width)] * (count + 1),
        out_specs=[lanes(dim, width), lanes(1, width)],
        out_shape=[
            jax.ShapeDtypeStruct((dim, rows), f32),
            jax.ShapeDtypeStruct((1, rows), f32),
        ],
        compiler_params=params(24),
        cost_estimate=cost(8 * dim * rows, (12 + 2 * count) * dim * rows),
    )(high, low, state, own_grad, *grads)


def grid_of(count):
    across = math.isqrt(count)
    while count % across:
        across -= 1
    return count // across, across


def choose(index, options):
    result = options[0]
    for k in range(1, len(options)):
        result = jnp.where(index == k, options[k], result)
    return result


def route(value, matching, x_first):
    count = lax.axis_size("dom")
    down, across = grid_of(count)
    axes = [(across, 1), (down, across)]
    (n1, stride1), (n2, stride2) = axes if x_first else axes[::-1]
    here = lax.axis_index("dom")

    def moved(device, n, stride, shift):
        place = (device // stride) % n
        return device + ((place + shift) % n - place) * stride

    def shifted(array, n, stride, shift):
        pairs = [(d, moved(d, n, stride, shift)) for d in range(count)]
        return lax.ppermute(array, "dom", pairs)

    held = [value] + [shifted(value, n1, stride1, k) for k in range(1, n1)]

    def wanted_by(device):
        source = jnp.take(matching, device)
        behind = ((here // stride1) % n1 - (source // stride1) % n1) % n1
        return choose(behind, held)

    found = [wanted_by(here)]
    for m in range(1, n2):
        found.append(shifted(wanted_by(moved(here, n2, stride2, m)), n2, stride2, m))
    source = jnp.take(matching, here)
    return choose(((here // stride2) % n2 - (source // stride2) % n2) % n2, found)


def route_halves(value, matching):
    half = value.shape[1] // 2
    parts = [route(value[:, :half], matching, True), route(value[:, half:], matching, False)]
    return jnp.concatenate(parts, axis=1)


def total_over_mesh(value):
    for axis in ("edge", "dom"):
        count = lax.axis_size(axis)
        step = 1
        while step < count:
            value = value + lax.ppermute(value, axis, [(i, i ^ step) for i in range(count)])
            step *= 2
    return value


def shards(
    src_table,
    src_state,
    dst_table,
    dst_state,
    relation,
    edge_src,
    edge_dst,
    edge_rel,
    matching,
    neg_rows,
    quotas,
):
    edge_count = lax.axis_size("edge")
    chips = edge_count // CORES
    dim, row_count = src_table.shape
    rel_count = relation.shape[1]
    edges = edge_src.shape[0]
    chunk = min(edges, 512)
    wave_chunk = min(edges, 1024)
    here = lax.axis_index("edge")

    src_ids = edge_src.reshape(1, edges)
    dst_ids = edge_dst.reshape(1, edges)
    rel_ids = edge_rel.reshape(1, edges)
    neg_ids = neg_rows.reshape(edge_count, QMAX, BLOCK)
    quota = quotas.reshape(edge_count)
    rel_parts = split_relation(relation)

    table_high = lax.reduce_precision(dst_table, 8, 7)
    table_low = (dst_table - table_high).astype(bf16)
    part_high = route_halves(table_high.astype(bf16), matching)
    table_low, held_state, part_high = lax.optimization_barrier((table_low, dst_state, part_high))
    part_low = route_halves(table_low, matching)
    part_state = route(held_state.reshape(1, row_count), matching, True)

    query, query_b = make_queries(src_table, rel_parts, src_ids, rel_ids, rel_count, chunk)
    query_grad, own_grad = positives(part_high, query, dst_ids, chunk)

    swap = [(i, i ^ 1) for i in range(edge_count)]

    def plan_of(places):
        live, at = [], []
        for place in places:
            inside = jnp.logical_and(place >= 0, place < edge_count)
            place = jnp.clip(place, 0, edge_count - 1)
            live.append(jnp.where(inside, jnp.take(quota, place), 0))
            at.append(place)
        return jnp.stack(live + at).astype(jnp.int32)

    other = here + 1 - 2 * (here % CORES)
    tables = [part_high, lax.ppermute(part_high, "edge", swap)]
    query_grad, mine, theirs = negative_wave(
        plan_of([here, other]), tables, neg_ids, query_b, query_grad, wave_chunk
    )
    arrived = [mine, lax.ppermute(theirs, "edge", swap)]

    from_below = from_above = part_high
    for s in range(1, chips):
        last = edge_count - CORES
        up = [(i, i + CORES) for i in range(CORES * (s - 1), last)]
        down = [(i + CORES, i) for i in range(0, last - CORES * (s - 1))]
        from_below = lax.ppermute(from_below, "edge", up)
        from_above = lax.ppermute(from_above, "edge", down)
        tables = [
            from_below,
            from_above,
            lax.ppermute(from_below, "edge", swap),
            lax.ppermute(from_above, "edge", swap),
        ]
        far = CORES * s
        plan = plan_of([here - far, here + far, other - far, other + far])
        query_grad, below, above, below_other, above_other = negative_wave(
            plan, tables, neg_ids, query_b, query_grad, wave_chunk
        )
        below = below.astype(f32) + lax.ppermute(below_other, "edge", swap).astype(f32)
        above = above.astype(f32) + lax.ppermute(above_other, "edge", swap).astype(f32)
        to_below = [(i, i - far) for i in range(far, edge_count)]
        to_above = [(i, i + far) for i in range(edge_count - far)]
        arrived.append(lax.ppermute(below.astype(bf16), "edge", to_below))
        arrived.append(lax.ppermute(above.astype(bf16), "edge", to_above))

    src_out, src_state_out, rel_grad = source_side(
        src_table,
        src_state.reshape(1, row_count),
        rel_parts,
        src_ids,
        rel_ids,
        query_grad,
        rel_count,
        chunk,
    )
    relation_out = relation - REL_RATE * total_over_mesh(rel_grad).T
    dst_out, dst_state_out = destination_side(part_high, part_low, part_state, own_grad, arrived)
    return (
        src_out,
        src_state_out.reshape(row_count),
        dst_out,
        dst_state_out.reshape(row_count),
        relation_out,
    )


def solution(mesh):
    in_specs = (
        P(None, ("dom", "edge")),
        P(("dom", "edge")),
        P(None, ("dom", "edge")),
        P(("dom", "edge")),
        P(),
        P(("dom", "edge")),
        P(("dom", "edge")),
        P(("dom", "edge")),
        P(),
        P(("dom", "edge"), None, None),
        P(("dom", "edge"), None),
    )
    out_specs = (
        P(None, ("dom", "edge")),
        P(("dom", "edge")),
        P(None, ("dom", "edge")),
        P(("dom", "edge")),
        P(),
    )
    return jax.shard_map(shards, mesh=mesh, in_specs=in_specs, out_specs=out_specs, check_vma=False)
```

```python
import math

import jax
import jax.numpy as jnp
from jax import lax
from jax.experimental import pallas as pl
from jax.experimental.pallas import tpu as pltpu
from jax.sharding import PartitionSpec as P

BLOCK = 128
QMAX = 2
QTOTAL = 12
NNEG = QTOTAL * BLOCK
CORES = 2
LEARN_RATE = 0.1
REL_RATE = 0.02


bf16 = jnp.bfloat16
f32 = jnp.float32
MIB = 2**20


def dot_nn(lhs, rhs):
    return lax.dot_general(lhs, rhs, (((1,), (0,)), ((), ())), preferred_element_type=f32)


def dot_nt(lhs, rhs):
    return lax.dot_general(lhs, rhs, (((1,), (1,)), ((), ())), preferred_element_type=f32)


def split2(value):
    high = value.astype(bf16)
    return high, (value - high.astype(f32)).astype(bf16)


def select_rows(ids, rows):
    places = lax.broadcasted_iota(jnp.int32, (rows, ids.shape[1]), 0)
    return jnp.where(places == ids, 1.0, 0.0).astype(bf16)


def product(one, other):
    half = one.shape[0] // 2
    a, b, c, d = one[:half], one[half:], other[:half], other[half:]
    return jnp.concatenate([a * c - b * d, a * d + b * c], axis=0)


def back(grad, value):
    half = grad.shape[0] // 2
    a, b, c, d = grad[:half], grad[half:], value[:half], value[half:]
    return jnp.concatenate([a * c + b * d, b * c - a * d], axis=0)


def whole(shape):
    return pl.BlockSpec(shape, lambda *_: (0,) * len(shape))


def lanes(rows, width):
    return pl.BlockSpec((rows, width), lambda i, *_: (0, i))


def params(mib):
    return pltpu.CompilerParams(
        vmem_limit_bytes=mib * MIB, dimension_semantics=("arbitrary",)
    )


def in_hbm(array):
    return pltpu.with_memory_space_constraint(array, pltpu.HBM)


def cost(flops, moved):
    return pl.CostEstimate(flops=int(flops), bytes_accessed=int(moved), transcendentals=0)


def split_relation(relation):
    high = lax.reduce_precision(relation, 8, 7)
    rest = relation - high
    mid = lax.reduce_precision(rest, 8, 7)
    low = rest - mid
    parts = jnp.concatenate([high, mid, low], axis=1).astype(bf16)
    return jnp.pad(parts, ((0, 0), (0, (-parts.shape[1]) % 128)))


def relation_rows(rel_parts, ids, count):
    width = rel_parts.shape[1]
    places = lax.broadcasted_iota(jnp.int32, (width, ids.shape[1]), 0)
    hit = jnp.logical_and(places % count == ids, places < 3 * count)
    return dot_nn(rel_parts, jnp.where(hit, 1.0, 0.0).astype(bf16))


def make_queries(src_table, rel_parts, src_ids, rel_ids, rel_count, chunk):
    dim, rows = src_table.shape
    edges = src_ids.shape[1]

    def body(table, parts, src, rel, query, query_b, high, low):
        @pl.when(pl.program_id(0) == 0)
        def _():
            high[...], low[...] = split2(table[...])

        pick = select_rows(src[...], rows)
        src_rows = dot_nn(high[...], pick) + dot_nn(low[...], pick)
        value = product(src_rows, relation_rows(parts[...], rel[...], rel_count))
        query[...] = value
        query_b[...] = value.astype(bf16)

    return pl.pallas_call(
        body,
        name="make_queries",
        grid=(edges // chunk,),
        in_specs=[whole((dim, rows)), whole(rel_parts.shape), lanes(1, chunk), lanes(1, chunk)],
        out_specs=[lanes(dim, chunk), lanes(dim, chunk)],
        out_shape=[pltpu.HBM((dim, edges), f32), pltpu.HBM((dim, edges), bf16)],
        scratch_shapes=[pltpu.VMEM((dim, rows), bf16)] * 2,
        compiler_params=params(16),
        cost_estimate=cost(4 * dim * rows * edges, 6 * dim * edges),
    )(src_table, rel_parts, src_ids, rel_ids)


def positives(part_high, query, dst_ids, chunk):
    dim, rows = part_high.shape
    edges = dst_ids.shape[1]

    def body(table, query_in, dst, query_grad, dst_grad):
        @pl.when(pl.program_id(0) == 0)
        def _():
            dst_grad[...] = jnp.zeros_like(dst_grad)

        pick = select_rows(dst[...], rows)
        dst_rows = dot_nn(table[...], pick)
        value = query_in[...]
        positive = jnp.sum(value * dst_rows, axis=0, keepdims=True)
        coef = -jax.nn.sigmoid(-positive)
        query_grad[...] = coef * dst_rows
        high, low = split2(coef * value)
        dst_grad[...] += dot_nt(high, pick) + dot_nt(low, pick)

    return pl.pallas_call(
        body,
        name="positives",
        grid=(edges // chunk,),
        in_specs=[whole((dim, rows)), lanes(dim, chunk), lanes(1, chunk)],
        out_specs=[lanes(dim, chunk), whole((dim, rows))],
        out_shape=[pltpu.HBM((dim, edges), f32), jax.ShapeDtypeStruct((dim, rows), f32)],
        compiler_params=params(16),
        cost_estimate=cost(6 * dim * rows * edges, 8 * dim * edges),
    )(part_high, in_hbm(query), dst_ids)


def negative_wave(tables, shifts, here, quota, neg_ids, query_b, query_grad, chunk):
    count = len(tables)
    dim, rows = tables[0].shape
    edges = query_b.shape[1]
    edge_count = neg_ids.shape[0]
    half_weight = 0.5 / math.sqrt(NNEG)
    own = [s for s in range(count) if shifts[s][0]]
    others = [s for s in range(count) if not shifts[s][0]]

    def body(here_ref, quota_ref, *refs):
        table_refs = refs[:count]
        ids, query_ref, grad_in, grad_out = refs[count : count + 4]
        own_refs = refs[count + 4 : count + 4 + len(own)]
        other_ref, neg, neg_t, neg_grad = refs[count + 4 + len(own) :]

        place = here_ref[0]
        across = place + 1 - 2 * (place % CORES)
        live, at, base = [], [], [jnp.int32(0)]
        for lane, shift in shifts:
            spot = (place if lane else across) + shift
            inside = jnp.logical_and(spot >= 0, spot < edge_count)
            spot = jnp.clip(spot, 0, edge_count - 1)
            at.append(spot)
            live.append(jnp.where(inside, quota_ref[0, spot], 0))
            base.append(base[-1] + live[-1])
        total = base[-1]

        step = pl.program_id(0)

        def picks(s, wide):
            parts = [select_rows(ids[at[s], b : b + 1, :], rows) for b in range(wide)]
            return jnp.concatenate(parts, axis=1) if wide > 1 else parts[0]

        def when_live(s, wide):
            return pl.when(jnp.logical_and(live[s] == wide, step == 0))

        def when_done(s, wide):
            return pl.when(jnp.logical_and(live[s] == wide, step == pl.num_programs(0) - 1))

        for s in range(count):
            for wide in range(1, QMAX + 1):

                @when_live(s, wide)
                def _(s=s, wide=wide):
                    value = dot_nn(table_refs[s][...], picks(s, wide))
                    for b in range(wide):
                        part = value[:, b * BLOCK : (b + 1) * BLOCK]
                        neg[base[s] + b] = part.astype(bf16)
                        neg_t[base[s] + b] = part.T.astype(bf16)
                        neg_grad[base[s] + b] = jnp.zeros((dim, BLOCK), f32)

        @pl.when(jnp.logical_and(total % 2 == 1, step == 0))
        def _():
            neg[total] = jnp.zeros((dim, BLOCK), bf16)
            neg_t[total] = jnp.zeros((BLOCK, dim), bf16)
            neg_grad[total] = jnp.zeros((dim, BLOCK), f32)

        @pl.when(total == 0)
        def _():
            grad_out[...] = grad_in[...]

        def pair(p, carry):
            left, right = 2 * p, 2 * p + 1
            columns = jnp.concatenate([neg[left], neg[right]], axis=1)
            columns_t = jnp.concatenate([neg_t[left], neg_t[right]], axis=0)
            query = query_ref[...]
            scores = dot_nn(columns_t, query)
            coef = (half_weight * jnp.tanh(0.5 * scores) + half_weight).astype(bf16)
            before = jnp.where(p == 0, grad_in[...], grad_out[...])
            grad_out[...] = before + dot_nn(columns, coef)
            added = dot_nt(query, coef)
            neg_grad[left] += added[:, :BLOCK]
            neg_grad[right] += added[:, BLOCK:]
            return carry

        lax.fori_loop(0, (total + 1) // 2, pair, 0)

        for s in range(count):

            def put(value, s=s):
                if s in own:
                    own_refs[own.index(s)][...] = value
                else:
                    other_ref[others.index(s)] = value

            @when_done(s, 0)
            def _(put=put):
                put(jnp.zeros((dim, rows), bf16))

            for wide in range(1, QMAX + 1):

                @when_done(s, wide)
                def _(s=s, wide=wide, put=put):
                    parts = [neg_grad[base[s] + b] for b in range(wide)]
                    value = jnp.concatenate(parts, axis=1) if wide > 1 else parts[0]
                    high, low = split2(value)
                    pick = picks(s, wide)
                    put((dot_nt(high, pick) + dot_nt(low, pick)).astype(bf16))

    slots = QMAX * count
    smem = pl.BlockSpec(memory_space=pltpu.SMEM)
    shard = jax.ShapeDtypeStruct((dim, rows), bf16)
    return pl.pallas_call(
        body,
        grid=(edges // chunk,),
        in_specs=[smem, smem]
        + [whole((dim, rows))] * count
        + [whole(neg_ids.shape), lanes(dim, chunk), lanes(dim, chunk)],
        out_specs=[lanes(dim, chunk)]
        + [whole((dim, rows))] * len(own)
        + [whole((len(others), dim, rows))],
        scratch_shapes=[
            pltpu.VMEM((slots, dim, BLOCK), bf16),
            pltpu.VMEM((slots, BLOCK, dim), bf16),
            pltpu.VMEM((slots, dim, BLOCK), f32),
        ],
        out_shape=[pltpu.HBM((dim, edges), f32)]
        + [shard] * len(own)
        + [jax.ShapeDtypeStruct((len(others), dim, rows), bf16)],
        input_output_aliases={count + 4: 0},
        compiler_params=params(32),
        cost_estimate=cost(6 * dim * 1.5 * count * BLOCK * edges, 10 * dim * edges),
    )(here, quota, *tables, neg_ids, in_hbm(query_b), in_hbm(query_grad))


def source_side(src_table, src_state, rel_parts, src_ids, rel_ids, query_grad, rel_count, chunk):
    dim, rows = src_table.shape
    edges = src_ids.shape[1]

    def body(table, state, parts, src, rel, grad_in, out, state_out, rel_out, high, low, acc):
        step = pl.program_id(0)

        @pl.when(step == 0)
        def _():
            high[...], low[...] = split2(table[...])
            acc[...] = jnp.zeros_like(acc)
            rel_out[...] = jnp.zeros_like(rel_out)

        pick = select_rows(src[...], rows)
        src_rows = dot_nn(high[...], pick) + dot_nn(low[...], pick)
        grad = grad_in[...]
        upper, lower = split2(back(grad, relation_rows(parts[...], rel[...], rel_count)))
        acc[...] += dot_nt(upper, pick) + dot_nt(lower, pick)
        kinds = select_rows(rel[...], rel_count)
        upper, lower = split2(back(grad, src_rows))
        rel_out[...] += dot_nt(kinds, upper) + dot_nt(kinds, lower)

        @pl.when(step == pl.num_programs(0) - 1)
        def _():
            total = acc[...]
            new_state = state[...] + jnp.sum(total * total, axis=0, keepdims=True) / dim
            state_out[...] = new_state
            out[...] = table[...] - LEARN_RATE * total / jnp.sqrt(new_state)

    return pl.pallas_call(
        body,
        name="source_side",
        grid=(edges // chunk,),
        in_specs=[
            whole((dim, rows)),
            whole((1, rows)),
            whole(rel_parts.shape),
            lanes(1, chunk),
            lanes(1, chunk),
            lanes(dim, chunk),
        ],
        out_specs=[whole((dim, rows)), whole((1, rows)), whole((rel_count, dim))],
        out_shape=[
            jax.ShapeDtypeStruct((dim, rows), f32),
            jax.ShapeDtypeStruct((1, rows), f32),
            jax.ShapeDtypeStruct((rel_count, dim), f32),
        ],
        scratch_shapes=[pltpu.VMEM((dim, rows), bf16)] * 2 + [pltpu.VMEM((dim, rows), f32)],
        compiler_params=params(16),
        cost_estimate=cost(8 * dim * rows * edges, 4 * dim * edges),
    )(src_table, src_state, rel_parts, src_ids, rel_ids, in_hbm(query_grad))


def destination_side(high, low_state, own_grad, grads):
    dim, rows = own_grad.shape
    count = len(grads)

    def body(*refs):
        high_ref, low_ref, own_ref = refs[:3]
        out, state_out = refs[3 + count :]
        total = own_ref[...]
        for ref in refs[3 : 3 + count]:
            total = total + (ref[0] if len(ref.shape) == 3 else ref[...]).astype(f32)
        packed = low_ref[...].astype(f32)
        state = packed[dim : dim + 1] + packed[dim + 1 : dim + 2] + packed[dim + 2 : dim + 3]
        new_state = state + jnp.sum(total * total, axis=0, keepdims=True) / dim
        state_out[...] = new_state
        table = high_ref[...].astype(f32) + packed[:dim]
        out[...] = table - LEARN_RATE * total / jnp.sqrt(new_state)

    width = min(rows, 128)

    def column(array):
        if array.ndim == 3:
            return pl.BlockSpec((1, dim, width), lambda i: (0, 0, i))
        return lanes(array.shape[0], width)

    operands = [high, low_state, own_grad, *grads]
    return pl.pallas_call(
        body,
        name="destination_side",
        grid=(rows // width,),
        in_specs=[column(array) for array in operands],
        out_specs=[lanes(dim, width), lanes(1, width)],
        out_shape=[
            jax.ShapeDtypeStruct((dim, rows), f32),
            jax.ShapeDtypeStruct((1, rows), f32),
        ],
        compiler_params=params(16),
        cost_estimate=cost(8 * dim * rows, (12 + 2 * count) * dim * rows),
    )(*operands)


def split_table(table, state):
    dim, rows = table.shape
    half = rows // 2
    tail = 16

    def body(table_ref, state_ref, left, right, rest):
        value = table_ref[...]
        high, low = split2(value)
        left[...] = high[:, :half]
        right[...] = high[:, half:]
        rest[:dim] = low
        first, _ = split2(state_ref[...])
        left_over = state_ref[...] - first.astype(f32)
        second, third = split2(left_over)
        parts = [first.astype(f32), second.astype(f32), third.astype(f32)]
        parts.append(jnp.zeros((tail - 3, rows), f32))
        rest[dim:] = jnp.concatenate(parts, axis=0).astype(bf16)

    return pl.pallas_call(
        body,
        name="split_table",
        in_specs=[pl.BlockSpec(memory_space=pltpu.VMEM)] * 2,
        out_specs=[pl.BlockSpec(memory_space=pltpu.VMEM)] * 3,
        out_shape=[
            jax.ShapeDtypeStruct((dim, half), bf16),
            jax.ShapeDtypeStruct((dim, rows - half), bf16),
            jax.ShapeDtypeStruct((dim + tail, rows), bf16),
        ],
        compiler_params=pltpu.CompilerParams(vmem_limit_bytes=16 * MIB),
        cost_estimate=cost(4 * dim * rows, 8 * dim * rows),
    )(table, state)


def grid_of(count):
    across = math.isqrt(count)
    while count % across:
        across -= 1
    return count // across, across


def moved(device, n, stride, shift):
    place = (device // stride) % n
    return device + ((place + shift) % n - place) * stride


def shifted(array, n, stride, shift):
    count = lax.axis_size("dom")
    return lax.ppermute(array, "dom", [(d, moved(d, n, stride, shift)) for d in range(count)])


def copy_chosen(index, options, out, columns):
    for k in range(len(options)):

        @pl.when(index == k)
        def _(k=k):
            out[:, columns] = options[k][...]


def route(values, matching, here):
    down, across = grid_of(lax.axis_size("dom"))
    axes = [(across, 1), (down, across)]
    orders = [axes, axes[::-1]][: len(values)]
    rows = values[0].shape[0]
    widths = [value.shape[1] for value in values]
    starts = [sum(widths[:i]) for i in range(len(widths))]
    vmem = pl.BlockSpec(memory_space=pltpu.VMEM)
    smem = pl.BlockSpec(memory_space=pltpu.SMEM)

    held = []
    for i, ((n1, stride1), _) in enumerate(orders):
        held.append([values[i]] + [shifted(values[i], n1, stride1, k) for k in range(1, n1)])
    flat = [array for group in held for array in group]

    def grouped(refs, groups):
        result, used = [], 0
        for group in groups:
            result.append(refs[used : used + len(group)])
            used += len(group)
        return result, refs[used:]

    def behind(place, source, n, stride):
        return ((place // stride) % n - (source // stride) % n + n) % n

    def pass_on(match_ref, here_ref, *refs):
        place = here_ref[0]
        held_refs, outs = grouped(refs, held)
        used = 0
        for i, ((n1, stride1), (n2, stride2)) in enumerate(orders):
            for m in range(1, n2):
                source = match_ref[moved(place, n2, stride2, m)]
                picked = behind(place, source, n1, stride1)
                copy_chosen(picked, held_refs[i], outs[used], slice(None))
                used += 1

    hops = [(i, m) for i in range(len(orders)) for m in range(1, orders[i][1][0])]
    passed = pl.pallas_call(
        pass_on,
        in_specs=[smem, smem] + [vmem] * len(flat),
        out_specs=[vmem] * len(hops),
        out_shape=[jax.ShapeDtypeStruct((rows, widths[i]), bf16) for i, _ in hops],
        compiler_params=pltpu.CompilerParams(vmem_limit_bytes=16 * MIB),
        cost_estimate=cost(0, 4 * rows * sum(widths)),
    )(matching, here, *flat)
    found = [[] for _ in orders]
    for (i, m), array in zip(hops, passed):
        found[i].append(shifted(array, *orders[i][1], m))
    flat_found = [array for group in found for array in group]

    def merge(match_ref, here_ref, *refs):
        place = here_ref[0]
        held_refs, rest = grouped(refs, held)
        found_refs, (out,) = grouped(rest, found)
        source = match_ref[place]
        for i, ((n1, stride1), (n2, stride2)) in enumerate(orders):
            columns = slice(starts[i], starts[i] + widths[i])
            near = behind(place, source, n1, stride1)
            far = behind(place, source, n2, stride2)
            index = jnp.where(far == 0, near, n1 - 1 + far)
            copy_chosen(index, list(held_refs[i]) + list(found_refs[i]), out, columns)

    return pl.pallas_call(
        merge,
        in_specs=[smem, smem] + [vmem] * (len(flat) + len(flat_found)),
        out_specs=vmem,
        out_shape=jax.ShapeDtypeStruct((rows, sum(widths)), bf16),
        compiler_params=pltpu.CompilerParams(vmem_limit_bytes=24 * MIB),
        cost_estimate=cost(0, 4 * rows * sum(widths)),
    )(matching, here, *flat, *flat_found)


def total_over_mesh(value):
    for axis in ("edge", "dom"):
        count = lax.axis_size(axis)
        step = 1
        while step < count:
            value = value + lax.ppermute(value, axis, [(i, i ^ step) for i in range(count)])
            step *= 2
    return value


def shards(
    src_table,
    src_state,
    dst_table,
    dst_state,
    relation,
    edge_src,
    edge_dst,
    edge_rel,
    matching,
    neg_rows,
    quotas,
):
    edge_count = lax.axis_size("edge")
    chips = edge_count // CORES
    _, row_count = src_table.shape
    rel_count = relation.shape[1]
    edges = edge_src.shape[0]
    chunk = min(edges, 512)
    wave_chunk = min(edges, 1024)
    here = lax.axis_index("edge").reshape(1).astype(jnp.int32)
    place = lax.axis_index("dom").reshape(1).astype(jnp.int32)

    src_ids = edge_src.reshape(1, edges)
    dst_ids = edge_dst.reshape(1, edges)
    rel_ids = edge_rel.reshape(1, edges)
    neg_ids = neg_rows.reshape(edge_count, QMAX, BLOCK)
    rel_parts = split_relation(relation)

    left, right, rest = split_table(dst_table, dst_state.reshape(1, row_count))
    part_high = route([left, right], matching, place)
    rest, part_high = lax.optimization_barrier((rest, part_high))
    low_state = route([rest], matching, place)

    query, query_b = make_queries(src_table, rel_parts, src_ids, rel_ids, rel_count, chunk)
    query_grad, own_grad = positives(part_high, query, dst_ids, chunk)

    swap = [(i, i ^ 1) for i in range(edge_count)]

    def swapped(array):
        return lax.ppermute(array, "edge", swap)

    query_grad, mine, theirs = negative_wave(
        [part_high, swapped(part_high)],
        [(True, 0), (False, 0)],
        here,
        quotas,
        neg_ids,
        query_b,
        query_grad,
        wave_chunk,
    )
    arrived = [mine, swapped(theirs)]

    from_below = from_above = part_high
    for s in range(1, chips):
        last = edge_count - CORES
        up = [(i, i + CORES) for i in range(CORES * (s - 1), last)]
        down = [(i + CORES, i) for i in range(0, last - CORES * (s - 1))]
        from_below = lax.ppermute(from_below, "edge", up)
        from_above = lax.ppermute(from_above, "edge", down)
        tables = [from_below, from_above, swapped(from_below), swapped(from_above)]
        far = CORES * s
        shifts = [(True, -far), (True, far), (False, -far), (False, far)]
        query_grad, below, above, theirs = negative_wave(
            tables, shifts, here, quotas, neg_ids, query_b, query_grad, wave_chunk
        )
        theirs = swapped(theirs).astype(f32)
        pairs = [(i, i - far) for i in range(far, edge_count)]
        arrived.append(lax.ppermute((below.astype(f32) + theirs[0]).astype(bf16), "edge", pairs))
        pairs = [(i, i + far) for i in range(edge_count - far)]
        arrived.append(lax.ppermute((above.astype(f32) + theirs[1]).astype(bf16), "edge", pairs))

    src_out, src_state_out, rel_grad = source_side(
        src_table,
        src_state.reshape(1, row_count),
        rel_parts,
        src_ids,
        rel_ids,
        query_grad,
        rel_count,
        chunk,
    )
    relation_out = relation - REL_RATE * total_over_mesh(rel_grad).T
    dst_out, dst_state_out = destination_side(part_high, low_state, own_grad, arrived)
    return (
        src_out,
        src_state_out.reshape(row_count),
        dst_out,
        dst_state_out.reshape(row_count),
        relation_out,
    )


def solution(mesh):
    in_specs = (
        P(None, ("dom", "edge")),
        P(("dom", "edge")),
        P(None, ("dom", "edge")),
        P(("dom", "edge")),
        P(),
        P(("dom", "edge")),
        P(("dom", "edge")),
        P(("dom", "edge")),
        P(),
        P(("dom", "edge"), None, None),
        P(("dom", "edge"), None),
    )
    out_specs = (
        P(None, ("dom", "edge")),
        P(("dom", "edge")),
        P(None, ("dom", "edge")),
        P(("dom", "edge")),
        P(),
    )

    return jax.shard_map(shards, mesh=mesh, in_specs=in_specs, out_specs=out_specs, check_vma=False)
```

```python
import math

import jax
import jax.numpy as jnp
from jax import lax
from jax.experimental import pallas as pl
from jax.experimental.pallas import tpu as pltpu
from jax.sharding import PartitionSpec as P

BLOCK = 128
QMAX = 2
QTOTAL = 12
NNEG = QTOTAL * BLOCK
CORES = 2
LEARN_RATE = 0.1
REL_RATE = 0.02


bf16 = jnp.bfloat16
f32 = jnp.float32
MIB = 2**20


def dot_nn(lhs, rhs):
    return lax.dot_general(lhs, rhs, (((1,), (0,)), ((), ())), preferred_element_type=f32)


def dot_nt(lhs, rhs):
    return lax.dot_general(lhs, rhs, (((1,), (1,)), ((), ())), preferred_element_type=f32)


def split2(value):
    high = value.astype(bf16)
    return high, (value - high.astype(f32)).astype(bf16)


def select_rows(ids, rows):
    places = lax.broadcasted_iota(jnp.int32, (rows, ids.shape[1]), 0)
    return jnp.where(places == ids, 1.0, 0.0).astype(bf16)


def product(one, other):
    half = one.shape[0] // 2
    a, b, c, d = one[:half], one[half:], other[:half], other[half:]
    return jnp.concatenate([a * c - b * d, a * d + b * c], axis=0)


def back(grad, value):
    half = grad.shape[0] // 2
    a, b, c, d = grad[:half], grad[half:], value[:half], value[half:]
    return jnp.concatenate([a * c + b * d, b * c - a * d], axis=0)


def whole(shape):
    return pl.BlockSpec(shape, lambda *_: (0,) * len(shape))


def lanes(rows, width):
    return pl.BlockSpec((rows, width), lambda i, *_: (0, i))


def params(mib):
    return pltpu.CompilerParams(
        vmem_limit_bytes=mib * MIB, dimension_semantics=("arbitrary",)
    )


def in_hbm(array):
    return pltpu.with_memory_space_constraint(array, pltpu.HBM)


def cost(flops, moved):
    return pl.CostEstimate(flops=int(flops), bytes_accessed=int(moved), transcendentals=0)


def split_relation(relation):
    high = lax.reduce_precision(relation, 8, 7)
    rest = relation - high
    mid = lax.reduce_precision(rest, 8, 7)
    low = rest - mid
    parts = jnp.concatenate([high, mid, low], axis=1).astype(bf16)
    return jnp.pad(parts, ((0, 0), (0, (-parts.shape[1]) % 128)))


def relation_rows(rel_parts, ids, count):
    width = rel_parts.shape[1]
    places = lax.broadcasted_iota(jnp.int32, (width, ids.shape[1]), 0)
    hit = jnp.logical_and(places % count == ids, places < 3 * count)
    return dot_nn(rel_parts, jnp.where(hit, 1.0, 0.0).astype(bf16))


def make_queries(src_table, rel_parts, src_ids, rel_ids, rel_count, chunk):
    dim, rows = src_table.shape
    edges = src_ids.shape[1]

    def body(table, parts, src, rel, query, query_b, high, low):
        @pl.when(pl.program_id(0) == 0)
        def _():
            high[...], low[...] = split2(table[...])

        pick = select_rows(src[...], rows)
        src_rows = dot_nn(high[...], pick) + dot_nn(low[...], pick)
        value = product(src_rows, relation_rows(parts[...], rel[...], rel_count))
        query[...] = value
        query_b[...] = value.astype(bf16)

    return pl.pallas_call(
        body,
        name="make_queries",
        grid=(edges // chunk,),
        in_specs=[whole((dim, rows)), whole(rel_parts.shape), lanes(1, chunk), lanes(1, chunk)],
        out_specs=[lanes(dim, chunk), lanes(dim, chunk)],
        out_shape=[pltpu.HBM((dim, edges), f32), pltpu.HBM((dim, edges), bf16)],
        scratch_shapes=[pltpu.VMEM((dim, rows), bf16)] * 2,
        compiler_params=params(16),
        cost_estimate=cost(4 * dim * rows * edges, 6 * dim * edges),
    )(in_hbm(src_table), rel_parts, in_hbm(src_ids), in_hbm(rel_ids))


def positives(part_high, query, dst_ids, chunk):
    dim, rows = part_high.shape
    edges = dst_ids.shape[1]

    def body(table, query_in, dst, query_grad, dst_grad):
        @pl.when(pl.program_id(0) == 0)
        def _():
            dst_grad[...] = jnp.zeros_like(dst_grad)

        pick = select_rows(dst[...], rows)
        dst_rows = dot_nn(table[...], pick)
        value = query_in[...]
        positive = jnp.sum(value * dst_rows, axis=0, keepdims=True)
        coef = -jax.nn.sigmoid(-positive)
        query_grad[...] = coef * dst_rows
        dst_grad[...] += dot_nt((coef * value).astype(bf16), pick)

    return pl.pallas_call(
        body,
        name="positives",
        grid=(edges // chunk,),
        in_specs=[whole((dim, rows)), lanes(dim, chunk), lanes(1, chunk)],
        out_specs=[lanes(dim, chunk), whole((dim, rows))],
        out_shape=[pltpu.HBM((dim, edges), f32), jax.ShapeDtypeStruct((dim, rows), f32)],
        compiler_params=params(16),
        cost_estimate=cost(6 * dim * rows * edges, 8 * dim * edges),
    )(part_high, in_hbm(query), in_hbm(dst_ids))


def negative_wave(tables, shifts, here, quota, neg_ids, query_b, query_grad, chunk):
    count = len(tables)
    dim, rows = tables[0].shape
    edges = query_b.shape[1]
    edge_count = neg_ids.shape[0]
    half_weight = 0.5 / math.sqrt(NNEG)
    own = [s for s in range(count) if shifts[s][0]]
    others = [s for s in range(count) if not shifts[s][0]]

    def body(here_ref, quota_ref, *refs):
        table_refs = refs[:count]
        ids, query_ref, grad_in, grad_out = refs[count : count + 4]
        own_refs = refs[count + 4 : count + 4 + len(own)]
        other_ref, neg, neg_t, neg_grad = refs[count + 4 + len(own) :]

        place = here_ref[0]
        across = place + 1 - 2 * (place % CORES)
        live, at, base = [], [], [jnp.int32(0)]
        for lane, shift in shifts:
            spot = (place if lane else across) + shift
            inside = jnp.logical_and(spot >= 0, spot < edge_count)
            spot = jnp.clip(spot, 0, edge_count - 1)
            at.append(spot)
            live.append(jnp.where(inside, quota_ref[0, spot], 0))
            base.append(base[-1] + live[-1])
        total = base[-1]

        step = pl.program_id(0)

        def picks(s, wide):
            parts = [select_rows(ids[at[s], b : b + 1, :], rows) for b in range(wide)]
            return jnp.concatenate(parts, axis=1) if wide > 1 else parts[0]

        def when_live(s, wide):
            return pl.when(jnp.logical_and(live[s] == wide, step == 0))

        def when_done(s, wide):
            return pl.when(jnp.logical_and(live[s] == wide, step == pl.num_programs(0) - 1))

        for s in range(count):
            for wide in range(1, QMAX + 1):

                @when_live(s, wide)
                def _(s=s, wide=wide):
                    value = dot_nn(table_refs[s][...], picks(s, wide))
                    for b in range(wide):
                        part = value[:, b * BLOCK : (b + 1) * BLOCK]
                        neg[base[s] + b] = part.astype(bf16)
                        neg_t[base[s] + b] = part.T.astype(bf16)
                        neg_grad[base[s] + b] = jnp.zeros((dim, BLOCK), f32)

        @pl.when(jnp.logical_and(total % 2 == 1, step == 0))
        def _():
            neg[total] = jnp.zeros((dim, BLOCK), bf16)
            neg_t[total] = jnp.zeros((BLOCK, dim), bf16)
            neg_grad[total] = jnp.zeros((dim, BLOCK), f32)

        @pl.when(total == 0)
        def _():
            grad_out[...] = grad_in[...]

        def pair(p, carry):
            left, right = 2 * p, 2 * p + 1
            columns = jnp.concatenate([neg[left], neg[right]], axis=1)
            columns_t = jnp.concatenate([neg_t[left], neg_t[right]], axis=0)
            query = query_ref[...]
            scores = dot_nn(columns_t, query)
            coef = (half_weight * jnp.tanh(0.5 * scores) + half_weight).astype(bf16)
            before = jnp.where(p == 0, grad_in[...], grad_out[...])
            grad_out[...] = before + dot_nn(columns, coef)
            added = dot_nt(query, coef)
            neg_grad[left] += added[:, :BLOCK]
            neg_grad[right] += added[:, BLOCK:]
            return carry

        lax.fori_loop(0, (total + 1) // 2, pair, 0)

        for s in range(count):

            def put(value, s=s):
                if s in own:
                    own_refs[own.index(s)][...] = value
                else:
                    other_ref[others.index(s)] = value

            @when_done(s, 0)
            def _(put=put):
                put(jnp.zeros((dim, rows), bf16))

            for wide in range(1, QMAX + 1):

                @when_done(s, wide)
                def _(s=s, wide=wide, put=put):
                    parts = [neg_grad[base[s] + b] for b in range(wide)]
                    value = jnp.concatenate(parts, axis=1) if wide > 1 else parts[0]
                    high, low = split2(value)
                    pick = picks(s, wide)
                    put((dot_nt(high, pick) + dot_nt(low, pick)).astype(bf16))

    slots = QMAX * count
    smem = pl.BlockSpec(memory_space=pltpu.SMEM)
    shard = jax.ShapeDtypeStruct((dim, rows), bf16)
    return pl.pallas_call(
        body,
        grid=(edges // chunk,),
        in_specs=[smem, smem]
        + [whole((dim, rows))] * count
        + [whole(neg_ids.shape), lanes(dim, chunk), lanes(dim, chunk)],
        out_specs=[lanes(dim, chunk)]
        + [whole((dim, rows))] * len(own)
        + [whole((len(others), dim, rows))],
        scratch_shapes=[
            pltpu.VMEM((slots, dim, BLOCK), bf16),
            pltpu.VMEM((slots, BLOCK, dim), bf16),
            pltpu.VMEM((slots, dim, BLOCK), f32),
        ],
        out_shape=[pltpu.HBM((dim, edges), f32)]
        + [shard] * len(own)
        + [jax.ShapeDtypeStruct((len(others), dim, rows), bf16)],
        input_output_aliases={count + 4: 0},
        compiler_params=params(32),
        cost_estimate=cost(6 * dim * 1.5 * count * BLOCK * edges, 10 * dim * edges),
    )(here, quota, *tables, neg_ids, in_hbm(query_b), in_hbm(query_grad))


def relation_side(src_table, src_ids, rel_ids, query_grad, rel_count, chunk):
    dim, rows = src_table.shape
    edges = src_ids.shape[1]

    def body(table, src, rel, grad_in, rel_out, high, low):
        @pl.when(pl.program_id(0) == 0)
        def _():
            high[...], low[...] = split2(table[...])
            rel_out[...] = jnp.zeros_like(rel_out)

        pick = select_rows(src[...], rows)
        src_rows = dot_nn(high[...], pick) + dot_nn(low[...], pick)
        kinds = select_rows(rel[...], rel_count)
        upper, lower = split2(back(grad_in[...], src_rows))
        rel_out[...] += dot_nt(kinds, upper) + dot_nt(kinds, lower)

    return pl.pallas_call(
        body,
        name="relation_side",
        grid=(edges // chunk,),
        in_specs=[whole((dim, rows)), lanes(1, chunk), lanes(1, chunk), lanes(dim, chunk)],
        out_specs=whole((rel_count, dim)),
        out_shape=jax.ShapeDtypeStruct((rel_count, dim), f32),
        scratch_shapes=[pltpu.VMEM((dim, rows), bf16)] * 2,
        compiler_params=params(24),
        cost_estimate=cost(4 * dim * rows * edges, 4 * dim * edges),
    )(in_hbm(src_table), in_hbm(src_ids), in_hbm(rel_ids), in_hbm(query_grad))


def source_side(src_table, src_state, rel_parts, src_ids, rel_ids, query_grad, rel_count, chunk):
    dim, rows = src_table.shape
    edges = src_ids.shape[1]

    def body(table, state, parts, src, rel, grad_in, out, state_out, acc):
        step = pl.program_id(0)

        @pl.when(step == 0)
        def _():
            acc[...] = jnp.zeros_like(acc)

        pick = select_rows(src[...], rows)
        term = back(grad_in[...], relation_rows(parts[...], rel[...], rel_count))
        acc[...] += dot_nt(term.astype(bf16), pick)

        @pl.when(step == pl.num_programs(0) - 1)
        def _():
            total = acc[...]
            new_state = state[...] + jnp.sum(total * total, axis=0, keepdims=True) / dim
            state_out[...] = new_state
            out[...] = table[...] - LEARN_RATE * total / jnp.sqrt(new_state)

    return pl.pallas_call(
        body,
        name="source_side",
        grid=(edges // chunk,),
        in_specs=[
            whole((dim, rows)),
            whole((1, rows)),
            whole(rel_parts.shape),
            lanes(1, chunk),
            lanes(1, chunk),
            lanes(dim, chunk),
        ],
        out_specs=[whole((dim, rows)), whole((1, rows))],
        out_shape=[
            jax.ShapeDtypeStruct((dim, rows), f32),
            jax.ShapeDtypeStruct((1, rows), f32),
        ],
        scratch_shapes=[pltpu.VMEM((dim, rows), f32)],
        compiler_params=params(24),
        cost_estimate=cost(4 * dim * rows * edges, 4 * dim * edges),
    )(
        in_hbm(src_table),
        in_hbm(src_state),
        rel_parts,
        in_hbm(src_ids),
        in_hbm(rel_ids),
        in_hbm(query_grad),
    )


def destination_side(high, low_state, own_grad, grads):
    dim, rows = own_grad.shape
    count = len(grads)

    def body(*refs):
        high_ref, low_ref, own_ref = refs[:3]
        out, state_out = refs[3 + count :]
        total = own_ref[...]
        for ref in refs[3 : 3 + count]:
            total = total + (ref[0] if len(ref.shape) == 3 else ref[...]).astype(f32)
        packed = low_ref[...].astype(f32)
        state = packed[dim : dim + 1] + packed[dim + 1 : dim + 2] + packed[dim + 2 : dim + 3]
        new_state = state + jnp.sum(total * total, axis=0, keepdims=True) / dim
        state_out[...] = new_state
        table = high_ref[...].astype(f32) + packed[:dim]
        out[...] = table - LEARN_RATE * total / jnp.sqrt(new_state)

    width = min(rows, 128)

    def column(array):
        if array.ndim == 3:
            return pl.BlockSpec((1, dim, width), lambda i: (0, 0, i))
        return lanes(array.shape[0], width)

    operands = [high, low_state, own_grad, *grads]
    return pl.pallas_call(
        body,
        name="destination_side",
        grid=(rows // width,),
        in_specs=[column(array) for array in operands],
        out_specs=[lanes(dim, width), lanes(1, width)],
        out_shape=[
            jax.ShapeDtypeStruct((dim, rows), f32),
            jax.ShapeDtypeStruct((1, rows), f32),
        ],
        compiler_params=params(16),
        cost_estimate=cost(8 * dim * rows, (12 + 2 * count) * dim * rows),
    )(*operands)


def split_table(table, state):
    dim, rows = table.shape
    half = rows // 2
    tail = 16

    def body(table_ref, state_ref, left, right, rest):
        value = table_ref[...]
        high, low = split2(value)
        left[...] = high[:, :half]
        right[...] = high[:, half:]
        rest[:dim] = low
        first, _ = split2(state_ref[...])
        left_over = state_ref[...] - first.astype(f32)
        second, third = split2(left_over)
        parts = [first.astype(f32), second.astype(f32), third.astype(f32)]
        parts.append(jnp.zeros((tail - 3, rows), f32))
        rest[dim:] = jnp.concatenate(parts, axis=0).astype(bf16)

    return pl.pallas_call(
        body,
        name="split_table",
        grid=(1,),
        in_specs=[whole((dim, rows)), whole((1, rows))],
        out_specs=[whole((dim, half)), whole((dim, rows - half)), whole((dim + tail, rows))],
        out_shape=[
            jax.ShapeDtypeStruct((dim, half), bf16),
            jax.ShapeDtypeStruct((dim, rows - half), bf16),
            jax.ShapeDtypeStruct((dim + tail, rows), bf16),
        ],
        compiler_params=params(16),
        cost_estimate=cost(4 * dim * rows, 8 * dim * rows),
    )(in_hbm(table), in_hbm(state))


def grid_of(count):
    across = math.isqrt(count)
    while count % across:
        across -= 1
    return count // across, across


def moved(device, n, stride, shift):
    place = (device // stride) % n
    return device + ((place + shift) % n - place) * stride


def shifted(array, n, stride, shift):
    count = lax.axis_size("dom")
    return lax.ppermute(array, "dom", [(d, moved(d, n, stride, shift)) for d in range(count)])


def copy_chosen(index, options, out, columns):
    for k in range(len(options)):

        @pl.when(index == k)
        def _(k=k):
            out[:, columns] = options[k][...]


def route(values, matching, here):
    down, across = grid_of(lax.axis_size("dom"))
    axes = [(across, 1), (down, across)]
    orders = [axes, axes[::-1]][: len(values)]
    rows = values[0].shape[0]
    widths = [value.shape[1] for value in values]
    starts = [sum(widths[:i]) for i in range(len(widths))]
    vmem = pl.BlockSpec(memory_space=pltpu.VMEM)
    smem = pl.BlockSpec(memory_space=pltpu.SMEM)

    held = []
    for i, ((n1, stride1), _) in enumerate(orders):
        held.append([values[i]] + [shifted(values[i], n1, stride1, k) for k in range(1, n1)])
    flat = [array for group in held for array in group]

    def grouped(refs, groups):
        result, used = [], 0
        for group in groups:
            result.append(refs[used : used + len(group)])
            used += len(group)
        return result, refs[used:]

    def behind(place, source, n, stride):
        return ((place // stride) % n - (source // stride) % n + n) % n

    def pass_on(match_ref, here_ref, *refs):
        place = here_ref[0]
        held_refs, outs = grouped(refs, held)
        used = 0
        for i, ((n1, stride1), (n2, stride2)) in enumerate(orders):
            for m in range(1, n2):
                source = match_ref[moved(place, n2, stride2, m)]
                picked = behind(place, source, n1, stride1)
                copy_chosen(picked, held_refs[i], outs[used], slice(None))
                used += 1

    hops = [(i, m) for i in range(len(orders)) for m in range(1, orders[i][1][0])]
    passed = pl.pallas_call(
        pass_on,
        in_specs=[smem, smem] + [vmem] * len(flat),
        out_specs=[vmem] * len(hops),
        out_shape=[jax.ShapeDtypeStruct((rows, widths[i]), bf16) for i, _ in hops],
        compiler_params=pltpu.CompilerParams(vmem_limit_bytes=16 * MIB),
        cost_estimate=cost(0, 4 * rows * sum(widths)),
    )(matching, here, *flat)
    found = [[] for _ in orders]
    for (i, m), array in zip(hops, passed):
        found[i].append(shifted(array, *orders[i][1], m))
    flat_found = [array for group in found for array in group]

    def merge(match_ref, here_ref, *refs):
        place = here_ref[0]
        held_refs, rest = grouped(refs, held)
        found_refs, (out,) = grouped(rest, found)
        source = match_ref[place]
        for i, ((n1, stride1), (n2, stride2)) in enumerate(orders):
            columns = slice(starts[i], starts[i] + widths[i])
            near = behind(place, source, n1, stride1)
            far = behind(place, source, n2, stride2)
            index = jnp.where(far == 0, near, n1 - 1 + far)
            copy_chosen(index, list(held_refs[i]) + list(found_refs[i]), out, columns)

    return pl.pallas_call(
        merge,
        in_specs=[smem, smem] + [vmem] * (len(flat) + len(flat_found)),
        out_specs=vmem,
        out_shape=jax.ShapeDtypeStruct((rows, sum(widths)), bf16),
        compiler_params=pltpu.CompilerParams(vmem_limit_bytes=24 * MIB),
        cost_estimate=cost(0, 4 * rows * sum(widths)),
    )(matching, here, *flat, *flat_found)


def total_over_mesh(value):
    for axis in ("edge", "dom"):
        count = lax.axis_size(axis)
        step = 1
        while step < count:
            other = lax.ppermute(value, axis, [(i, i ^ step) for i in range(count)])
            value = value + other
            step *= 2
    return value


def shards(
    src_table,
    src_state,
    dst_table,
    dst_state,
    relation,
    edge_src,
    edge_dst,
    edge_rel,
    matching,
    neg_rows,
    quotas,
):
    edge_count = lax.axis_size("edge")
    chips = edge_count // CORES
    _, row_count = src_table.shape
    rel_count = relation.shape[1]
    edges = edge_src.shape[0]
    chunk = min(edges, 1024)
    wave_chunk = min(edges, 2048)
    here = lax.axis_index("edge").reshape(1).astype(jnp.int32)
    place = lax.axis_index("dom").reshape(1).astype(jnp.int32)

    src_ids = edge_src.reshape(1, edges)
    dst_ids = edge_dst.reshape(1, edges)
    rel_ids = edge_rel.reshape(1, edges)
    neg_ids = neg_rows.reshape(edge_count, QMAX, BLOCK)
    rel_parts = split_relation(relation)

    left, right, rest = split_table(dst_table, dst_state.reshape(1, row_count))
    part_high = route([left, right], matching, place)
    rest, part_high = lax.optimization_barrier((rest, part_high))
    low_state = route([rest], matching, place)

    query, query_b = make_queries(src_table, rel_parts, src_ids, rel_ids, rel_count, chunk)
    query_grad, own_grad = positives(part_high, query, dst_ids, chunk)

    swap = [(i, i ^ 1) for i in range(edge_count)]

    def swapped(array):
        return lax.ppermute(array, "edge", swap)

    near = swapped(part_high)
    from_below = from_above = part_high
    arrived = []
    for group in groups_of(chips):
        tables, shifts = [], []
        for s in group:
            if s == 0:
                tables += [part_high, near]
                shifts += [(True, 0), (False, 0)]
                continue
            last = edge_count - CORES
            up = [(i, i + CORES) for i in range(CORES * (s - 1), last)]
            down = [(i + CORES, i) for i in range(0, last - CORES * (s - 1))]
            from_below = lax.ppermute(from_below, "edge", up)
            from_above = lax.ppermute(from_above, "edge", down)
            far = CORES * s
            tables += [from_below, from_above]
            tables += [swapped(from_below), swapped(from_above)]
            shifts += [(True, -far), (True, far), (False, -far), (False, far)]
        query_grad, *mine, theirs = negative_wave(
            tables, shifts, here, quotas, neg_ids, query_b, query_grad, wave_chunk
        )
        theirs = swapped(theirs).astype(f32)
        at = 0
        for s in group:
            far = CORES * s
            below = [(i, i - far) for i in range(far, edge_count)]
            above = [(i, i + far) for i in range(edge_count - far)]
            for pairs in (below, above):
                total = mine[at].astype(f32) + theirs[at]
                at += 1
                if s == 0:
                    arrived.append(total)
                    break
                arrived.append(lax.ppermute(total.astype(bf16), "edge", pairs))

    rel_grad = relation_side(src_table, src_ids, rel_ids, query_grad, rel_count, chunk)
    src_out, src_state_out = source_side(
        src_table,
        src_state.reshape(1, row_count),
        rel_parts,
        src_ids,
        rel_ids,
        query_grad,
        rel_count,
        chunk,
    )
    relation_out = relation - REL_RATE * total_over_mesh(rel_grad).T
    dst_out, dst_state_out = destination_side(part_high, low_state, own_grad, arrived)
    return (
        src_out,
        src_state_out.reshape(row_count),
        dst_out,
        dst_state_out.reshape(row_count),
        relation_out,
    )


def groups_of(chips):
    return [list(range(min(2, chips)))] + [[s] for s in range(2, chips)]


def solution(mesh):
    in_specs = (
        P(None, ("dom", "edge")),
        P(("dom", "edge")),
        P(None, ("dom", "edge")),
        P(("dom", "edge")),
        P(),
        P(("dom", "edge")),
        P(("dom", "edge")),
        P(("dom", "edge")),
        P(),
        P(("dom", "edge"), None, None),
        P(("dom", "edge"), None),
    )
    out_specs = (
        P(None, ("dom", "edge")),
        P(("dom", "edge")),
        P(None, ("dom", "edge")),
        P(("dom", "edge")),
        P(),
    )

    return jax.shard_map(shards, mesh=mesh, in_specs=in_specs, out_specs=out_specs, check_vma=False)
```

```python
import math

import jax
import jax.numpy as jnp
from jax import lax
from jax.experimental import pallas as pl
from jax.experimental.pallas import tpu as pltpu
from jax.sharding import PartitionSpec as P

BLOCK = 128
QMAX = 2
QTOTAL = 12
NNEG = QTOTAL * BLOCK
CORES = 2
LEARN_RATE = 0.1
REL_RATE = 0.02


bf16 = jnp.bfloat16
f32 = jnp.float32
MIB = 2**20


def dot_nn(lhs, rhs):
    return lax.dot_general(lhs, rhs, (((1,), (0,)), ((), ())), preferred_element_type=f32)


def dot_nt(lhs, rhs):
    return lax.dot_general(lhs, rhs, (((1,), (1,)), ((), ())), preferred_element_type=f32)


def split2(value):
    high = value.astype(bf16)
    return high, (value - high.astype(f32)).astype(bf16)


def select_rows(ids, rows):
    places = lax.broadcasted_iota(jnp.int32, (rows, ids.shape[1]), 0)
    return jnp.where(places == ids, 1.0, 0.0).astype(bf16)


def product(one, other):
    half = one.shape[0] // 2
    a, b, c, d = one[:half], one[half:], other[:half], other[half:]
    return jnp.concatenate([a * c - b * d, a * d + b * c], axis=0)


def back(grad, value):
    half = grad.shape[0] // 2
    a, b, c, d = grad[:half], grad[half:], value[:half], value[half:]
    return jnp.concatenate([a * c + b * d, b * c - a * d], axis=0)


def whole(shape):
    return pl.BlockSpec(shape, lambda *_: (0,) * len(shape))


def lanes(rows, width):
    return pl.BlockSpec((rows, width), lambda i, *_: (0, i))


def params(mib):
    return pltpu.CompilerParams(
        vmem_limit_bytes=mib * MIB, dimension_semantics=("arbitrary",)
    )


def in_hbm(array):
    return pltpu.with_memory_space_constraint(array, pltpu.HBM)


def cost(flops, moved):
    return pl.CostEstimate(flops=int(flops), bytes_accessed=int(moved), transcendentals=0)


def split_relation(relation):
    high = lax.reduce_precision(relation, 8, 7)
    rest = relation - high
    mid = lax.reduce_precision(rest, 8, 7)
    low = rest - mid
    parts = jnp.concatenate([high, mid, low], axis=1).astype(bf16)
    return jnp.pad(parts, ((0, 0), (0, (-parts.shape[1]) % 128)))


def relation_rows(rel_parts, ids, count):
    width = rel_parts.shape[1]
    places = lax.broadcasted_iota(jnp.int32, (width, ids.shape[1]), 0)
    hit = jnp.logical_and(places % count == ids, places < 3 * count)
    return dot_nn(rel_parts, jnp.where(hit, 1.0, 0.0).astype(bf16))


def make_queries(src_table, rel_parts, src_ids, rel_ids, rel_count, chunk):
    dim, rows = src_table.shape
    edges = src_ids.shape[1]

    def body(table, parts, src, rel, query, query_b, rows_out, high, low):
        @pl.when(pl.program_id(0) == 0)
        def _():
            high[...], low[...] = split2(table[...])

        pick = select_rows(src[...], rows)
        src_rows = dot_nn(high[...], pick) + dot_nn(low[...], pick)
        rows_out[...] = src_rows
        value = product(src_rows, relation_rows(parts[...], rel[...], rel_count))
        query[...] = value
        query_b[...] = value.astype(bf16)

    return pl.pallas_call(
        body,
        name="make_queries",
        grid=(edges // chunk,),
        in_specs=[whole((dim, rows)), whole(rel_parts.shape), lanes(1, chunk), lanes(1, chunk)],
        out_specs=[lanes(dim, chunk)] * 3,
        out_shape=[
            pltpu.HBM((dim, edges), f32),
            pltpu.HBM((dim, edges), bf16),
            pltpu.HBM((dim, edges), f32),
        ],
        scratch_shapes=[pltpu.VMEM((dim, rows), bf16)] * 2,
        compiler_params=params(32),
        cost_estimate=cost(4 * dim * rows * edges, 6 * dim * edges),
    )(in_hbm(src_table), rel_parts, in_hbm(src_ids), in_hbm(rel_ids))


def positives(part_high, query, dst_ids, chunk):
    dim, rows = part_high.shape
    edges = dst_ids.shape[1]

    def body(table, query_in, dst, query_grad, dst_grad):
        @pl.when(pl.program_id(0) == 0)
        def _():
            dst_grad[...] = jnp.zeros_like(dst_grad)

        pick = select_rows(dst[...], rows)
        dst_rows = dot_nn(table[...], pick)
        value = query_in[...]
        positive = jnp.sum(value * dst_rows, axis=0, keepdims=True)
        coef = -jax.nn.sigmoid(-positive)
        query_grad[...] = coef * dst_rows
        dst_grad[...] += dot_nt((coef * value).astype(bf16), pick)

    return pl.pallas_call(
        body,
        name="positives",
        grid=(edges // chunk,),
        in_specs=[whole((dim, rows)), lanes(dim, chunk), lanes(1, chunk)],
        out_specs=[lanes(dim, chunk), whole((dim, rows))],
        out_shape=[pltpu.HBM((dim, edges), f32), jax.ShapeDtypeStruct((dim, rows), f32)],
        compiler_params=params(32),
        cost_estimate=cost(6 * dim * rows * edges, 8 * dim * edges),
    )(part_high, in_hbm(query), in_hbm(dst_ids))


def negative_wave(tables, chip, quota, neg_ids, query_b, query_grad, lane, chunk):
    count = len(tables)
    dim, rows = tables[0].shape
    edges = query_b.shape[1]
    half_weight = 0.5 / math.sqrt(NNEG)

    def body(chip_ref, lane_ref, quota_ref, *refs):
        table_refs = refs[:count]
        ids, query_ref, grad_in, grad_out = refs[count : count + 4]
        grad_refs = refs[count + 4 : 2 * count + 4]
        neg, neg_t, neg_grad = refs[2 * count + 4 :]

        live, at, base = [], [], [jnp.int32(0)]
        for s in range(count):
            spot = CORES * chip_ref[0] + (lane_ref[0] + s) % CORES
            at.append(spot)
            live.append(quota_ref[0, spot])
            base.append(base[-1] + live[-1])
        total = base[-1]

        step = pl.program_id(0)

        def picks(s, wide):
            parts = [select_rows(ids[at[s], b : b + 1, :], rows) for b in range(wide)]
            return jnp.concatenate(parts, axis=1) if wide > 1 else parts[0]

        def when_live(s, wide):
            return pl.when(jnp.logical_and(live[s] == wide, step == 0))

        def when_done(s, wide):
            return pl.when(jnp.logical_and(live[s] == wide, step == pl.num_programs(0) - 1))

        for s in range(count):
            for wide in range(1, QMAX + 1):

                @when_live(s, wide)
                def _(s=s, wide=wide):
                    value = dot_nn(table_refs[s][...], picks(s, wide))
                    for b in range(wide):
                        part = value[:, b * BLOCK : (b + 1) * BLOCK]
                        neg[base[s] + b] = part.astype(bf16)
                        neg_t[base[s] + b] = part.T.astype(bf16)
                        neg_grad[base[s] + b] = jnp.zeros((dim, BLOCK), f32)

        @pl.when(jnp.logical_and(total % 2 == 1, step == 0))
        def _():
            neg[total] = jnp.zeros((dim, BLOCK), bf16)
            neg_t[total] = jnp.zeros((BLOCK, dim), bf16)
            neg_grad[total] = jnp.zeros((dim, BLOCK), f32)

        @pl.when(total == 0)
        def _():
            grad_out[...] = grad_in[...]

        def pair(p, carry):
            left, right = 2 * p, 2 * p + 1
            columns = jnp.concatenate([neg[left], neg[right]], axis=1)
            columns_t = jnp.concatenate([neg_t[left], neg_t[right]], axis=0)
            query = query_ref[...]
            scores = dot_nn(columns_t, query)
            coef = (half_weight * jnp.tanh(0.5 * scores) + half_weight).astype(bf16)
            before = jnp.where(p == 0, grad_in[...], grad_out[...])
            grad_out[...] = before + dot_nn(columns, coef)
            added = dot_nt(query, coef)
            neg_grad[left] += added[:, :BLOCK]
            neg_grad[right] += added[:, BLOCK:]
            return carry

        lax.fori_loop(0, (total + 1) // 2, pair, 0)

        for s in range(count):

            @when_done(s, 0)
            def _(s=s):
                grad_refs[s][...] = jnp.zeros((dim, rows), bf16)

            for wide in range(1, QMAX + 1):

                @when_done(s, wide)
                def _(s=s, wide=wide):
                    parts = [neg_grad[base[s] + b] for b in range(wide)]
                    value = jnp.concatenate(parts, axis=1) if wide > 1 else parts[0]
                    high, low = split2(value)
                    pick = picks(s, wide)
                    grad_refs[s][...] = (dot_nt(high, pick) + dot_nt(low, pick)).astype(bf16)

    slots = QMAX * count
    smem = pl.BlockSpec(memory_space=pltpu.SMEM)
    shard = jax.ShapeDtypeStruct((dim, rows), bf16)
    return pl.pallas_call(
        body,
        grid=(edges // chunk,),
        in_specs=[smem, smem, smem]
        + [whole((dim, rows))] * count
        + [whole(neg_ids.shape), lanes(dim, chunk), lanes(dim, chunk)],
        out_specs=[lanes(dim, chunk)] + [whole((dim, rows))] * count,
        scratch_shapes=[
            pltpu.VMEM((slots, dim, BLOCK), bf16),
            pltpu.VMEM((slots, BLOCK, dim), bf16),
            pltpu.VMEM((slots, dim, BLOCK), f32),
        ],
        out_shape=[pltpu.HBM((dim, edges), f32)] + [shard] * count,
        input_output_aliases={count + 5: 0},
        compiler_params=params(32),
        cost_estimate=cost(6 * dim * 1.5 * count * BLOCK * edges, 10 * dim * edges),
    )(chip, lane, quota, *tables, neg_ids, in_hbm(query_b), in_hbm(query_grad))


def relation_side(src_rows, rel_ids, query_grad, rel_count, chunk):
    dim, edges = src_rows.shape

    def body(rows_in, rel, grad_in, rel_out):
        @pl.when(pl.program_id(0) == 0)
        def _():
            rel_out[...] = jnp.zeros_like(rel_out)

        kinds = select_rows(rel[...], rel_count)
        upper, lower = split2(back(grad_in[...], rows_in[...]))
        rel_out[...] += dot_nt(kinds, upper) + dot_nt(kinds, lower)

    return pl.pallas_call(
        body,
        name="relation_side",
        grid=(edges // chunk,),
        in_specs=[lanes(dim, chunk), lanes(1, chunk), lanes(dim, chunk)],
        out_specs=whole((rel_count, dim)),
        out_shape=jax.ShapeDtypeStruct((rel_count, dim), f32),
        compiler_params=params(24),
        cost_estimate=cost(4 * dim * rel_count * edges, 8 * dim * edges),
    )(in_hbm(src_rows), in_hbm(rel_ids), in_hbm(query_grad))


def source_side(src_table, src_state, rel_parts, src_ids, rel_ids, query_grad, rel_count, chunk):
    dim, rows = src_table.shape
    edges = src_ids.shape[1]

    def body(table, state, parts, src, rel, grad_in, out, state_out, acc):
        step = pl.program_id(0)

        @pl.when(step == 0)
        def _():
            acc[...] = jnp.zeros_like(acc)

        pick = select_rows(src[...], rows)
        term = back(grad_in[...], relation_rows(parts[...], rel[...], rel_count))
        acc[...] += dot_nt(term.astype(bf16), pick)

        @pl.when(step == pl.num_programs(0) - 1)
        def _():
            total = acc[...]
            new_state = state[...] + jnp.sum(total * total, axis=0, keepdims=True) / dim
            state_out[...] = new_state
            out[...] = table[...] - LEARN_RATE * total / jnp.sqrt(new_state)

    return pl.pallas_call(
        body,
        name="source_side",
        grid=(edges // chunk,),
        in_specs=[
            whole((dim, rows)),
            whole((1, rows)),
            whole(rel_parts.shape),
            lanes(1, chunk),
            lanes(1, chunk),
            lanes(dim, chunk),
        ],
        out_specs=[whole((dim, rows)), whole((1, rows))],
        out_shape=[
            jax.ShapeDtypeStruct((dim, rows), f32),
            jax.ShapeDtypeStruct((1, rows), f32),
        ],
        scratch_shapes=[pltpu.VMEM((dim, rows), f32)],
        compiler_params=params(24),
        cost_estimate=cost(4 * dim * rows * edges, 4 * dim * edges),
    )(
        in_hbm(src_table),
        in_hbm(src_state),
        rel_parts,
        in_hbm(src_ids),
        in_hbm(rel_ids),
        in_hbm(query_grad),
    )


def destination_side(high, low_state, own_grad, grads):
    dim, rows = own_grad.shape
    count = len(grads)

    def body(*refs):
        high_ref, low_ref, own_ref = refs[:3]
        out, state_out = refs[3 + count :]
        total = own_ref[...]
        for ref in refs[3 : 3 + count]:
            total = total + ref[...].astype(f32)
        packed = low_ref[...].astype(f32)
        state = packed[dim : dim + 1] + packed[dim + 1 : dim + 2] + packed[dim + 2 : dim + 3]
        new_state = state + jnp.sum(total * total, axis=0, keepdims=True) / dim
        state_out[...] = new_state
        table = high_ref[...].astype(f32) + packed[:dim]
        out[...] = table - LEARN_RATE * total / jnp.sqrt(new_state)

    width = min(rows, 128)

    operands = [high, low_state, own_grad, *grads]
    return pl.pallas_call(
        body,
        name="destination_side",
        grid=(rows // width,),
        in_specs=[lanes(array.shape[0], width) for array in operands],
        out_specs=[lanes(dim, width), lanes(1, width)],
        out_shape=[
            jax.ShapeDtypeStruct((dim, rows), f32),
            jax.ShapeDtypeStruct((1, rows), f32),
        ],
        compiler_params=params(16),
        cost_estimate=cost(8 * dim * rows, (12 + 2 * count) * dim * rows),
    )(*operands)


def split_table(table, state):
    dim, rows = table.shape
    half = rows // 2
    tail = 16

    def body(table_ref, state_ref, left, right, rest):
        value = table_ref[...]
        high, low = split2(value)
        left[...] = high[:, :half]
        right[...] = high[:, half:]
        rest[:dim] = low
        first, _ = split2(state_ref[...])
        left_over = state_ref[...] - first.astype(f32)
        second, third = split2(left_over)
        parts = [first.astype(f32), second.astype(f32), third.astype(f32)]
        parts.append(jnp.zeros((tail - 3, rows), f32))
        rest[dim:] = jnp.concatenate(parts, axis=0).astype(bf16)

    return pl.pallas_call(
        body,
        name="split_table",
        grid=(1,),
        in_specs=[whole((dim, rows)), whole((1, rows))],
        out_specs=[whole((dim, half)), whole((dim, rows - half)), whole((dim + tail, rows))],
        out_shape=[
            jax.ShapeDtypeStruct((dim, half), bf16),
            jax.ShapeDtypeStruct((dim, rows - half), bf16),
            jax.ShapeDtypeStruct((dim + tail, rows), bf16),
        ],
        compiler_params=params(16),
        cost_estimate=cost(4 * dim * rows, 8 * dim * rows),
    )(in_hbm(table), in_hbm(state))


def grid_of(count):
    across = math.isqrt(count)
    while count % across:
        across -= 1
    return count // across, across


def moved(device, n, stride, shift):
    place = (device // stride) % n
    return device + ((place + shift) % n - place) * stride


def shifted(array, n, stride, shift):
    count = lax.axis_size("dom")
    return lax.ppermute(array, "dom", [(d, moved(d, n, stride, shift)) for d in range(count)])


def copy_chosen(index, options, out, columns):
    for k in range(len(options)):

        @pl.when(index == k)
        def _(k=k):
            out[:, columns] = options[k][...]


def route(values, matching, here):
    down, across = grid_of(lax.axis_size("dom"))
    axes = [(across, 1), (down, across)]
    orders = [axes, axes[::-1]][: len(values)]
    rows = values[0].shape[0]
    widths = [value.shape[1] for value in values]
    starts = [sum(widths[:i]) for i in range(len(widths))]
    vmem = pl.BlockSpec(memory_space=pltpu.VMEM)
    smem = pl.BlockSpec(memory_space=pltpu.SMEM)

    held = []
    for i, ((n1, stride1), _) in enumerate(orders):
        held.append([values[i]] + [shifted(values[i], n1, stride1, k) for k in range(1, n1)])
    flat = [array for group in held for array in group]

    def grouped(refs, groups):
        result, used = [], 0
        for group in groups:
            result.append(refs[used : used + len(group)])
            used += len(group)
        return result, refs[used:]

    def behind(place, source, n, stride):
        return ((place // stride) % n - (source // stride) % n + n) % n

    def pass_on(match_ref, here_ref, *refs):
        place = here_ref[0]
        held_refs, outs = grouped(refs, held)
        used = 0
        for i, ((n1, stride1), (n2, stride2)) in enumerate(orders):
            for m in range(1, n2):
                source = match_ref[moved(place, n2, stride2, m)]
                picked = behind(place, source, n1, stride1)
                copy_chosen(picked, held_refs[i], outs[used], slice(None))
                used += 1

    hops = [(i, m) for i in range(len(orders)) for m in range(1, orders[i][1][0])]
    passed = pl.pallas_call(
        pass_on,
        in_specs=[smem, smem] + [vmem] * len(flat),
        out_specs=[vmem] * len(hops),
        out_shape=[jax.ShapeDtypeStruct((rows, widths[i]), bf16) for i, _ in hops],
        compiler_params=pltpu.CompilerParams(vmem_limit_bytes=16 * MIB),
        cost_estimate=cost(0, 4 * rows * sum(widths)),
    )(matching, here, *flat)
    found = [[] for _ in orders]
    for (i, m), array in zip(hops, passed):
        found[i].append(shifted(array, *orders[i][1], m))
    flat_found = [array for group in found for array in group]

    def merge(match_ref, here_ref, *refs):
        place = here_ref[0]
        held_refs, rest = grouped(refs, held)
        found_refs, (out,) = grouped(rest, found)
        source = match_ref[place]
        for i, ((n1, stride1), (n2, stride2)) in enumerate(orders):
            columns = slice(starts[i], starts[i] + widths[i])
            near = behind(place, source, n1, stride1)
            far = behind(place, source, n2, stride2)
            index = jnp.where(far == 0, near, n1 - 1 + far)
            copy_chosen(index, list(held_refs[i]) + list(found_refs[i]), out, columns)

    return pl.pallas_call(
        merge,
        in_specs=[smem, smem] + [vmem] * (len(flat) + len(flat_found)),
        out_specs=vmem,
        out_shape=jax.ShapeDtypeStruct((rows, sum(widths)), bf16),
        compiler_params=pltpu.CompilerParams(vmem_limit_bytes=24 * MIB),
        cost_estimate=cost(0, 4 * rows * sum(widths)),
    )(matching, here, *flat, *flat_found)


def total_of_peers(value, axis, stride, n):
    count = lax.axis_size(axis)

    def peer(i, k):
        digit = (i // stride) % n
        return i + ((digit ^ k) - digit) * stride

    terms = [value]
    terms += [
        lax.ppermute(value, axis, [(i, peer(i, k)) for i in range(count)]) for k in range(1, n)
    ]
    while len(terms) > 1:
        terms = [terms[i] + terms[i + 1] for i in range(0, len(terms), 2)]
    return terms[0]


def total_over_mesh(value):
    down, across = grid_of(lax.axis_size("dom"))
    value = total_of_peers(value, "edge", 1, CORES)
    value = total_of_peers(value, "edge", CORES, lax.axis_size("edge") // CORES)
    if down * across <= 4:
        return total_of_peers(value, "dom", 1, down * across)
    value = total_of_peers(value, "dom", 1, across)
    return total_of_peers(value, "dom", across, down)


def visits(chips):
    orders = []
    for z in range(chips):
        left, order = set(range(chips)) - {z}, []
        for k in range(1, chips):
            near = [t for t in left if abs(t - z) <= k]
            near.sort(key=lambda t: (abs(t - z), (t > z) == (2 * z < chips)))
            order.append(near[-1])
            left.remove(near[-1])
        orders.append(order)
    return orders


def rounds(orders, step):
    result = []
    for z, order in enumerate(orders):
        pair = (z, order[step])
        for group in result:
            if all(pair[1] != other[1] for other in group):
                group.append(pair)
                break
        else:
            result.append([pair])
    return result


def pick_table(candidates, which, chip):
    if len(candidates) == 1:
        return candidates[0]

    def body(chip_ref, *refs):
        out = refs[-1]
        place = chip_ref[0]
        for k in range(len(candidates)):
            hits = [place == z for z in range(len(which)) if which[z] == k]
            hit = hits[0]
            for more in hits[1:]:
                hit = jnp.logical_or(hit, more)

            @pl.when(hit)
            def _(k=k):
                out[...] = refs[k][...]

    vmem = pl.BlockSpec(memory_space=pltpu.VMEM)
    return pl.pallas_call(
        body,
        in_specs=[pl.BlockSpec(memory_space=pltpu.SMEM)] + [vmem] * len(candidates),
        out_specs=vmem,
        out_shape=jax.ShapeDtypeStruct(candidates[0].shape, bf16),
        compiler_params=pltpu.CompilerParams(vmem_limit_bytes=16 * MIB),
        cost_estimate=cost(0, 4 * candidates[0].size),
    )(chip, *candidates)


def shards(
    src_table,
    src_state,
    dst_table,
    dst_state,
    relation,
    edge_src,
    edge_dst,
    edge_rel,
    matching,
    neg_rows,
    quotas,
):
    edge_count = lax.axis_size("edge")
    chips = edge_count // CORES
    _, row_count = src_table.shape
    rel_count = relation.shape[1]
    edges = edge_src.shape[0]
    chunk = min(edges, 1024)
    wave_chunk = min(edges, 2048)
    here = lax.axis_index("edge").reshape(1).astype(jnp.int32)
    place = lax.axis_index("dom").reshape(1).astype(jnp.int32)

    src_ids = edge_src.reshape(1, edges)
    dst_ids = edge_dst.reshape(1, edges)
    rel_ids = edge_rel.reshape(1, edges)
    neg_ids = neg_rows.reshape(edge_count, QMAX, BLOCK)
    rel_parts = split_relation(relation)

    left, right, rest = split_table(dst_table, dst_state.reshape(1, row_count))
    part_high = route([left, right], matching, place)
    rest, part_high = lax.optimization_barrier((rest, part_high))
    low_state = route([rest], matching, place)

    query, query_b, src_rows = make_queries(src_table, rel_parts, src_ids, rel_ids, rel_count, chunk)
    query_grad, own_grad = positives(part_high, query, dst_ids, chunk)

    swap = [(i, i ^ 1) for i in range(edge_count)]

    def swapped(array):
        return lax.ppermute(array, "edge", swap)

    orders = visits(chips)
    chip = here // CORES
    lane = here % CORES
    goals = [chip] + [
        sum(jnp.where(chip == z, orders[z][k], 0) for z in range(chips)) for k in range(chips - 1)
    ]
    at_offset = {0: part_high}
    arrived = []
    for k in range(chips):
        if k:
            last = edge_count - CORES
            up = [(i, i + CORES) for i in range(CORES * (k - 1), last)]
            down = [(i + CORES, i) for i in range(0, last - CORES * (k - 1))]
            at_offset[-k] = lax.ppermute(at_offset[1 - k], "edge", up)
            at_offset[k] = lax.ppermute(at_offset[k - 1], "edge", down)
        offsets = [orders[z][k - 1] - z if k else 0 for z in range(chips)]
        kinds = sorted(set(offsets))
        table = pick_table([at_offset[d] for d in kinds], [kinds.index(d) for d in offsets], chip)
        tables = [table, swapped(table)]
        query_grad, mine, theirs = negative_wave(
            tables, goals[k], quotas, neg_ids, query_b, query_grad, lane, wave_chunk
        )
        total = mine.astype(f32) + swapped(theirs).astype(f32)
        if not k:
            arrived.append(total)
            continue
        total = total.astype(bf16)
        for group in rounds(orders, k - 1):
            pairs = [(CORES * z + c, CORES * t + c) for z, t in group for c in range(CORES)]
            arrived.append(lax.ppermute(total, "edge", pairs))

    rel_grad = relation_side(src_rows, rel_ids, query_grad, rel_count, chunk)
    src_out, src_state_out = source_side(
        src_table,
        src_state.reshape(1, row_count),
        rel_parts,
        src_ids,
        rel_ids,
        query_grad,
        rel_count,
        chunk,
    )
    relation_out = relation - REL_RATE * total_over_mesh(rel_grad).T
    dst_out, dst_state_out = destination_side(part_high, low_state, own_grad, arrived)
    return (
        src_out,
        src_state_out.reshape(row_count),
        dst_out,
        dst_state_out.reshape(row_count),
        relation_out,
    )


def solution(mesh):
    in_specs = (
        P(None, ("dom", "edge")),
        P(("dom", "edge")),
        P(None, ("dom", "edge")),
        P(("dom", "edge")),
        P(),
        P(("dom", "edge")),
        P(("dom", "edge")),
        P(("dom", "edge")),
        P(),
        P(("dom", "edge"), None, None),
        P(("dom", "edge"), None),
    )
    out_specs = (
        P(None, ("dom", "edge")),
        P(("dom", "edge")),
        P(None, ("dom", "edge")),
        P(("dom", "edge")),
        P(),
    )

    return jax.shard_map(shards, mesh=mesh, in_specs=in_specs, out_specs=out_specs, check_vma=False)
```

```python
import math

import jax
import jax.numpy as jnp
from jax import lax
from jax.experimental import pallas as pl
from jax.experimental.pallas import tpu as pltpu
from jax.sharding import PartitionSpec as P

BLOCK = 128
QMAX = 2
QTOTAL = 12
NNEG = QTOTAL * BLOCK
CORES = 2
LEARN_RATE = 0.1
REL_RATE = 0.02


bf16 = jnp.bfloat16
f32 = jnp.float32
MIB = 2**20


def dot_nn(lhs, rhs):
    return lax.dot_general(lhs, rhs, (((1,), (0,)), ((), ())), preferred_element_type=f32)


def dot_nt(lhs, rhs):
    return lax.dot_general(lhs, rhs, (((1,), (1,)), ((), ())), preferred_element_type=f32)


def split2(value):
    high = value.astype(bf16)
    return high, (value - high.astype(f32)).astype(bf16)


def select_rows(ids, rows):
    places = lax.broadcasted_iota(jnp.int32, (rows, ids.shape[1]), 0)
    return jnp.where(places == ids, 1.0, 0.0).astype(bf16)


def product(one, other):
    half = one.shape[0] // 2
    a, b, c, d = one[:half], one[half:], other[:half], other[half:]
    return jnp.concatenate([a * c - b * d, a * d + b * c], axis=0)


def back(grad, value):
    half = grad.shape[0] // 2
    a, b, c, d = grad[:half], grad[half:], value[:half], value[half:]
    return jnp.concatenate([a * c + b * d, b * c - a * d], axis=0)


def whole(shape):
    return pl.BlockSpec(shape, lambda *_: (0,) * len(shape))


def lanes(rows, width):
    return pl.BlockSpec((rows, width), lambda i, *_: (0, i))


def params(mib):
    return pltpu.CompilerParams(
        vmem_limit_bytes=mib * MIB, dimension_semantics=("arbitrary",)
    )


def in_hbm(array):
    return pltpu.with_memory_space_constraint(array, pltpu.HBM)


def cost(flops, moved):
    return pl.CostEstimate(flops=int(flops), bytes_accessed=int(moved), transcendentals=0)


def split_relation(relation):
    high = lax.reduce_precision(relation, 8, 7)
    rest = relation - high
    mid = lax.reduce_precision(rest, 8, 7)
    low = rest - mid
    parts = jnp.concatenate([high, mid, low], axis=1).astype(bf16)
    return jnp.pad(parts, ((0, 0), (0, (-parts.shape[1]) % 128)))


def relation_rows(rel_parts, ids, count):
    width = rel_parts.shape[1]
    places = lax.broadcasted_iota(jnp.int32, (width, ids.shape[1]), 0)
    hit = jnp.logical_and(places % count == ids, places < 3 * count)
    return dot_nn(rel_parts, jnp.where(hit, 1.0, 0.0).astype(bf16))


def make_queries(src_table, rel_parts, src_ids, rel_ids, rel_count, chunk, part, parts, before):
    dim, rows = src_table.shape
    edges = src_ids.shape[1]
    steps = edges // chunk // parts
    dtypes = (f32, bf16, f32)

    def body(table, parts_ref, src, rel, *refs):
        query, query_b, rows_out, high, low = refs[len(before) :]

        @pl.when(pl.program_id(0) == 0)
        def _():
            high[...], low[...] = split2(table[...])

        pick = select_rows(src[...], rows)
        src_rows = dot_nn(high[...], pick) + dot_nn(low[...], pick)
        rows_out[...] = src_rows
        value = product(src_rows, relation_rows(parts_ref[...], rel[...], rel_count))
        query[...] = value
        query_b[...] = value.astype(bf16)

    def columns(height):
        return pl.BlockSpec((height, chunk), lambda i: (0, i + part * steps))

    return pl.pallas_call(
        body,
        name="make_queries",
        grid=(steps,),
        in_specs=[whole((dim, rows)), whole(rel_parts.shape), columns(1), columns(1)]
        + [pl.BlockSpec(memory_space=pl.ANY)] * len(before),
        out_specs=[columns(dim)] * 3,
        out_shape=[pltpu.HBM((dim, edges), dtype) for dtype in dtypes],
        input_output_aliases={4 + i: i for i in range(len(before))},
        scratch_shapes=[pltpu.VMEM((dim, rows), bf16)] * 2,
        compiler_params=params(32),
        cost_estimate=cost(4 * dim * rows * edges // parts, 10 * dim * edges // parts),
    )(in_hbm(src_table), rel_parts, in_hbm(src_ids), in_hbm(rel_ids), *map(in_hbm, before))


def positives(part_high, query, dst_ids, chunk):
    dim, rows = part_high.shape
    edges = dst_ids.shape[1]

    def body(table, query_in, dst, query_grad, dst_grad):
        @pl.when(pl.program_id(0) == 0)
        def _():
            dst_grad[...] = jnp.zeros_like(dst_grad)

        pick = select_rows(dst[...], rows)
        dst_rows = dot_nn(table[...], pick)
        value = query_in[...]
        positive = jnp.sum(value * dst_rows, axis=0, keepdims=True)
        coef = -jax.nn.sigmoid(-positive)
        query_grad[...] = coef * dst_rows
        dst_grad[...] += dot_nt((coef * value).astype(bf16), pick)

    return pl.pallas_call(
        body,
        name="positives",
        grid=(edges // chunk,),
        in_specs=[whole((dim, rows)), lanes(dim, chunk), lanes(1, chunk)],
        out_specs=[lanes(dim, chunk), whole((dim, rows))],
        out_shape=[pltpu.HBM((dim, edges), f32), jax.ShapeDtypeStruct((dim, rows), f32)],
        compiler_params=params(32),
        cost_estimate=cost(6 * dim * rows * edges, 8 * dim * edges),
    )(part_high, in_hbm(query), in_hbm(dst_ids))


def negative_wave(tables, chip, quota, neg_ids, query_b, query_grad, lane, chunk):
    count = len(tables)
    dim, rows = tables[0].shape
    edges = query_b.shape[1]
    half_weight = 0.5 / math.sqrt(NNEG)

    def body(chip_ref, lane_ref, quota_ref, *refs):
        table_refs = refs[:count]
        ids, query_ref, grad_in, grad_out = refs[count : count + 4]
        grad_refs = refs[count + 4 : 2 * count + 4]
        neg, neg_t, neg_grad = refs[2 * count + 4 :]

        live, at, base = [], [], [jnp.int32(0)]
        for s in range(count):
            spot = CORES * chip_ref[0] + (lane_ref[0] + s) % CORES
            at.append(spot)
            live.append(quota_ref[0, spot])
            base.append(base[-1] + live[-1])
        total = base[-1]

        step = pl.program_id(0)

        def picks(s, wide):
            parts = [select_rows(ids[at[s], b : b + 1, :], rows) for b in range(wide)]
            return jnp.concatenate(parts, axis=1) if wide > 1 else parts[0]

        def when_live(s, wide):
            return pl.when(jnp.logical_and(live[s] == wide, step == 0))

        def when_done(s, wide):
            return pl.when(jnp.logical_and(live[s] == wide, step == pl.num_programs(0) - 1))

        for s in range(count):
            for wide in range(1, QMAX + 1):

                @when_live(s, wide)
                def _(s=s, wide=wide):
                    value = dot_nn(table_refs[s][...], picks(s, wide))
                    for b in range(wide):
                        part = value[:, b * BLOCK : (b + 1) * BLOCK]
                        neg[base[s] + b] = part.astype(bf16)
                        neg_t[base[s] + b] = part.T.astype(bf16)
                        neg_grad[base[s] + b] = jnp.zeros((dim, BLOCK), f32)

        @pl.when(jnp.logical_and(total % 2 == 1, step == 0))
        def _():
            neg[total] = jnp.zeros((dim, BLOCK), bf16)
            neg_t[total] = jnp.zeros((BLOCK, dim), bf16)
            neg_grad[total] = jnp.zeros((dim, BLOCK), f32)

        @pl.when(total == 0)
        def _():
            grad_out[...] = grad_in[...]

        def pair(p, carry):
            left, right = 2 * p, 2 * p + 1
            columns = jnp.concatenate([neg[left], neg[right]], axis=1)
            columns_t = jnp.concatenate([neg_t[left], neg_t[right]], axis=0)
            query = query_ref[...]
            scores = dot_nn(columns_t, query)
            coef = (half_weight * jnp.tanh(0.5 * scores) + half_weight).astype(bf16)
            before = jnp.where(p == 0, grad_in[...], grad_out[...])
            grad_out[...] = before + dot_nn(columns, coef)
            added = dot_nt(query, coef)
            neg_grad[left] += added[:, :BLOCK]
            neg_grad[right] += added[:, BLOCK:]
            return carry

        lax.fori_loop(0, (total + 1) // 2, pair, 0)

        for s in range(count):

            @when_done(s, 0)
            def _(s=s):
                grad_refs[s][...] = jnp.zeros((dim, rows), bf16)

            for wide in range(1, QMAX + 1):

                @when_done(s, wide)
                def _(s=s, wide=wide):
                    parts = [neg_grad[base[s] + b] for b in range(wide)]
                    value = jnp.concatenate(parts, axis=1) if wide > 1 else parts[0]
                    high, low = split2(value)
                    pick = picks(s, wide)
                    grad_refs[s][...] = (dot_nt(high, pick) + dot_nt(low, pick)).astype(bf16)

    slots = QMAX * count
    smem = pl.BlockSpec(memory_space=pltpu.SMEM)
    shard = jax.ShapeDtypeStruct((dim, rows), bf16)
    return pl.pallas_call(
        body,
        grid=(edges // chunk,),
        in_specs=[smem, smem, smem]
        + [whole((dim, rows))] * count
        + [whole(neg_ids.shape), lanes(dim, chunk), lanes(dim, chunk)],
        out_specs=[lanes(dim, chunk)] + [whole((dim, rows))] * count,
        scratch_shapes=[
            pltpu.VMEM((slots, dim, BLOCK), bf16),
            pltpu.VMEM((slots, BLOCK, dim), bf16),
            pltpu.VMEM((slots, dim, BLOCK), f32),
        ],
        out_shape=[pltpu.HBM((dim, edges), f32)] + [shard] * count,
        input_output_aliases={count + 5: 0},
        compiler_params=params(32),
        cost_estimate=cost(6 * dim * 1.5 * count * BLOCK * edges, 10 * dim * edges),
    )(chip, lane, quota, *tables, neg_ids, in_hbm(query_b), in_hbm(query_grad))


def relation_side(src_rows, rel_ids, query_grad, rel_count, chunk):
    dim, edges = src_rows.shape

    def body(rows_in, rel, grad_in, rel_out):
        @pl.when(pl.program_id(0) == 0)
        def _():
            rel_out[...] = jnp.zeros_like(rel_out)

        kinds = select_rows(rel[...], rel_count)
        upper, lower = split2(back(grad_in[...], rows_in[...]))
        rel_out[...] += dot_nt(kinds, upper) + dot_nt(kinds, lower)

    return pl.pallas_call(
        body,
        name="relation_side",
        grid=(edges // chunk,),
        in_specs=[lanes(dim, chunk), lanes(1, chunk), lanes(dim, chunk)],
        out_specs=whole((rel_count, dim)),
        out_shape=jax.ShapeDtypeStruct((rel_count, dim), f32),
        compiler_params=params(24),
        cost_estimate=cost(4 * dim * rel_count * edges, 8 * dim * edges),
    )(in_hbm(src_rows), in_hbm(rel_ids), in_hbm(query_grad))


def source_side(src_table, src_state, rel_parts, src_ids, rel_ids, query_grad, rel_count, chunk):
    dim, rows = src_table.shape
    edges = src_ids.shape[1]

    def body(table, state, parts, src, rel, grad_in, out, state_out, acc):
        step = pl.program_id(0)

        @pl.when(step == 0)
        def _():
            acc[...] = jnp.zeros_like(acc)

        pick = select_rows(src[...], rows)
        term = back(grad_in[...], relation_rows(parts[...], rel[...], rel_count))
        acc[...] += dot_nt(term.astype(bf16), pick)

        @pl.when(step == pl.num_programs(0) - 1)
        def _():
            total = acc[...]
            new_state = state[...] + jnp.sum(total * total, axis=0, keepdims=True) / dim
            state_out[...] = new_state
            out[...] = table[...] - LEARN_RATE * total / jnp.sqrt(new_state)

    return pl.pallas_call(
        body,
        name="source_side",
        grid=(edges // chunk,),
        in_specs=[
            whole((dim, rows)),
            whole((1, rows)),
            whole(rel_parts.shape),
            lanes(1, chunk),
            lanes(1, chunk),
            lanes(dim, chunk),
        ],
        out_specs=[whole((dim, rows)), whole((1, rows))],
        out_shape=[
            jax.ShapeDtypeStruct((dim, rows), f32),
            jax.ShapeDtypeStruct((1, rows), f32),
        ],
        scratch_shapes=[pltpu.VMEM((dim, rows), f32)],
        compiler_params=params(24),
        cost_estimate=cost(4 * dim * rows * edges, 4 * dim * edges),
    )(
        in_hbm(src_table),
        in_hbm(src_state),
        rel_parts,
        in_hbm(src_ids),
        in_hbm(rel_ids),
        in_hbm(query_grad),
    )


def destination_side(high, low_state, own_grad, grads):
    dim, rows = own_grad.shape
    count = len(grads)

    def body(*refs):
        high_ref, low_ref, own_ref = refs[:3]
        out, state_out = refs[3 + count :]
        total = own_ref[...]
        for ref in refs[3 : 3 + count]:
            total = total + ref[...].astype(f32)
        packed = low_ref[...].astype(f32)
        state = packed[dim : dim + 1] + packed[dim + 1 : dim + 2] + packed[dim + 2 : dim + 3]
        new_state = state + jnp.sum(total * total, axis=0, keepdims=True) / dim
        state_out[...] = new_state
        table = high_ref[...].astype(f32) + packed[:dim]
        out[...] = table - LEARN_RATE * total / jnp.sqrt(new_state)

    width = min(rows, 128)

    operands = [high, low_state, own_grad, *grads]
    return pl.pallas_call(
        body,
        name="destination_side",
        grid=(rows // width,),
        in_specs=[lanes(array.shape[0], width) for array in operands],
        out_specs=[lanes(dim, width), lanes(1, width)],
        out_shape=[
            jax.ShapeDtypeStruct((dim, rows), f32),
            jax.ShapeDtypeStruct((1, rows), f32),
        ],
        compiler_params=params(16),
        cost_estimate=cost(8 * dim * rows, (12 + 2 * count) * dim * rows),
    )(*operands)


def split_table(table, state):
    dim, rows = table.shape
    half = rows // 2
    tail = 16

    def body(table_ref, state_ref, left, right, rest):
        value = table_ref[...]
        high, low = split2(value)
        left[...] = high[:, :half]
        right[...] = high[:, half:]
        rest[:dim] = low
        first, _ = split2(state_ref[...])
        left_over = state_ref[...] - first.astype(f32)
        second, third = split2(left_over)
        parts = [first.astype(f32), second.astype(f32), third.astype(f32)]
        parts.append(jnp.zeros((tail - 3, rows), f32))
        rest[dim:] = jnp.concatenate(parts, axis=0).astype(bf16)

    return pl.pallas_call(
        body,
        name="split_table",
        grid=(1,),
        in_specs=[whole((dim, rows)), whole((1, rows))],
        out_specs=[whole((dim, half)), whole((dim, rows - half)), whole((dim + tail, rows))],
        out_shape=[
            jax.ShapeDtypeStruct((dim, half), bf16),
            jax.ShapeDtypeStruct((dim, rows - half), bf16),
            jax.ShapeDtypeStruct((dim + tail, rows), bf16),
        ],
        compiler_params=params(16),
        cost_estimate=cost(4 * dim * rows, 8 * dim * rows),
    )(in_hbm(table), in_hbm(state))


def grid_of(count):
    across = math.isqrt(count)
    while count % across:
        across -= 1
    return count // across, across


def moved(device, n, stride, shift):
    place = (device // stride) % n
    return device + ((place + shift) % n - place) * stride


def shifted(array, n, stride, shift):
    count = lax.axis_size("dom")
    return lax.ppermute(array, "dom", [(d, moved(d, n, stride, shift)) for d in range(count)])


def copy_chosen(index, options, out, columns):
    for k in range(len(options)):

        @pl.when(index == k)
        def _(k=k):
            out[:, columns] = options[k][...]


def route(values, matching, here):
    down, across = grid_of(lax.axis_size("dom"))
    axes = [(across, 1), (down, across)]
    orders = [axes, axes[::-1]][: len(values)]
    rows = values[0].shape[0]
    widths = [value.shape[1] for value in values]
    starts = [sum(widths[:i]) for i in range(len(widths))]
    vmem = pl.BlockSpec(memory_space=pltpu.VMEM)
    smem = pl.BlockSpec(memory_space=pltpu.SMEM)

    held = []
    for i, ((n1, stride1), _) in enumerate(orders):
        held.append([values[i]] + [shifted(values[i], n1, stride1, k) for k in range(1, n1)])
    flat = [array for group in held for array in group]

    def grouped(refs, groups):
        result, used = [], 0
        for group in groups:
            result.append(refs[used : used + len(group)])
            used += len(group)
        return result, refs[used:]

    def behind(place, source, n, stride):
        return ((place // stride) % n - (source // stride) % n + n) % n

    def pass_on(match_ref, here_ref, *refs):
        place = here_ref[0]
        held_refs, outs = grouped(refs, held)
        used = 0
        for i, ((n1, stride1), (n2, stride2)) in enumerate(orders):
            for m in range(1, n2):
                source = match_ref[moved(place, n2, stride2, m)]
                picked = behind(place, source, n1, stride1)
                copy_chosen(picked, held_refs[i], outs[used], slice(None))
                used += 1

    hops = [(i, m) for i in range(len(orders)) for m in range(1, orders[i][1][0])]
    passed = pl.pallas_call(
        pass_on,
        in_specs=[smem, smem] + [vmem] * len(flat),
        out_specs=[vmem] * len(hops),
        out_shape=[jax.ShapeDtypeStruct((rows, widths[i]), bf16) for i, _ in hops],
        compiler_params=pltpu.CompilerParams(vmem_limit_bytes=16 * MIB),
        cost_estimate=cost(0, 4 * rows * sum(widths)),
    )(matching, here, *flat)
    found = [[] for _ in orders]
    for (i, m), array in zip(hops, passed):
        found[i].append(shifted(array, *orders[i][1], m))
    flat_found = [array for group in found for array in group]

    def merge(match_ref, here_ref, *refs):
        place = here_ref[0]
        held_refs, rest = grouped(refs, held)
        found_refs, (out,) = grouped(rest, found)
        source = match_ref[place]
        for i, ((n1, stride1), (n2, stride2)) in enumerate(orders):
            columns = slice(starts[i], starts[i] + widths[i])
            near = behind(place, source, n1, stride1)
            far = behind(place, source, n2, stride2)
            index = jnp.where(far == 0, near, n1 - 1 + far)
            copy_chosen(index, list(held_refs[i]) + list(found_refs[i]), out, columns)

    return pl.pallas_call(
        merge,
        in_specs=[smem, smem] + [vmem] * (len(flat) + len(flat_found)),
        out_specs=vmem,
        out_shape=jax.ShapeDtypeStruct((rows, sum(widths)), bf16),
        compiler_params=pltpu.CompilerParams(vmem_limit_bytes=24 * MIB),
        cost_estimate=cost(0, 4 * rows * sum(widths)),
    )(matching, here, *flat, *flat_found)


def total_of_peers(value, axis, stride, n):
    count = lax.axis_size(axis)

    def peer(i, k):
        digit = (i // stride) % n
        return i + ((digit ^ k) - digit) * stride

    terms = [value]
    for k in range(1, n):
        terms.append(lax.ppermute(value, axis, [(i, peer(i, k)) for i in range(count)]))
    while len(terms) > 1:
        terms = [terms[i] + terms[i + 1] for i in range(0, len(terms), 2)]
    return terms[0]


def total_over_mesh(value):
    down, across = grid_of(lax.axis_size("dom"))
    value = total_of_peers(value, "edge", 1, CORES)
    value = total_of_peers(value, "edge", CORES, lax.axis_size("edge") // CORES)
    if down * across <= 4:
        return total_of_peers(value, "dom", 1, down * across)
    value = total_of_peers(value, "dom", 1, across)
    return total_of_peers(value, "dom", across, down)


def shards(
    src_table,
    src_state,
    dst_table,
    dst_state,
    relation,
    edge_src,
    edge_dst,
    edge_rel,
    matching,
    neg_rows,
    quotas,
):
    edge_count = lax.axis_size("edge")
    chips = edge_count // CORES
    _, row_count = src_table.shape
    rel_count = relation.shape[1]
    edges = edge_src.shape[0]
    chunk = min(edges, 1024)
    wave_chunk = min(edges, 2048)
    here = lax.axis_index("edge").reshape(1).astype(jnp.int32)
    place = lax.axis_index("dom").reshape(1).astype(jnp.int32)

    src_ids = edge_src.reshape(1, edges)
    dst_ids = edge_dst.reshape(1, edges)
    rel_ids = edge_rel.reshape(1, edges)
    neg_ids = neg_rows.reshape(edge_count, QMAX, BLOCK)
    rel_parts = split_relation(relation)

    left, right, rest = split_table(dst_table, dst_state.reshape(1, row_count))
    part_high = route([left, right], matching, place)
    rest, part_high = lax.optimization_barrier((rest, part_high))
    low_state = route([rest], matching, place)

    made = []
    for part in range(2):
        made = make_queries(
            src_table, rel_parts, src_ids, rel_ids, rel_count, min(chunk, edges // 2), part, 2, made
        )
    query, query_b, src_rows = made
    query_grad, own_grad = positives(part_high, query, dst_ids, chunk)

    swap = [(i, i ^ 1) for i in range(edge_count)]

    def swapped(array):
        return lax.ppermute(array, "edge", swap)

    chip = here // CORES
    lane = here % CORES
    arrived, done = [], []
    for k in range(chips):
        pairs = [(i, i ^ (CORES * k)) for i in range(edge_count)]
        table = part_high
        if k:
            if k >= 3:
                table, _ = lax.optimization_barrier((table, done[k - 3]))
            table = lax.ppermute(table, "edge", pairs)
        query_grad, mine, theirs = negative_wave(
            [table, swapped(table)],
            chip ^ k,
            quotas,
            neg_ids,
            query_b,
            query_grad,
            lane,
            wave_chunk,
        )
        total = mine.astype(f32) + swapped(theirs).astype(f32)
        if k:
            total = lax.ppermute(total.astype(bf16), "edge", pairs)
        arrived.append(total)
        done.append(mine)

    rel_grad = relation_side(src_rows, rel_ids, query_grad, rel_count, chunk)
    src_out, src_state_out = source_side(
        src_table,
        src_state.reshape(1, row_count),
        rel_parts,
        src_ids,
        rel_ids,
        query_grad,
        rel_count,
        chunk,
    )
    relation_out = relation - REL_RATE * total_over_mesh(rel_grad).T
    dst_out, dst_state_out = destination_side(part_high, low_state, own_grad, arrived)
    return (
        src_out,
        src_state_out.reshape(row_count),
        dst_out,
        dst_state_out.reshape(row_count),
        relation_out,
    )


def solution(mesh):
    in_specs = (
        P(None, ("dom", "edge")),
        P(("dom", "edge")),
        P(None, ("dom", "edge")),
        P(("dom", "edge")),
        P(),
        P(("dom", "edge")),
        P(("dom", "edge")),
        P(("dom", "edge")),
        P(),
        P(("dom", "edge"), None, None),
        P(("dom", "edge"), None),
    )
    out_specs = (
        P(None, ("dom", "edge")),
        P(("dom", "edge")),
        P(None, ("dom", "edge")),
        P(("dom", "edge")),
        P(),
    )

    return jax.shard_map(shards, mesh=mesh, in_specs=in_specs, out_specs=out_specs, check_vma=False)
```

```python
import math

import jax
import jax.numpy as jnp
from jax import lax
from jax.experimental import pallas as pl
from jax.experimental.pallas import tpu as pltpu
from jax.sharding import PartitionSpec as P

BLOCK = 128
QMAX = 2
QTOTAL = 12
NNEG = QTOTAL * BLOCK
CORES = 2
LEARN_RATE = 0.1
REL_RATE = 0.02


bf16 = jnp.bfloat16
f32 = jnp.float32
MIB = 2**20


def dot_nn(lhs, rhs):
    return lax.dot_general(lhs, rhs, (((1,), (0,)), ((), ())), preferred_element_type=f32)


def dot_nt(lhs, rhs):
    return lax.dot_general(lhs, rhs, (((1,), (1,)), ((), ())), preferred_element_type=f32)


def split2(value):
    high = value.astype(bf16)
    return high, (value - high.astype(f32)).astype(bf16)


def select_rows(ids, rows):
    places = lax.broadcasted_iota(jnp.int32, (rows, ids.shape[1]), 0)
    return jnp.where(places == ids, 1.0, 0.0).astype(bf16)


def product(one, other):
    half = one.shape[0] // 2
    a, b, c, d = one[:half], one[half:], other[:half], other[half:]
    return jnp.concatenate([a * c - b * d, a * d + b * c], axis=0)


def back(grad, value):
    half = grad.shape[0] // 2
    a, b, c, d = grad[:half], grad[half:], value[:half], value[half:]
    return jnp.concatenate([a * c + b * d, b * c - a * d], axis=0)


def whole(shape):
    return pl.BlockSpec(shape, lambda *_: (0,) * len(shape))


def lanes(rows, width):
    return pl.BlockSpec((rows, width), lambda i, *_: (0, i))


def params(mib):
    return pltpu.CompilerParams(
        vmem_limit_bytes=mib * MIB, dimension_semantics=("arbitrary",)
    )


def in_hbm(array):
    return pltpu.with_memory_space_constraint(array, pltpu.HBM)


def cost(flops, moved):
    return pl.CostEstimate(flops=int(flops), bytes_accessed=int(moved), transcendentals=0)


def split_relation(relation):
    high = lax.reduce_precision(relation, 8, 7)
    rest = relation - high
    mid = lax.reduce_precision(rest, 8, 7)
    low = rest - mid
    parts = jnp.concatenate([high, mid, low], axis=1).astype(bf16)
    return jnp.pad(parts, ((0, 0), (0, (-parts.shape[1]) % 128)))


def relation_rows(rel_parts, ids, count):
    width = rel_parts.shape[1]
    places = lax.broadcasted_iota(jnp.int32, (width, ids.shape[1]), 0)
    hit = jnp.logical_and(places % count == ids, places < 3 * count)
    return dot_nn(rel_parts, jnp.where(hit, 1.0, 0.0).astype(bf16))


def make_queries(src_table, rel_parts, src_ids, rel_ids, rel_count, chunk, part, parts, before):
    dim, rows = src_table.shape
    edges = src_ids.shape[1]
    steps = edges // chunk // parts
    dtypes = (f32, bf16, f32)

    def body(table, parts_ref, src, rel, *refs):
        query, query_b, rows_out, high, low = refs[len(before) :]

        @pl.when(pl.program_id(0) == 0)
        def _():
            high[...], low[...] = split2(table[...])

        pick = select_rows(src[...], rows)
        src_rows = dot_nn(high[...], pick) + dot_nn(low[...], pick)
        rows_out[...] = src_rows
        value = product(src_rows, relation_rows(parts_ref[...], rel[...], rel_count))
        query[...] = value
        query_b[...] = value.astype(bf16)

    def columns(height):
        return pl.BlockSpec((height, chunk), lambda i: (0, i + part * steps))

    return pl.pallas_call(
        body,
        name="make_queries",
        grid=(steps,),
        in_specs=[whole((dim, rows)), whole(rel_parts.shape), columns(1), columns(1)]
        + [pl.BlockSpec(memory_space=pl.ANY)] * len(before),
        out_specs=[columns(dim)] * 3,
        out_shape=[pltpu.HBM((dim, edges), dtype) for dtype in dtypes],
        input_output_aliases={4 + i: i for i in range(len(before))},
        scratch_shapes=[pltpu.VMEM((dim, rows), bf16)] * 2,
        compiler_params=params(32),
        cost_estimate=cost(4 * dim * rows * edges // parts, 10 * dim * edges // parts),
    )(in_hbm(src_table), rel_parts, in_hbm(src_ids), in_hbm(rel_ids), *map(in_hbm, before))


def positives(part_high, query, dst_ids, chunk):
    dim, rows = part_high.shape
    edges = dst_ids.shape[1]

    def body(table, query_in, dst, query_grad, dst_grad):
        @pl.when(pl.program_id(0) == 0)
        def _():
            dst_grad[...] = jnp.zeros_like(dst_grad)

        pick = select_rows(dst[...], rows)
        dst_rows = dot_nn(table[...], pick)
        value = query_in[...]
        positive = jnp.sum(value * dst_rows, axis=0, keepdims=True)
        coef = -jax.nn.sigmoid(-positive)
        query_grad[...] = coef * dst_rows
        dst_grad[...] += dot_nt((coef * value).astype(bf16), pick)

    return pl.pallas_call(
        body,
        name="positives",
        grid=(edges // chunk,),
        in_specs=[whole((dim, rows)), lanes(dim, chunk), lanes(1, chunk)],
        out_specs=[lanes(dim, chunk), whole((dim, rows))],
        out_shape=[pltpu.HBM((dim, edges), f32), jax.ShapeDtypeStruct((dim, rows), f32)],
        compiler_params=params(32),
        cost_estimate=cost(6 * dim * rows * edges, 8 * dim * edges),
    )(part_high, in_hbm(query), in_hbm(dst_ids))


def negative_wave(tables, chip, quota, neg_ids, query_b, lane, chunk):
    count = len(tables)
    dim, rows = tables[0].shape
    edges = query_b.shape[1]
    slots = QMAX * count
    half_weight = 0.5 / math.sqrt(NNEG)

    def body(chip_ref, lane_ref, quota_ref, *refs):
        table_refs = refs[:count]
        ids, query_ref, neg, coef_out = refs[count : count + 4]
        grad_refs = refs[count + 4 : 2 * count + 4]
        neg_t, neg_grad = refs[2 * count + 4 :]

        live, at, base = [], [], [jnp.int32(0)]
        for s in range(count):
            spot = CORES * chip_ref[0] + (lane_ref[0] + s) % CORES
            at.append(spot)
            live.append(quota_ref[0, spot])
            base.append(base[-1] + live[-1])
        total = base[-1]

        step = pl.program_id(0)

        def picks(s, wide):
            parts = [select_rows(ids[at[s], b : b + 1, :], rows) for b in range(wide)]
            return jnp.concatenate(parts, axis=1) if wide > 1 else parts[0]

        def when_live(s, wide):
            return pl.when(jnp.logical_and(live[s] == wide, step == 0))

        def when_done(s, wide):
            return pl.when(jnp.logical_and(live[s] == wide, step == pl.num_programs(0) - 1))

        for s in range(count):
            for wide in range(1, QMAX + 1):

                @when_live(s, wide)
                def _(s=s, wide=wide):
                    value = dot_nn(table_refs[s][...], picks(s, wide))
                    for b in range(wide):
                        part = value[:, b * BLOCK : (b + 1) * BLOCK]
                        neg[base[s] + b] = part.astype(bf16)
                        neg_t[base[s] + b] = part.T.astype(bf16)
                        neg_grad[base[s] + b] = jnp.zeros((dim, BLOCK), f32)

        @pl.when(jnp.logical_and(total % 2 == 1, step == 0))
        def _():
            neg[total] = jnp.zeros((dim, BLOCK), bf16)
            neg_t[total] = jnp.zeros((BLOCK, dim), bf16)
            neg_grad[total] = jnp.zeros((dim, BLOCK), f32)

        def pair(p, carry):
            left, right = 2 * p, 2 * p + 1
            columns_t = jnp.concatenate([neg_t[left], neg_t[right]], axis=0)
            query = query_ref[...]
            scores = dot_nn(columns_t, query)
            coef = (half_weight * jnp.tanh(0.5 * scores) + half_weight).astype(bf16)
            coef_out[pl.ds(pl.multiple_of(left * BLOCK, 2 * BLOCK), 2 * BLOCK)] = coef
            added = dot_nt(query, coef)
            neg_grad[left] += added[:, :BLOCK]
            neg_grad[right] += added[:, BLOCK:]
            return carry

        lax.fori_loop(0, (total + 1) // 2, pair, 0)

        for s in range(count):

            @when_done(s, 0)
            def _(s=s):
                grad_refs[s][...] = jnp.zeros((dim, rows), bf16)

            for wide in range(1, QMAX + 1):

                @when_done(s, wide)
                def _(s=s, wide=wide):
                    parts = [neg_grad[base[s] + b] for b in range(wide)]
                    value = jnp.concatenate(parts, axis=1) if wide > 1 else parts[0]
                    high, low = split2(value)
                    pick = picks(s, wide)
                    grad_refs[s][...] = (dot_nt(high, pick) + dot_nt(low, pick)).astype(bf16)

    smem = pl.BlockSpec(memory_space=pltpu.SMEM)
    shard = jax.ShapeDtypeStruct((dim, rows), bf16)
    return pl.pallas_call(
        body,
        grid=(edges // chunk,),
        in_specs=[smem, smem, smem]
        + [whole((dim, rows))] * count
        + [whole(neg_ids.shape), lanes(dim, chunk)],
        out_specs=[whole((slots, dim, BLOCK)), lanes(slots * BLOCK, chunk)]
        + [whole((dim, rows))] * count,
        scratch_shapes=[
            pltpu.VMEM((slots, BLOCK, dim), bf16),
            pltpu.VMEM((slots, dim, BLOCK), f32),
        ],
        out_shape=[
            jax.ShapeDtypeStruct((slots, dim, BLOCK), bf16),
            pltpu.HBM((slots * BLOCK, edges), bf16),
        ]
        + [shard] * count,
        compiler_params=params(32),
        cost_estimate=cost(6 * dim * 1.5 * count * BLOCK * edges, 10 * dim * edges),
    )(chip, lane, quota, *tables, neg_ids, in_hbm(query_b))


def combine(src_rows, rel_ids, query_grad, negatives, coefs, chip, lane, quota, rel_count, chunk):
    dim, edges = src_rows.shape
    count = len(negatives)
    slots = negatives[0].shape[0]
    wide = 2 * BLOCK

    def body(chip_ref, lane_ref, quota_ref, rows_in, rel, grad_in, *refs):
        neg_refs, coef_refs = refs[:count], refs[count : 2 * count]
        grad_out, rel_out = refs[2 * count :]

        @pl.when(pl.program_id(0) == 0)
        def _():
            rel_out[...] = jnp.zeros_like(rel_out)

        grad_out[...] = grad_in[...]
        for k in range(count):
            first = CORES * (chip_ref[0] ^ k)
            total = quota_ref[0, first]
            for c in range(1, CORES):
                total = total + quota_ref[0, first + c]
            for pairs in range(1, slots // 2 + 1):

                @pl.when((total + 1) // 2 == pairs)
                def _(k=k, pairs=pairs):
                    columns = [neg_refs[k][j] for j in range(2 * pairs)]
                    columns = jnp.concatenate(columns, axis=1)
                    grad_out[...] += dot_nn(columns, coef_refs[k][: pairs * wide])

        kinds = select_rows(rel[...], rel_count)
        upper, lower = split2(back(grad_out[...], rows_in[...]))
        rel_out[...] += dot_nt(kinds, upper) + dot_nt(kinds, lower)

    smem = pl.BlockSpec(memory_space=pltpu.SMEM)
    return pl.pallas_call(
        body,
        name="combine",
        grid=(edges // chunk,),
        in_specs=[smem, smem, smem, lanes(dim, chunk), lanes(1, chunk), lanes(dim, chunk)]
        + [whole(negatives[0].shape)] * count
        + [lanes(slots * BLOCK, chunk)] * count,
        out_specs=[lanes(dim, chunk), whole((rel_count, dim))],
        out_shape=[
            pltpu.HBM((dim, edges), f32),
            jax.ShapeDtypeStruct((rel_count, dim), f32),
        ],
        compiler_params=params(44),
        cost_estimate=cost(2 * dim * NNEG * edges, 12 * dim * edges + 2 * NNEG * edges),
    )(
        chip,
        lane,
        quota,
        in_hbm(src_rows),
        in_hbm(rel_ids),
        in_hbm(query_grad),
        *negatives,
        *map(in_hbm, coefs),
    )


def source_side(src_table, src_state, rel_parts, src_ids, rel_ids, query_grad, rel_count, chunk):
    dim, rows = src_table.shape
    edges = src_ids.shape[1]

    def body(table, state, parts, src, rel, grad_in, out, state_out, acc):
        step = pl.program_id(0)

        @pl.when(step == 0)
        def _():
            acc[...] = jnp.zeros_like(acc)

        pick = select_rows(src[...], rows)
        term = back(grad_in[...], relation_rows(parts[...], rel[...], rel_count))
        acc[...] += dot_nt(term.astype(bf16), pick)

        @pl.when(step == pl.num_programs(0) - 1)
        def _():
            total = acc[...]
            new_state = state[...] + jnp.sum(total * total, axis=0, keepdims=True) / dim
            state_out[...] = new_state
            out[...] = table[...] - LEARN_RATE * total / jnp.sqrt(new_state)

    return pl.pallas_call(
        body,
        name="source_side",
        grid=(edges // chunk,),
        in_specs=[
            whole((dim, rows)),
            whole((1, rows)),
            whole(rel_parts.shape),
            lanes(1, chunk),
            lanes(1, chunk),
            lanes(dim, chunk),
        ],
        out_specs=[whole((dim, rows)), whole((1, rows))],
        out_shape=[
            jax.ShapeDtypeStruct((dim, rows), f32),
            jax.ShapeDtypeStruct((1, rows), f32),
        ],
        scratch_shapes=[pltpu.VMEM((dim, rows), f32)],
        compiler_params=params(24),
        cost_estimate=cost(4 * dim * rows * edges, 4 * dim * edges),
    )(
        in_hbm(src_table),
        in_hbm(src_state),
        rel_parts,
        in_hbm(src_ids),
        in_hbm(rel_ids),
        in_hbm(query_grad),
    )


def destination_side(high, low_state, own_grad, grads):
    dim, rows = own_grad.shape
    count = len(grads)

    def body(*refs):
        high_ref, low_ref, own_ref = refs[:3]
        out, state_out = refs[3 + count :]
        total = own_ref[...]
        for ref in refs[3 : 3 + count]:
            total = total + ref[...].astype(f32)
        packed = low_ref[...].astype(f32)
        state = packed[dim : dim + 1] + packed[dim + 1 : dim + 2] + packed[dim + 2 : dim + 3]
        new_state = state + jnp.sum(total * total, axis=0, keepdims=True) / dim
        state_out[...] = new_state
        table = high_ref[...].astype(f32) + packed[:dim]
        out[...] = table - LEARN_RATE * total / jnp.sqrt(new_state)

    width = min(rows, 128)

    operands = [high, low_state, own_grad, *grads]
    return pl.pallas_call(
        body,
        name="destination_side",
        grid=(rows // width,),
        in_specs=[lanes(array.shape[0], width) for array in operands],
        out_specs=[lanes(dim, width), lanes(1, width)],
        out_shape=[
            jax.ShapeDtypeStruct((dim, rows), f32),
            jax.ShapeDtypeStruct((1, rows), f32),
        ],
        compiler_params=params(16),
        cost_estimate=cost(8 * dim * rows, (12 + 2 * count) * dim * rows),
    )(*operands)


def split_table(table, state):
    dim, rows = table.shape
    half = rows // 2
    tail = 16

    def body(table_ref, state_ref, left, right, rest):
        value = table_ref[...]
        high, low = split2(value)
        left[...] = high[:, :half]
        right[...] = high[:, half:]
        rest[:dim] = low
        first, _ = split2(state_ref[...])
        left_over = state_ref[...] - first.astype(f32)
        second, third = split2(left_over)
        parts = [first.astype(f32), second.astype(f32), third.astype(f32)]
        parts.append(jnp.zeros((tail - 3, rows), f32))
        rest[dim:] = jnp.concatenate(parts, axis=0).astype(bf16)

    return pl.pallas_call(
        body,
        name="split_table",
        grid=(1,),
        in_specs=[whole((dim, rows)), whole((1, rows))],
        out_specs=[whole((dim, half)), whole((dim, rows - half)), whole((dim + tail, rows))],
        out_shape=[
            jax.ShapeDtypeStruct((dim, half), bf16),
            jax.ShapeDtypeStruct((dim, rows - half), bf16),
            jax.ShapeDtypeStruct((dim + tail, rows), bf16),
        ],
        compiler_params=params(16),
        cost_estimate=cost(4 * dim * rows, 8 * dim * rows),
    )(in_hbm(table), in_hbm(state))


def grid_of(count):
    across = math.isqrt(count)
    while count % across:
        across -= 1
    return count // across, across


def moved(device, n, stride, shift):
    place = (device // stride) % n
    return device + ((place + shift) % n - place) * stride


def shifted(array, n, stride, shift):
    count = lax.axis_size("dom")
    return lax.ppermute(array, "dom", [(d, moved(d, n, stride, shift)) for d in range(count)])


def copy_chosen(index, options, out, columns):
    for k in range(len(options)):

        @pl.when(index == k)
        def _(k=k):
            out[:, columns] = options[k][...]


def route(values, matching, here):
    down, across = grid_of(lax.axis_size("dom"))
    axes = [(across, 1), (down, across)]
    orders = [axes, axes[::-1]][: len(values)]
    rows = values[0].shape[0]
    widths = [value.shape[1] for value in values]
    starts = [sum(widths[:i]) for i in range(len(widths))]
    vmem = pl.BlockSpec(memory_space=pltpu.VMEM)
    smem = pl.BlockSpec(memory_space=pltpu.SMEM)

    held = []
    for i, ((n1, stride1), _) in enumerate(orders):
        held.append([values[i]] + [shifted(values[i], n1, stride1, k) for k in range(1, n1)])
    flat = [array for group in held for array in group]

    def grouped(refs, groups):
        result, used = [], 0
        for group in groups:
            result.append(refs[used : used + len(group)])
            used += len(group)
        return result, refs[used:]

    def behind(place, source, n, stride):
        return ((place // stride) % n - (source // stride) % n + n) % n

    def pass_on(match_ref, here_ref, *refs):
        place = here_ref[0]
        held_refs, outs = grouped(refs, held)
        used = 0
        for i, ((n1, stride1), (n2, stride2)) in enumerate(orders):
            for m in range(1, n2):
                source = match_ref[moved(place, n2, stride2, m)]
                picked = behind(place, source, n1, stride1)
                copy_chosen(picked, held_refs[i], outs[used], slice(None))
                used += 1

    hops = [(i, m) for i in range(len(orders)) for m in range(1, orders[i][1][0])]
    passed = pl.pallas_call(
        pass_on,
        in_specs=[smem, smem] + [vmem] * len(flat),
        out_specs=[vmem] * len(hops),
        out_shape=[jax.ShapeDtypeStruct((rows, widths[i]), bf16) for i, _ in hops],
        compiler_params=pltpu.CompilerParams(vmem_limit_bytes=16 * MIB),
        cost_estimate=cost(0, 4 * rows * sum(widths)),
    )(matching, here, *flat)
    found = [[] for _ in orders]
    for (i, m), array in zip(hops, passed):
        found[i].append(shifted(array, *orders[i][1], m))
    flat_found = [array for group in found for array in group]

    def merge(match_ref, here_ref, *refs):
        place = here_ref[0]
        held_refs, rest = grouped(refs, held)
        found_refs, (out,) = grouped(rest, found)
        source = match_ref[place]
        for i, ((n1, stride1), (n2, stride2)) in enumerate(orders):
            columns = slice(starts[i], starts[i] + widths[i])
            near = behind(place, source, n1, stride1)
            far = behind(place, source, n2, stride2)
            index = jnp.where(far == 0, near, n1 - 1 + far)
            copy_chosen(index, list(held_refs[i]) + list(found_refs[i]), out, columns)

    return pl.pallas_call(
        merge,
        in_specs=[smem, smem] + [vmem] * (len(flat) + len(flat_found)),
        out_specs=vmem,
        out_shape=jax.ShapeDtypeStruct((rows, sum(widths)), bf16),
        compiler_params=pltpu.CompilerParams(vmem_limit_bytes=24 * MIB),
        cost_estimate=cost(0, 4 * rows * sum(widths)),
    )(matching, here, *flat, *flat_found)


def total_of_peers(value, axis, stride, n):
    count = lax.axis_size(axis)

    def peer(i, k):
        digit = (i // stride) % n
        return i + ((digit ^ k) - digit) * stride

    terms = [value]
    for k in range(1, n):
        terms.append(lax.ppermute(value, axis, [(i, peer(i, k)) for i in range(count)]))
    while len(terms) > 1:
        terms = [terms[i] + terms[i + 1] for i in range(0, len(terms), 2)]
    return terms[0]


def total_over_mesh(value):
    down, across = grid_of(lax.axis_size("dom"))
    value = total_of_peers(value, "edge", 1, CORES)
    value = total_of_peers(value, "edge", CORES, lax.axis_size("edge") // CORES)
    if down * across <= 4:
        return total_of_peers(value, "dom", 1, down * across)
    value = total_of_peers(value, "dom", 1, across)
    return total_of_peers(value, "dom", across, down)


def shards(
    src_table,
    src_state,
    dst_table,
    dst_state,
    relation,
    edge_src,
    edge_dst,
    edge_rel,
    matching,
    neg_rows,
    quotas,
):
    edge_count = lax.axis_size("edge")
    chips = edge_count // CORES
    _, row_count = src_table.shape
    rel_count = relation.shape[1]
    edges = edge_src.shape[0]
    chunk = min(edges, 1024)
    wave_chunk = min(edges, 2048)
    here = lax.axis_index("edge").reshape(1).astype(jnp.int32)
    place = lax.axis_index("dom").reshape(1).astype(jnp.int32)

    src_ids = edge_src.reshape(1, edges)
    dst_ids = edge_dst.reshape(1, edges)
    rel_ids = edge_rel.reshape(1, edges)
    neg_ids = neg_rows.reshape(edge_count, QMAX, BLOCK)
    rel_parts = split_relation(relation)

    left, right, rest = split_table(dst_table, dst_state.reshape(1, row_count))
    part_high = route([left, right], matching, place)
    rest, part_high = lax.optimization_barrier((rest, part_high))
    low_state = route([rest], matching, place)

    made = []
    for part in range(2):
        made = make_queries(
            src_table, rel_parts, src_ids, rel_ids, rel_count, min(chunk, edges // 2), part, 2, made
        )
    query, query_b, src_rows = made
    query_grad, own_grad = positives(part_high, query, dst_ids, chunk)

    swap = [(i, i ^ 1) for i in range(edge_count)]

    def swapped(array):
        return lax.ppermute(array, "edge", swap)

    chip = here // CORES
    lane = here % CORES
    arrived, negatives, coefs = [], [], []
    done = [own_grad]
    for k in range(chips):
        pairs = [(i, i ^ (CORES * k)) for i in range(edge_count)]
        table = part_high
        if k:
            if k >= 2:
                table, _ = lax.optimization_barrier((table, done[k - 2]))
            table = lax.ppermute(table, "edge", pairs)
        live, coef, mine, theirs = negative_wave(
            [table, swapped(table)], chip ^ k, quotas, neg_ids, query_b, lane, wave_chunk
        )
        total = mine.astype(f32) + swapped(theirs).astype(f32)
        if k:
            total = lax.ppermute(total.astype(bf16), "edge", pairs)
        arrived.append(total)
        done.append(mine)
        negatives.append(live)
        coefs.append(coef)

    query_grad, rel_grad = combine(
        src_rows,
        rel_ids,
        query_grad,
        negatives,
        coefs,
        chip,
        lane,
        quotas,
        rel_count,
        chunk,
    )
    src_out, src_state_out = source_side(
        src_table,
        src_state.reshape(1, row_count),
        rel_parts,
        src_ids,
        rel_ids,
        query_grad,
        rel_count,
        chunk,
    )
    relation_out = relation - REL_RATE * total_over_mesh(rel_grad).T
    dst_out, dst_state_out = destination_side(part_high, low_state, own_grad, arrived)
    return (
        src_out,
        src_state_out.reshape(row_count),
        dst_out,
        dst_state_out.reshape(row_count),
        relation_out,
    )


def solution(mesh):
    in_specs = (
        P(None, ("dom", "edge")),
        P(("dom", "edge")),
        P(None, ("dom", "edge")),
        P(("dom", "edge")),
        P(),
        P(("dom", "edge")),
        P(("dom", "edge")),
        P(("dom", "edge")),
        P(),
        P(("dom", "edge"), None, None),
        P(("dom", "edge"), None),
    )
    out_specs = (
        P(None, ("dom", "edge")),
        P(("dom", "edge")),
        P(None, ("dom", "edge")),
        P(("dom", "edge")),
        P(),
    )

    return jax.shard_map(shards, mesh=mesh, in_specs=in_specs, out_specs=out_specs, check_vma=False)
```

```python
import math

import jax
import jax.numpy as jnp
from jax import lax
from jax.experimental import pallas as pl
from jax.experimental.pallas import tpu as pltpu
from jax.sharding import PartitionSpec as P

BLOCK = 128
QMAX = 2
QTOTAL = 12
NNEG = QTOTAL * BLOCK
CORES = 2
LEARN_RATE = 0.1
REL_RATE = 0.02


bf16 = jnp.bfloat16
f32 = jnp.float32
MIB = 2**20


def dot_nn(lhs, rhs):
    return lax.dot_general(lhs, rhs, (((1,), (0,)), ((), ())), preferred_element_type=f32)


def dot_nt(lhs, rhs):
    return lax.dot_general(lhs, rhs, (((1,), (1,)), ((), ())), preferred_element_type=f32)


def split2(value):
    high = value.astype(bf16)
    return high, (value - high.astype(f32)).astype(bf16)


def select_rows(ids, rows):
    places = lax.broadcasted_iota(jnp.int32, (rows, ids.shape[1]), 0)
    return jnp.where(places == ids, 1.0, 0.0).astype(bf16)


def product(one, other):
    half = one.shape[0] // 2
    a, b, c, d = one[:half], one[half:], other[:half], other[half:]
    return jnp.concatenate([a * c - b * d, a * d + b * c], axis=0)


def back(grad, value):
    half = grad.shape[0] // 2
    a, b, c, d = grad[:half], grad[half:], value[:half], value[half:]
    return jnp.concatenate([a * c + b * d, b * c - a * d], axis=0)


def whole(shape):
    return pl.BlockSpec(shape, lambda *_: (0,) * len(shape))


def lanes(rows, width):
    return pl.BlockSpec((rows, width), lambda i, *_: (0, i))


def params(mib):
    return pltpu.CompilerParams(
        vmem_limit_bytes=mib * MIB, dimension_semantics=("arbitrary",)
    )


def in_hbm(array):
    return pltpu.with_memory_space_constraint(array, pltpu.HBM)


def cost(flops, moved):
    return pl.CostEstimate(flops=int(flops), bytes_accessed=int(moved), transcendentals=0)


def split_relation(relation):
    high = lax.reduce_precision(relation, 8, 7)
    rest = relation - high
    mid = lax.reduce_precision(rest, 8, 7)
    low = rest - mid
    parts = jnp.concatenate([high, mid, low], axis=1).astype(bf16)
    return jnp.pad(parts, ((0, 0), (0, (-parts.shape[1]) % 128)))


def relation_rows(rel_parts, ids, count):
    width = rel_parts.shape[1]
    places = lax.broadcasted_iota(jnp.int32, (width, ids.shape[1]), 0)
    hit = jnp.logical_and(places % count == ids, places < 3 * count)
    return dot_nn(rel_parts, jnp.where(hit, 1.0, 0.0).astype(bf16))


def make_queries(src_table, rel_parts, src_ids, rel_ids, rel_count, chunk, part, parts, before):
    dim, rows = src_table.shape
    edges = src_ids.shape[1]
    steps = edges // chunk // parts
    dtypes = (f32, bf16, f32)

    def body(table, parts_ref, src, rel, *refs):
        query, query_b, rows_out, high, low = refs[len(before) :]

        @pl.when(pl.program_id(0) == 0)
        def _():
            high[...], low[...] = split2(table[...])

        pick = select_rows(src[...], rows)
        src_rows = dot_nn(high[...], pick) + dot_nn(low[...], pick)
        rows_out[...] = src_rows
        value = product(src_rows, relation_rows(parts_ref[...], rel[...], rel_count))
        query[...] = value
        query_b[...] = value.astype(bf16)

    def columns(height):
        return pl.BlockSpec((height, chunk), lambda i: (0, i + part * steps))

    return pl.pallas_call(
        body,
        name="make_queries",
        grid=(steps,),
        in_specs=[whole((dim, rows)), whole(rel_parts.shape), columns(1), columns(1)]
        + [pl.BlockSpec(memory_space=pl.ANY)] * len(before),
        out_specs=[columns(dim)] * 3,
        out_shape=[pltpu.HBM((dim, edges), dtype) for dtype in dtypes],
        input_output_aliases={4 + i: i for i in range(len(before))},
        scratch_shapes=[pltpu.VMEM((dim, rows), bf16)] * 2,
        compiler_params=params(32),
        cost_estimate=cost(4 * dim * rows * edges // parts, 10 * dim * edges // parts),
    )(in_hbm(src_table), rel_parts, in_hbm(src_ids), in_hbm(rel_ids), *map(in_hbm, before))


def positives(part_high, query, dst_ids, chunk):
    dim, rows = part_high.shape
    edges = dst_ids.shape[1]

    def body(table, query_in, dst, coefs, dst_grad):
        @pl.when(pl.program_id(0) == 0)
        def _():
            dst_grad[...] = jnp.zeros_like(dst_grad)

        pick = select_rows(dst[...], rows)
        dst_rows = dot_nn(table[...], pick)
        value = query_in[...]
        positive = jnp.sum(value * dst_rows, axis=0, keepdims=True)
        coef = -jax.nn.sigmoid(-positive)
        coefs[...] = coef
        dst_grad[...] += dot_nt((coef * value).astype(bf16), pick)

    return pl.pallas_call(
        body,
        name="positives",
        grid=(edges // chunk,),
        in_specs=[whole((dim, rows)), lanes(dim, chunk), lanes(1, chunk)],
        out_specs=[lanes(1, chunk), whole((dim, rows))],
        out_shape=[pltpu.HBM((1, edges), f32), jax.ShapeDtypeStruct((dim, rows), f32)],
        compiler_params=params(32),
        cost_estimate=cost(6 * dim * rows * edges, 8 * dim * edges),
    )(part_high, in_hbm(query), in_hbm(dst_ids))


def negative_wave(tables, chip, quota, neg_ids, query_b, lane, chunk):
    count = len(tables)
    dim, rows = tables[0].shape
    edges = query_b.shape[1]
    slots = QMAX * count
    half_weight = 0.5 / math.sqrt(NNEG)

    def body(chip_ref, lane_ref, quota_ref, *refs):
        table_refs = refs[:count]
        ids, query_ref, neg, coef_out = refs[count : count + 4]
        grad_refs = refs[count + 4 : 2 * count + 4]
        neg_t, neg_grad = refs[2 * count + 4 :]

        live, at, base = [], [], [jnp.int32(0)]
        for s in range(count):
            spot = CORES * chip_ref[0] + (lane_ref[0] + s) % CORES
            at.append(spot)
            live.append(quota_ref[0, spot])
            base.append(base[-1] + live[-1])
        total = base[-1]

        step = pl.program_id(0)

        def picks(s, wide):
            parts = [select_rows(ids[at[s], b : b + 1, :], rows) for b in range(wide)]
            return jnp.concatenate(parts, axis=1) if wide > 1 else parts[0]

        def when_live(s, wide):
            return pl.when(jnp.logical_and(live[s] == wide, step == 0))

        def when_done(s, wide):
            return pl.when(jnp.logical_and(live[s] == wide, step == pl.num_programs(0) - 1))

        for s in range(count):
            for wide in range(1, QMAX + 1):

                @when_live(s, wide)
                def _(s=s, wide=wide):
                    value = dot_nn(table_refs[s][...], picks(s, wide))
                    for b in range(wide):
                        part = value[:, b * BLOCK : (b + 1) * BLOCK]
                        neg[base[s] + b] = part.astype(bf16)
                        neg_t[base[s] + b] = part.T.astype(bf16)
                        neg_grad[base[s] + b] = jnp.zeros((dim, BLOCK), f32)

        @pl.when(jnp.logical_and(total % 2 == 1, step == 0))
        def _():
            neg[total] = jnp.zeros((dim, BLOCK), bf16)
            neg_t[total] = jnp.zeros((BLOCK, dim), bf16)
            neg_grad[total] = jnp.zeros((dim, BLOCK), f32)

        def pair(p, carry):
            left, right = 2 * p, 2 * p + 1
            columns_t = jnp.concatenate([neg_t[left], neg_t[right]], axis=0)
            query = query_ref[...]
            scores = dot_nn(columns_t, query)
            coef = (half_weight * jnp.tanh(0.5 * scores) + half_weight).astype(bf16)
            coef_out[pl.ds(pl.multiple_of(left * BLOCK, 2 * BLOCK), 2 * BLOCK)] = coef
            added = dot_nt(query, coef)
            neg_grad[left] += added[:, :BLOCK]
            neg_grad[right] += added[:, BLOCK:]
            return carry

        lax.fori_loop(0, (total + 1) // 2, pair, 0)

        for s in range(count):

            @when_done(s, 0)
            def _(s=s):
                grad_refs[s][...] = jnp.zeros((dim, rows), bf16)

            for wide in range(1, QMAX + 1):

                @when_done(s, wide)
                def _(s=s, wide=wide):
                    parts = [neg_grad[base[s] + b] for b in range(wide)]
                    value = jnp.concatenate(parts, axis=1) if wide > 1 else parts[0]
                    high, low = split2(value)
                    pick = picks(s, wide)
                    grad_refs[s][...] = (dot_nt(high, pick) + dot_nt(low, pick)).astype(bf16)

    smem = pl.BlockSpec(memory_space=pltpu.SMEM)
    shard = jax.ShapeDtypeStruct((dim, rows), bf16)
    return pl.pallas_call(
        body,
        grid=(edges // chunk,),
        in_specs=[smem, smem, smem]
        + [whole((dim, rows))] * count
        + [whole(neg_ids.shape), lanes(dim, chunk)],
        out_specs=[whole((slots, dim, BLOCK)), lanes(slots * BLOCK, chunk)]
        + [whole((dim, rows))] * count,
        scratch_shapes=[
            pltpu.VMEM((slots, BLOCK, dim), bf16),
            pltpu.VMEM((slots, dim, BLOCK), f32),
        ],
        out_shape=[
            jax.ShapeDtypeStruct((slots, dim, BLOCK), bf16),
            pltpu.HBM((slots * BLOCK, edges), bf16),
        ]
        + [shard] * count,
        compiler_params=params(32),
        cost_estimate=cost(6 * dim * 1.5 * count * BLOCK * edges, 10 * dim * edges),
    )(chip, lane, quota, *tables, neg_ids, in_hbm(query_b))


def combine(
    src_rows, rel_ids, part_high, dst_ids, pos_coef, negatives, coefs, chip, lane, quota, rel_count, chunk
):
    dim, edges = src_rows.shape
    rows = part_high.shape[1]
    count = len(negatives)
    slots = negatives[0].shape[0]
    wide = 2 * BLOCK

    def body(chip_ref, lane_ref, quota_ref, rows_in, rel, table, dst, pos, *refs):
        neg_refs, coef_refs = refs[:count], refs[count : 2 * count]
        grad_out, rel_out = refs[2 * count :]

        @pl.when(pl.program_id(0) == 0)
        def _():
            rel_out[...] = jnp.zeros_like(rel_out)

        dst_rows = dot_nn(table[...], select_rows(dst[...], rows))
        grad_out[...] = pos[...] * dst_rows
        for k in range(count):
            first = CORES * (chip_ref[0] ^ k)
            total = quota_ref[0, first]
            for c in range(1, CORES):
                total = total + quota_ref[0, first + c]
            for pairs in range(1, slots // 2 + 1):

                @pl.when((total + 1) // 2 == pairs)
                def _(k=k, pairs=pairs):
                    columns = [neg_refs[k][j] for j in range(2 * pairs)]
                    columns = jnp.concatenate(columns, axis=1)
                    grad_out[...] += dot_nn(columns, coef_refs[k][: pairs * wide])

        kinds = select_rows(rel[...], rel_count)
        upper, lower = split2(back(grad_out[...], rows_in[...]))
        rel_out[...] += dot_nt(kinds, upper) + dot_nt(kinds, lower)

    smem = pl.BlockSpec(memory_space=pltpu.SMEM)
    return pl.pallas_call(
        body,
        name="combine",
        grid=(edges // chunk,),
        in_specs=[smem, smem, smem, lanes(dim, chunk), lanes(1, chunk)]
        + [whole((dim, rows)), lanes(1, chunk), lanes(1, chunk)]
        + [whole(negatives[0].shape)] * count
        + [lanes(slots * BLOCK, chunk)] * count,
        out_specs=[lanes(dim, chunk), whole((rel_count, dim))],
        out_shape=[
            pltpu.HBM((dim, edges), f32),
            jax.ShapeDtypeStruct((rel_count, dim), f32),
        ],
        compiler_params=params(44),
        cost_estimate=cost(2 * dim * NNEG * edges, 12 * dim * edges + 2 * NNEG * edges),
    )(
        chip,
        lane,
        quota,
        in_hbm(src_rows),
        in_hbm(rel_ids),
        part_high,
        in_hbm(dst_ids),
        in_hbm(pos_coef),
        *negatives,
        *map(in_hbm, coefs),
    )


def source_side(src_table, src_state, rel_parts, src_ids, rel_ids, query_grad, rel_count, chunk):
    dim, rows = src_table.shape
    edges = src_ids.shape[1]

    def body(table, state, parts, src, rel, grad_in, out, state_out, acc):
        step = pl.program_id(0)

        @pl.when(step == 0)
        def _():
            acc[...] = jnp.zeros_like(acc)

        pick = select_rows(src[...], rows)
        term = back(grad_in[...], relation_rows(parts[...], rel[...], rel_count))
        acc[...] += dot_nt(term.astype(bf16), pick)

        @pl.when(step == pl.num_programs(0) - 1)
        def _():
            total = acc[...]
            new_state = state[...] + jnp.sum(total * total, axis=0, keepdims=True) / dim
            state_out[...] = new_state
            out[...] = table[...] - LEARN_RATE * total / jnp.sqrt(new_state)

    return pl.pallas_call(
        body,
        name="source_side",
        grid=(edges // chunk,),
        in_specs=[
            whole((dim, rows)),
            whole((1, rows)),
            whole(rel_parts.shape),
            lanes(1, chunk),
            lanes(1, chunk),
            lanes(dim, chunk),
        ],
        out_specs=[whole((dim, rows)), whole((1, rows))],
        out_shape=[
            jax.ShapeDtypeStruct((dim, rows), f32),
            jax.ShapeDtypeStruct((1, rows), f32),
        ],
        scratch_shapes=[pltpu.VMEM((dim, rows), f32)],
        compiler_params=params(24),
        cost_estimate=cost(4 * dim * rows * edges, 4 * dim * edges),
    )(
        in_hbm(src_table),
        in_hbm(src_state),
        rel_parts,
        in_hbm(src_ids),
        in_hbm(rel_ids),
        in_hbm(query_grad),
    )


def destination_side(high, low_state, own_grad, grads):
    dim, rows = own_grad.shape
    count = len(grads)

    def body(*refs):
        high_ref, low_ref, own_ref = refs[:3]
        out, state_out = refs[3 + count :]
        total = own_ref[...]
        for ref in refs[3 : 3 + count]:
            total = total + ref[...].astype(f32)
        packed = low_ref[...].astype(f32)
        state = packed[dim : dim + 1] + packed[dim + 1 : dim + 2] + packed[dim + 2 : dim + 3]
        new_state = state + jnp.sum(total * total, axis=0, keepdims=True) / dim
        state_out[...] = new_state
        table = high_ref[...].astype(f32) + packed[:dim]
        out[...] = table - LEARN_RATE * total / jnp.sqrt(new_state)

    width = min(rows, 128)

    operands = [high, low_state, own_grad, *grads]
    return pl.pallas_call(
        body,
        name="destination_side",
        grid=(rows // width,),
        in_specs=[lanes(array.shape[0], width) for array in operands],
        out_specs=[lanes(dim, width), lanes(1, width)],
        out_shape=[
            jax.ShapeDtypeStruct((dim, rows), f32),
            jax.ShapeDtypeStruct((1, rows), f32),
        ],
        compiler_params=params(16),
        cost_estimate=cost(8 * dim * rows, (12 + 2 * count) * dim * rows),
    )(*operands)


def split_table(table, state):
    dim, rows = table.shape
    half = rows // 2
    tail = 16

    def body(table_ref, state_ref, left, right, rest):
        value = table_ref[...]
        high, low = split2(value)
        left[...] = high[:, :half]
        right[...] = high[:, half:]
        rest[:dim] = low
        first, _ = split2(state_ref[...])
        left_over = state_ref[...] - first.astype(f32)
        second, third = split2(left_over)
        parts = [first.astype(f32), second.astype(f32), third.astype(f32)]
        parts.append(jnp.zeros((tail - 3, rows), f32))
        rest[dim:] = jnp.concatenate(parts, axis=0).astype(bf16)

    return pl.pallas_call(
        body,
        name="split_table",
        grid=(1,),
        in_specs=[whole((dim, rows)), whole((1, rows))],
        out_specs=[whole((dim, half)), whole((dim, rows - half)), whole((dim + tail, rows))],
        out_shape=[
            jax.ShapeDtypeStruct((dim, half), bf16),
            jax.ShapeDtypeStruct((dim, rows - half), bf16),
            jax.ShapeDtypeStruct((dim + tail, rows), bf16),
        ],
        compiler_params=params(16),
        cost_estimate=cost(4 * dim * rows, 8 * dim * rows),
    )(in_hbm(table), in_hbm(state))


def grid_of(count):
    across = math.isqrt(count)
    while count % across:
        across -= 1
    return count // across, across


def moved(device, n, stride, shift):
    place = (device // stride) % n
    return device + ((place + shift) % n - place) * stride


def shifted(array, n, stride, shift):
    count = lax.axis_size("dom")
    return lax.ppermute(array, "dom", [(d, moved(d, n, stride, shift)) for d in range(count)])


def copy_chosen(index, options, out, columns):
    for k in range(len(options)):

        @pl.when(index == k)
        def _(k=k):
            out[:, columns] = options[k][...]


def route(values, matching, here):
    down, across = grid_of(lax.axis_size("dom"))
    axes = [(across, 1), (down, across)]
    orders = [axes, axes[::-1]][: len(values)]
    rows = values[0].shape[0]
    widths = [value.shape[1] for value in values]
    starts = [sum(widths[:i]) for i in range(len(widths))]
    vmem = pl.BlockSpec(memory_space=pltpu.VMEM)
    smem = pl.BlockSpec(memory_space=pltpu.SMEM)

    held = []
    for i, ((n1, stride1), _) in enumerate(orders):
        held.append([values[i]] + [shifted(values[i], n1, stride1, k) for k in range(1, n1)])
    flat = [array for group in held for array in group]

    def grouped(refs, groups):
        result, used = [], 0
        for group in groups:
            result.append(refs[used : used + len(group)])
            used += len(group)
        return result, refs[used:]

    def behind(place, source, n, stride):
        return ((place // stride) % n - (source // stride) % n + n) % n

    def pass_on(match_ref, here_ref, *refs):
        place = here_ref[0]
        held_refs, outs = grouped(refs, held)
        used = 0
        for i, ((n1, stride1), (n2, stride2)) in enumerate(orders):
            for m in range(1, n2):
                source = match_ref[moved(place, n2, stride2, m)]
                picked = behind(place, source, n1, stride1)
                copy_chosen(picked, held_refs[i], outs[used], slice(None))
                used += 1

    hops = [(i, m) for i in range(len(orders)) for m in range(1, orders[i][1][0])]
    passed = pl.pallas_call(
        pass_on,
        in_specs=[smem, smem] + [vmem] * len(flat),
        out_specs=[vmem] * len(hops),
        out_shape=[jax.ShapeDtypeStruct((rows, widths[i]), bf16) for i, _ in hops],
        compiler_params=pltpu.CompilerParams(vmem_limit_bytes=16 * MIB),
        cost_estimate=cost(0, 4 * rows * sum(widths)),
    )(matching, here, *flat)
    found = [[] for _ in orders]
    for (i, m), array in zip(hops, passed):
        found[i].append(shifted(array, *orders[i][1], m))
    flat_found = [array for group in found for array in group]

    def merge(match_ref, here_ref, *refs):
        place = here_ref[0]
        held_refs, rest = grouped(refs, held)
        found_refs, (out,) = grouped(rest, found)
        source = match_ref[place]
        for i, ((n1, stride1), (n2, stride2)) in enumerate(orders):
            columns = slice(starts[i], starts[i] + widths[i])
            near = behind(place, source, n1, stride1)
            far = behind(place, source, n2, stride2)
            index = jnp.where(far == 0, near, n1 - 1 + far)
            copy_chosen(index, list(held_refs[i]) + list(found_refs[i]), out, columns)

    return pl.pallas_call(
        merge,
        in_specs=[smem, smem] + [vmem] * (len(flat) + len(flat_found)),
        out_specs=vmem,
        out_shape=jax.ShapeDtypeStruct((rows, sum(widths)), bf16),
        compiler_params=pltpu.CompilerParams(vmem_limit_bytes=24 * MIB),
        cost_estimate=cost(0, 4 * rows * sum(widths)),
    )(matching, here, *flat, *flat_found)


def total_of_peers(value, axis, stride, n):
    count = lax.axis_size(axis)

    def peer(i, k):
        digit = (i // stride) % n
        return i + ((digit ^ k) - digit) * stride

    terms = [value]
    for k in range(1, n):
        terms.append(lax.ppermute(value, axis, [(i, peer(i, k)) for i in range(count)]))
    while len(terms) > 1:
        terms = [terms[i] + terms[i + 1] for i in range(0, len(terms), 2)]
    return terms[0]


def total_over_mesh(value):
    down, across = grid_of(lax.axis_size("dom"))
    value = total_of_peers(value, "edge", 1, CORES)
    value = total_of_peers(value, "edge", CORES, lax.axis_size("edge") // CORES)
    if down * across <= 4:
        return total_of_peers(value, "dom", 1, down * across)
    value = total_of_peers(value, "dom", 1, across)
    return total_of_peers(value, "dom", across, down)


def shards(
    src_table,
    src_state,
    dst_table,
    dst_state,
    relation,
    edge_src,
    edge_dst,
    edge_rel,
    matching,
    neg_rows,
    quotas,
):
    edge_count = lax.axis_size("edge")
    chips = edge_count // CORES
    _, row_count = src_table.shape
    rel_count = relation.shape[1]
    edges = edge_src.shape[0]
    chunk = min(edges, 1024)
    wave_chunk = min(edges, 2048)
    here = lax.axis_index("edge").reshape(1).astype(jnp.int32)
    place = lax.axis_index("dom").reshape(1).astype(jnp.int32)

    src_ids = edge_src.reshape(1, edges)
    dst_ids = edge_dst.reshape(1, edges)
    rel_ids = edge_rel.reshape(1, edges)
    neg_ids = neg_rows.reshape(edge_count, QMAX, BLOCK)
    rel_parts = split_relation(relation)

    left, right, rest = split_table(dst_table, dst_state.reshape(1, row_count))
    part_high = route([left, right], matching, place)
    rest, part_high = lax.optimization_barrier((rest, part_high))
    low_state = route([rest], matching, place)

    made = []
    for part in range(2):
        made = make_queries(
            src_table, rel_parts, src_ids, rel_ids, rel_count, min(chunk, edges // 2), part, 2, made
        )
    query, query_b, src_rows = made
    pos_coef, own_grad = positives(part_high, query, dst_ids, chunk)

    swap = [(i, i ^ 1) for i in range(edge_count)]

    def swapped(array):
        return lax.ppermute(array, "edge", swap)

    chip = here // CORES
    lane = here % CORES
    arrived, negatives, coefs = [], [], []
    done, brought = [own_grad], {}
    for k in range(chips):
        pairs = [(i, i ^ (CORES * k)) for i in range(edge_count)]
        near = k & -k
        table = brought.get(k - near, part_high)
        if k:
            if k == near >= 2:
                table, _ = lax.optimization_barrier((table, done[k // 2 - 1]))
            hop = [(i, i ^ (CORES * near)) for i in range(edge_count)]
            table = lax.ppermute(table, "edge", hop)
        brought[k] = table
        live, coef, mine, theirs = negative_wave(
            [table, swapped(table)], chip ^ k, quotas, neg_ids, query_b, lane, wave_chunk
        )
        total = mine.astype(f32) + swapped(theirs).astype(f32)
        if k:
            total = lax.ppermute(total.astype(bf16), "edge", pairs)
        arrived.append(total)
        done.append(mine)
        negatives.append(live)
        coefs.append(coef)

    query_grad, rel_grad = combine(
        src_rows,
        rel_ids,
        part_high,
        dst_ids,
        pos_coef,
        negatives,
        coefs,
        chip,
        lane,
        quotas,
        rel_count,
        chunk,
    )
    src_out, src_state_out = source_side(
        src_table,
        src_state.reshape(1, row_count),
        rel_parts,
        src_ids,
        rel_ids,
        query_grad,
        rel_count,
        chunk,
    )
    relation_out = relation - REL_RATE * total_over_mesh(rel_grad).T
    dst_out, dst_state_out = destination_side(part_high, low_state, own_grad, arrived)
    return (
        src_out,
        src_state_out.reshape(row_count),
        dst_out,
        dst_state_out.reshape(row_count),
        relation_out,
    )


def solution(mesh):
    in_specs = (
        P(None, ("dom", "edge")),
        P(("dom", "edge")),
        P(None, ("dom", "edge")),
        P(("dom", "edge")),
        P(),
        P(("dom", "edge")),
        P(("dom", "edge")),
        P(("dom", "edge")),
        P(),
        P(("dom", "edge"), None, None),
        P(("dom", "edge"), None),
    )
    out_specs = (
        P(None, ("dom", "edge")),
        P(("dom", "edge")),
        P(None, ("dom", "edge")),
        P(("dom", "edge")),
        P(),
    )

    return jax.shard_map(shards, mesh=mesh, in_specs=in_specs, out_specs=out_specs, check_vma=False)
```

```python
import math

import jax
import jax.numpy as jnp
from jax import lax
from jax.experimental import pallas as pl
from jax.experimental.pallas import tpu as pltpu
from jax.sharding import PartitionSpec as P

BLOCK = 128
QMAX = 2
QTOTAL = 12
NNEG = QTOTAL * BLOCK
CORES = 2
LEARN_RATE = 0.1
REL_RATE = 0.02
SUB = 1024


bf16 = jnp.bfloat16
f32 = jnp.float32
MIB = 2**20


def dot_nn(lhs, rhs):
    return lax.dot_general(lhs, rhs, (((1,), (0,)), ((), ())), preferred_element_type=f32)


def dot_nt(lhs, rhs):
    return lax.dot_general(lhs, rhs, (((1,), (1,)), ((), ())), preferred_element_type=f32)


def split2(value):
    high = value.astype(bf16)
    return high, (value - high.astype(f32)).astype(bf16)


def select_rows(ids, rows):
    places = lax.broadcasted_iota(jnp.int32, (rows, ids.shape[1]), 0)
    return jnp.where(places == ids, 1.0, 0.0).astype(bf16)


def product(one, other):
    half = one.shape[0] // 2
    a, b, c, d = one[:half], one[half:], other[:half], other[half:]
    return jnp.concatenate([a * c - b * d, a * d + b * c], axis=0)


def back(grad, value):
    half = grad.shape[0] // 2
    a, b, c, d = grad[:half], grad[half:], value[:half], value[half:]
    return jnp.concatenate([a * c + b * d, b * c - a * d], axis=0)


def whole(shape):
    return pl.BlockSpec(shape, lambda *_: (0,) * len(shape))


def lanes(rows, width):
    return pl.BlockSpec((rows, width), lambda i, *_: (0, i))


def params(mib):
    return pltpu.CompilerParams(
        vmem_limit_bytes=mib * MIB, dimension_semantics=("arbitrary",)
    )


def in_hbm(array):
    return pltpu.with_memory_space_constraint(array, pltpu.HBM)


def cost(flops, moved):
    return pl.CostEstimate(flops=int(flops), bytes_accessed=int(moved), transcendentals=0)


def split_relation(relation):
    high = lax.reduce_precision(relation, 8, 7)
    rest = relation - high
    mid = lax.reduce_precision(rest, 8, 7)
    low = rest - mid
    parts = jnp.concatenate([high, mid, low], axis=1).astype(bf16)
    return jnp.pad(parts, ((0, 0), (0, (-parts.shape[1]) % 128)))


def relation_rows(rel_parts, ids, count):
    width = rel_parts.shape[1]
    places = lax.broadcasted_iota(jnp.int32, (width, ids.shape[1]), 0)
    hit = jnp.logical_and(places % count == ids, places < 3 * count)
    return dot_nn(rel_parts, jnp.where(hit, 1.0, 0.0).astype(bf16))


def make_queries(src_table, rel_parts, src_ids, rel_ids, rel_count, chunk, part, parts, before):
    dim, rows = src_table.shape
    edges = src_ids.shape[1]
    steps = edges // chunk // parts
    dtypes = (f32, bf16, f32)

    def body(table, parts_ref, src, rel, *refs):
        query, query_b, rows_out, high, low = refs[len(before) :]

        @pl.when(pl.program_id(0) == 0)
        def _():
            high[...], low[...] = split2(table[...])

        pick = select_rows(src[...], rows)
        src_rows = dot_nn(high[...], pick) + dot_nn(low[...], pick)
        rows_out[...] = src_rows
        value = product(src_rows, relation_rows(parts_ref[...], rel[...], rel_count))
        query[...] = value
        query_b[...] = value.astype(bf16)

    def columns(height):
        return pl.BlockSpec((height, chunk), lambda i: (0, i + part * steps))

    return pl.pallas_call(
        body,
        name="make_queries",
        grid=(steps,),
        in_specs=[whole((dim, rows)), whole(rel_parts.shape), columns(1), columns(1)]
        + [pl.BlockSpec(memory_space=pl.ANY)] * len(before),
        out_specs=[columns(dim)] * 3,
        out_shape=[pltpu.HBM((dim, edges), dtype) for dtype in dtypes],
        input_output_aliases={4 + i: i for i in range(len(before))},
        scratch_shapes=[pltpu.VMEM((dim, rows), bf16)] * 2,
        compiler_params=params(32),
        cost_estimate=cost(4 * dim * rows * edges // parts, 10 * dim * edges // parts),
    )(in_hbm(src_table), rel_parts, in_hbm(src_ids), in_hbm(rel_ids), *map(in_hbm, before))


def positives(part_high, query, dst_ids, chunk):
    dim, rows = part_high.shape
    edges = dst_ids.shape[1]

    def body(table, query_in, dst, coefs, dst_grad):
        @pl.when(pl.program_id(0) == 0)
        def _():
            dst_grad[...] = jnp.zeros_like(dst_grad)

        pick = select_rows(dst[...], rows)
        dst_rows = dot_nn(table[...], pick)
        value = query_in[...]
        positive = jnp.sum(value * dst_rows, axis=0, keepdims=True)
        coef = -jax.nn.sigmoid(-positive)
        coefs[...] = coef
        dst_grad[...] += dot_nt((coef * value).astype(bf16), pick)

    return pl.pallas_call(
        body,
        name="positives",
        grid=(edges // chunk,),
        in_specs=[whole((dim, rows)), lanes(dim, chunk), lanes(1, chunk)],
        out_specs=[lanes(1, chunk), whole((dim, rows))],
        out_shape=[pltpu.HBM((1, edges), f32), jax.ShapeDtypeStruct((dim, rows), f32)],
        compiler_params=params(32),
        cost_estimate=cost(6 * dim * rows * edges, 8 * dim * edges),
    )(part_high, in_hbm(query), in_hbm(dst_ids))


def negative_wave(tables, chip, quota, neg_ids, query_b, lane, chunk):
    count = len(tables)
    dim, rows = tables[0].shape
    edges = query_b.shape[1]
    slots = QMAX * count
    half_weight = 0.5 / math.sqrt(NNEG)

    def body(chip_ref, lane_ref, quota_ref, *refs):
        table_refs = refs[:count]
        ids, query_ref, neg, coef_out = refs[count : count + 4]
        grad_refs = refs[count + 4 : 2 * count + 4]
        neg_t, neg_grad = refs[2 * count + 4 :]

        live, at, base = [], [], [jnp.int32(0)]
        for s in range(count):
            spot = CORES * chip_ref[0] + (lane_ref[0] + s) % CORES
            at.append(spot)
            live.append(quota_ref[0, spot])
            base.append(base[-1] + live[-1])
        total = base[-1]

        step = pl.program_id(0)

        def picks(s, wide):
            parts = [select_rows(ids[at[s], b : b + 1, :], rows) for b in range(wide)]
            return jnp.concatenate(parts, axis=1) if wide > 1 else parts[0]

        def when_live(s, wide):
            return pl.when(jnp.logical_and(live[s] == wide, step == 0))

        def when_done(s, wide):
            return pl.when(jnp.logical_and(live[s] == wide, step == pl.num_programs(0) - 1))

        for s in range(count):
            for wide in range(1, QMAX + 1):

                @when_live(s, wide)
                def _(s=s, wide=wide):
                    value = dot_nn(table_refs[s][...], picks(s, wide))
                    for b in range(wide):
                        part = value[:, b * BLOCK : (b + 1) * BLOCK]
                        neg[base[s] + b] = part.astype(bf16)
                        neg_t[base[s] + b] = part.T.astype(bf16)
                        neg_grad[base[s] + b] = jnp.zeros((dim, BLOCK), f32)

        @pl.when(jnp.logical_and(total % 2 == 1, step == 0))
        def _():
            neg[total] = jnp.zeros((dim, BLOCK), bf16)
            neg_t[total] = jnp.zeros((BLOCK, dim), bf16)
            neg_grad[total] = jnp.zeros((dim, BLOCK), f32)

        for pairs in range(1, slots // 2 + 1):

            @pl.when((total + 1) // 2 == pairs)
            def _(blocks=2 * pairs):
                query = query_ref[...]
                rows_t = jnp.concatenate([neg_t[j] for j in range(blocks)], axis=0)
                scores = dot_nn(rows_t, query)
                coef = (half_weight * jnp.tanh(0.5 * scores) + half_weight).astype(bf16)
                coef_out[: blocks * BLOCK] = coef
                added = dot_nt(query, coef)
                for j in range(blocks):
                    neg_grad[j] += added[:, j * BLOCK : (j + 1) * BLOCK]

        for p in range(slots // 2):

            @pl.when(p >= (total + 1) // 2)
            def _(p=p):
                coef_out[2 * p * BLOCK : 2 * (p + 1) * BLOCK] = jnp.zeros((2 * BLOCK, chunk), bf16)
                neg[2 * p] = jnp.zeros((dim, BLOCK), bf16)
                neg[2 * p + 1] = jnp.zeros((dim, BLOCK), bf16)

        for s in range(count):

            @when_done(s, 0)
            def _(s=s):
                grad_refs[s][...] = jnp.zeros((dim, rows), bf16)

            for wide in range(1, QMAX + 1):

                @when_done(s, wide)
                def _(s=s, wide=wide):
                    parts = [neg_grad[base[s] + b] for b in range(wide)]
                    value = jnp.concatenate(parts, axis=1) if wide > 1 else parts[0]
                    grad_refs[s][...] = dot_nt(value.astype(bf16), picks(s, wide)).astype(bf16)

    smem = pl.BlockSpec(memory_space=pltpu.SMEM)
    shard = jax.ShapeDtypeStruct((dim, rows), bf16)
    return pl.pallas_call(
        body,
        grid=(edges // chunk,),
        in_specs=[smem, smem, smem]
        + [whole((dim, rows))] * count
        + [whole(neg_ids.shape), lanes(dim, chunk)],
        out_specs=[whole((slots, dim, BLOCK)), lanes(slots * BLOCK, chunk)]
        + [whole((dim, rows))] * count,
        scratch_shapes=[
            pltpu.VMEM((slots, BLOCK, dim), bf16),
            pltpu.VMEM((slots, dim, BLOCK), f32),
        ],
        out_shape=[
            jax.ShapeDtypeStruct((slots, dim, BLOCK), bf16),
            pltpu.HBM((slots * BLOCK, edges), bf16),
        ]
        + [shard] * count,
        compiler_params=params(32),
        cost_estimate=cost(6 * dim * 1.5 * count * BLOCK * edges, 10 * dim * edges),
    )(chip, lane, quota, *tables, neg_ids, in_hbm(query_b))


def combine(
    src_rows, rel_ids, part_high, dst_ids, pos_coef, negatives, coefs, rel_count, chunk
):
    dim, edges = src_rows.shape
    rows = part_high.shape[1]
    count = len(negatives)
    slots = negatives[0].shape[0]
    sub = min(SUB, chunk)

    def body(rows_in, rel, table, dst, pos, *refs):
        neg_refs, coef_refs = refs[:count], refs[count : 2 * count]
        grad_out, rel_out, all_neg = refs[2 * count :]

        @pl.when(pl.program_id(0) == 0)
        def _():
            rel_out[...] = jnp.zeros_like(rel_out)
            for k in range(count):
                for j in range(slots):
                    all_neg[k, :, j * BLOCK : (j + 1) * BLOCK] = neg_refs[k][j]

        found = None
        for h in range(chunk // sub):
            part = slice(h * sub, (h + 1) * sub)
            grad = pos[:, part] * dot_nn(table[...], select_rows(dst[:, part], rows))
            for k in range(count):
                grad = grad + dot_nn(all_neg[k], coef_refs[k][:, part])
            grad_out[:, part] = grad
            kinds = select_rows(rel[:, part], rel_count)
            upper, lower = split2(back(grad, rows_in[:, part]))
            more = dot_nt(kinds, upper) + dot_nt(kinds, lower)
            found = more if found is None else found + more
        rel_out[...] += found

    return pl.pallas_call(
        body,
        name="combine",
        grid=(edges // chunk,),
        in_specs=[lanes(dim, chunk), lanes(1, chunk)]
        + [whole((dim, rows)), lanes(1, chunk), lanes(1, chunk)]
        + [whole(negatives[0].shape)] * count
        + [lanes(slots * BLOCK, chunk)] * count,
        out_specs=[lanes(dim, chunk), whole((rel_count, dim))],
        out_shape=[
            pltpu.HBM((dim, edges), f32),
            jax.ShapeDtypeStruct((rel_count, dim), f32),
        ],
        scratch_shapes=[pltpu.VMEM((count, dim, slots * BLOCK), bf16)],
        compiler_params=params(48),
        cost_estimate=cost(2 * dim * NNEG * edges, 12 * dim * edges + 2 * NNEG * edges),
    )(
        in_hbm(src_rows),
        in_hbm(rel_ids),
        part_high,
        in_hbm(dst_ids),
        in_hbm(pos_coef),
        *negatives,
        *map(in_hbm, coefs),
    )


def source_side(src_table, src_state, rel_parts, src_ids, rel_ids, query_grad, rel_count, chunk):
    dim, rows = src_table.shape
    edges = src_ids.shape[1]
    sub = min(SUB, chunk)

    def body(table, state, parts, src, rel, grad_in, out, state_out, acc):
        step = pl.program_id(0)

        @pl.when(step == 0)
        def _():
            acc[...] = jnp.zeros_like(acc)

        found = None
        for h in range(chunk // sub):
            part = slice(h * sub, (h + 1) * sub)
            pick = select_rows(src[:, part], rows)
            rel_rows = relation_rows(parts[...], rel[:, part], rel_count)
            term = back(grad_in[:, part], rel_rows).astype(bf16)
            more = dot_nt(term, pick)
            found = more if found is None else found + more
        acc[...] += found

        @pl.when(step == pl.num_programs(0) - 1)
        def _():
            total = acc[...]
            new_state = state[...] + jnp.sum(total * total, axis=0, keepdims=True) / dim
            state_out[...] = new_state
            out[...] = table[...] - LEARN_RATE * total / jnp.sqrt(new_state)

    return pl.pallas_call(
        body,
        name="source_side",
        grid=(edges // chunk,),
        in_specs=[
            whole((dim, rows)),
            whole((1, rows)),
            whole(rel_parts.shape),
            lanes(1, chunk),
            lanes(1, chunk),
            lanes(dim, chunk),
        ],
        out_specs=[whole((dim, rows)), whole((1, rows))],
        out_shape=[
            jax.ShapeDtypeStruct((dim, rows), f32),
            jax.ShapeDtypeStruct((1, rows), f32),
        ],
        scratch_shapes=[pltpu.VMEM((dim, rows), f32)],
        compiler_params=params(24),
        cost_estimate=cost(4 * dim * rows * edges, 4 * dim * edges),
    )(
        in_hbm(src_table),
        in_hbm(src_state),
        rel_parts,
        in_hbm(src_ids),
        in_hbm(rel_ids),
        in_hbm(query_grad),
    )


def destination_side(high, low_state, own_grad, grads):
    dim, rows = own_grad.shape
    count = len(grads)

    def body(*refs):
        high_ref, low_ref, own_ref = refs[:3]
        out, state_out = refs[3 + count :]
        total = own_ref[...]
        for ref in refs[3 : 3 + count]:
            total = total + ref[...].astype(f32)
        packed = low_ref[...].astype(f32)
        state = packed[dim : dim + 1] + packed[dim + 1 : dim + 2] + packed[dim + 2 : dim + 3]
        new_state = state + jnp.sum(total * total, axis=0, keepdims=True) / dim
        state_out[...] = new_state
        table = high_ref[...].astype(f32) + packed[:dim]
        out[...] = table - LEARN_RATE * total / jnp.sqrt(new_state)

    width = min(rows, 128)

    operands = [high, low_state, own_grad, *grads]
    return pl.pallas_call(
        body,
        name="destination_side",
        grid=(rows // width,),
        in_specs=[lanes(array.shape[0], width) for array in operands],
        out_specs=[lanes(dim, width), lanes(1, width)],
        out_shape=[
            jax.ShapeDtypeStruct((dim, rows), f32),
            jax.ShapeDtypeStruct((1, rows), f32),
        ],
        compiler_params=params(16),
        cost_estimate=cost(8 * dim * rows, (12 + 2 * count) * dim * rows),
    )(*operands)


def split_table(table, state):
    dim, rows = table.shape
    half = rows // 2
    tail = 16

    def body(table_ref, state_ref, left, right, rest):
        value = table_ref[...]
        high, low = split2(value)
        left[...] = high[:, :half]
        right[...] = high[:, half:]
        rest[:dim] = low
        first, _ = split2(state_ref[...])
        left_over = state_ref[...] - first.astype(f32)
        second, third = split2(left_over)
        parts = [first.astype(f32), second.astype(f32), third.astype(f32)]
        parts.append(jnp.zeros((tail - 3, rows), f32))
        rest[dim:] = jnp.concatenate(parts, axis=0).astype(bf16)

    return pl.pallas_call(
        body,
        name="split_table",
        grid=(1,),
        in_specs=[whole((dim, rows)), whole((1, rows))],
        out_specs=[whole((dim, half)), whole((dim, rows - half)), whole((dim + tail, rows))],
        out_shape=[
            jax.ShapeDtypeStruct((dim, half), bf16),
            jax.ShapeDtypeStruct((dim, rows - half), bf16),
            jax.ShapeDtypeStruct((dim + tail, rows), bf16),
        ],
        compiler_params=params(16),
        cost_estimate=cost(4 * dim * rows, 8 * dim * rows),
    )(in_hbm(table), in_hbm(state))


def grid_of(count):
    across = math.isqrt(count)
    while count % across:
        across -= 1
    return count // across, across


def moved(device, n, stride, shift):
    place = (device // stride) % n
    return device + ((place + shift) % n - place) * stride


def shifted(array, n, stride, shift):
    count = lax.axis_size("dom")
    return lax.ppermute(array, "dom", [(d, moved(d, n, stride, shift)) for d in range(count)])


def copy_chosen(index, options, out, columns):
    for k in range(len(options)):

        @pl.when(index == k)
        def _(k=k):
            out[:, columns] = options[k][...]


def route(values, matching, here):
    down, across = grid_of(lax.axis_size("dom"))
    axes = [(across, 1), (down, across)]
    orders = [axes, axes[::-1]][: len(values)]
    rows = values[0].shape[0]
    widths = [value.shape[1] for value in values]
    starts = [sum(widths[:i]) for i in range(len(widths))]
    vmem = pl.BlockSpec(memory_space=pltpu.VMEM)
    smem = pl.BlockSpec(memory_space=pltpu.SMEM)

    held = []
    for i, ((n1, stride1), _) in enumerate(orders):
        held.append([values[i]] + [shifted(values[i], n1, stride1, k) for k in range(1, n1)])
    flat = [array for group in held for array in group]

    def grouped(refs, groups):
        result, used = [], 0
        for group in groups:
            result.append(refs[used : used + len(group)])
            used += len(group)
        return result, refs[used:]

    def behind(place, source, n, stride):
        return ((place // stride) % n - (source // stride) % n + n) % n

    def pass_on(match_ref, here_ref, *refs):
        place = here_ref[0]
        held_refs, outs = grouped(refs, held)
        used = 0
        for i, ((n1, stride1), (n2, stride2)) in enumerate(orders):
            for m in range(1, n2):
                source = match_ref[moved(place, n2, stride2, m)]
                picked = behind(place, source, n1, stride1)
                copy_chosen(picked, held_refs[i], outs[used], slice(None))
                used += 1

    hops = [(i, m) for i in range(len(orders)) for m in range(1, orders[i][1][0])]
    passed = pl.pallas_call(
        pass_on,
        in_specs=[smem, smem] + [vmem] * len(flat),
        out_specs=[vmem] * len(hops),
        out_shape=[jax.ShapeDtypeStruct((rows, widths[i]), bf16) for i, _ in hops],
        compiler_params=pltpu.CompilerParams(vmem_limit_bytes=16 * MIB),
        cost_estimate=cost(0, 4 * rows * sum(widths)),
    )(matching, here, *flat)
    found = [[] for _ in orders]
    for (i, m), array in zip(hops, passed):
        found[i].append(shifted(array, *orders[i][1], m))
    flat_found = [array for group in found for array in group]

    def merge(match_ref, here_ref, *refs):
        place = here_ref[0]
        held_refs, rest = grouped(refs, held)
        found_refs, (out,) = grouped(rest, found)
        source = match_ref[place]
        for i, ((n1, stride1), (n2, stride2)) in enumerate(orders):
            columns = slice(starts[i], starts[i] + widths[i])
            near = behind(place, source, n1, stride1)
            far = behind(place, source, n2, stride2)
            index = jnp.where(far == 0, near, n1 - 1 + far)
            copy_chosen(index, list(held_refs[i]) + list(found_refs[i]), out, columns)

    return pl.pallas_call(
        merge,
        in_specs=[smem, smem] + [vmem] * (len(flat) + len(flat_found)),
        out_specs=vmem,
        out_shape=jax.ShapeDtypeStruct((rows, sum(widths)), bf16),
        compiler_params=pltpu.CompilerParams(vmem_limit_bytes=24 * MIB),
        cost_estimate=cost(0, 4 * rows * sum(widths)),
    )(matching, here, *flat, *flat_found)


def total_of_peers(value, axis, stride, n):
    count = lax.axis_size(axis)

    def peer(i, k):
        digit = (i // stride) % n
        return i + ((digit ^ k) - digit) * stride

    terms = [value]
    for k in range(1, n):
        terms.append(lax.ppermute(value, axis, [(i, peer(i, k)) for i in range(count)]))
    while len(terms) > 1:
        terms = [terms[i] + terms[i + 1] for i in range(0, len(terms), 2)]
    return terms[0]


def total_over_mesh(value):
    down, across = grid_of(lax.axis_size("dom"))
    value = total_of_peers(value, "edge", 1, CORES)
    value = total_of_peers(value, "edge", CORES, lax.axis_size("edge") // CORES)
    if down * across <= 4:
        return total_of_peers(value, "dom", 1, down * across)
    value = total_of_peers(value, "dom", 1, across)
    return total_of_peers(value, "dom", across, down)


def shards(
    src_table,
    src_state,
    dst_table,
    dst_state,
    relation,
    edge_src,
    edge_dst,
    edge_rel,
    matching,
    neg_rows,
    quotas,
):
    edge_count = lax.axis_size("edge")
    chips = edge_count // CORES
    _, row_count = src_table.shape
    rel_count = relation.shape[1]
    edges = edge_src.shape[0]
    chunk = min(edges, 1024)
    wave_chunk = min(edges, 2048)
    here = lax.axis_index("edge").reshape(1).astype(jnp.int32)
    place = lax.axis_index("dom").reshape(1).astype(jnp.int32)

    src_ids = edge_src.reshape(1, edges)
    dst_ids = edge_dst.reshape(1, edges)
    rel_ids = edge_rel.reshape(1, edges)
    neg_ids = neg_rows.reshape(edge_count, QMAX, BLOCK)
    rel_parts = split_relation(relation)

    left, right, rest = split_table(dst_table, dst_state.reshape(1, row_count))
    part_high = route([left, right], matching, place)
    rest, part_high = lax.optimization_barrier((rest, part_high))
    low_state = route([rest], matching, place)

    made = []
    for part in range(2):
        made = make_queries(
            src_table, rel_parts, src_ids, rel_ids, rel_count, min(chunk, edges // 2), part, 2, made
        )
    query, query_b, src_rows = made
    pos_coef, own_grad = positives(part_high, query, dst_ids, chunk)

    swap = [(i, i ^ 1) for i in range(edge_count)]

    def swapped(array):
        return lax.ppermute(array, "edge", swap)

    chip = here // CORES
    lane = here % CORES
    arrived, negatives, coefs = [], [], []
    done, brought = [own_grad], {}
    for k in range(chips):
        pairs = [(i, i ^ (CORES * k)) for i in range(edge_count)]
        near = k & -k
        table = brought.get(k - near, part_high)
        if k:
            if k == near >= 2:
                table, _ = lax.optimization_barrier((table, done[k // 2 - 1]))
            hop = [(i, i ^ (CORES * near)) for i in range(edge_count)]
            table = lax.ppermute(table, "edge", hop)
        brought[k] = table
        live, coef, mine, theirs = negative_wave(
            [table, swapped(table)], chip ^ k, quotas, neg_ids, query_b, lane, wave_chunk
        )
        total = mine.astype(f32) + swapped(theirs).astype(f32)
        if k:
            total = lax.ppermute(total.astype(bf16), "edge", pairs)
        arrived.append(total)
        done.append(mine)
        negatives.append(live)
        coefs.append(coef)

    query_grad, rel_grad = combine(
        src_rows,
        rel_ids,
        part_high,
        dst_ids,
        pos_coef,
        negatives,
        coefs,
        rel_count,
        chunk,
    )
    src_out, src_state_out = source_side(
        src_table,
        src_state.reshape(1, row_count),
        rel_parts,
        src_ids,
        rel_ids,
        query_grad,
        rel_count,
        chunk,
    )
    relation_out = relation - REL_RATE * total_over_mesh(rel_grad).T
    dst_out, dst_state_out = destination_side(part_high, low_state, own_grad, arrived)
    return (
        src_out,
        src_state_out.reshape(row_count),
        dst_out,
        dst_state_out.reshape(row_count),
        relation_out,
    )


def solution(mesh):
    in_specs = (
        P(None, ("dom", "edge")),
        P(("dom", "edge")),
        P(None, ("dom", "edge")),
        P(("dom", "edge")),
        P(),
        P(("dom", "edge")),
        P(("dom", "edge")),
        P(("dom", "edge")),
        P(),
        P(("dom", "edge"), None, None),
        P(("dom", "edge"), None),
    )
    out_specs = (
        P(None, ("dom", "edge")),
        P(("dom", "edge")),
        P(None, ("dom", "edge")),
        P(("dom", "edge")),
        P(),
    )

    return jax.shard_map(shards, mesh=mesh, in_specs=in_specs, out_specs=out_specs, check_vma=False)
```

```python
import math

import jax
import jax.numpy as jnp
from jax import lax
from jax.experimental import pallas as pl
from jax.experimental.pallas import tpu as pltpu
from jax.sharding import PartitionSpec as P

BLOCK = 128
QMAX = 2
QTOTAL = 12
NNEG = QTOTAL * BLOCK
CORES = 2
LEARN_RATE = 0.1
REL_RATE = 0.02
SUB = 1024


bf16 = jnp.bfloat16
f32 = jnp.float32
MIB = 2**20


def dot_nn(lhs, rhs):
    return lax.dot_general(lhs, rhs, (((1,), (0,)), ((), ())), preferred_element_type=f32)


def dot_nt(lhs, rhs):
    return lax.dot_general(lhs, rhs, (((1,), (1,)), ((), ())), preferred_element_type=f32)


def split2(value):
    high = value.astype(bf16)
    return high, (value - high.astype(f32)).astype(bf16)


def select_rows(ids, rows):
    places = lax.broadcasted_iota(jnp.int32, (rows, ids.shape[1]), 0)
    return jnp.where(places == ids, 1.0, 0.0).astype(bf16)


def product(one, other):
    half = one.shape[0] // 2
    a, b, c, d = one[:half], one[half:], other[:half], other[half:]
    return jnp.concatenate([a * c - b * d, a * d + b * c], axis=0)


def back(grad, value):
    half = grad.shape[0] // 2
    a, b, c, d = grad[:half], grad[half:], value[:half], value[half:]
    return jnp.concatenate([a * c + b * d, b * c - a * d], axis=0)


def whole(shape):
    return pl.BlockSpec(shape, lambda *_: (0,) * len(shape))


def lanes(rows, width):
    return pl.BlockSpec((rows, width), lambda i, *_: (0, i))


def params(mib):
    return pltpu.CompilerParams(
        vmem_limit_bytes=mib * MIB, dimension_semantics=("arbitrary",)
    )


def in_hbm(array):
    return pltpu.with_memory_space_constraint(array, pltpu.HBM)


def cost(flops, moved):
    return pl.CostEstimate(flops=int(flops), bytes_accessed=int(moved), transcendentals=0)


def split_relation(relation):
    high = lax.reduce_precision(relation, 8, 7)
    rest = relation - high
    mid = lax.reduce_precision(rest, 8, 7)
    low = rest - mid
    parts = jnp.concatenate([high, mid, low], axis=1).astype(bf16)
    return jnp.pad(parts, ((0, 0), (0, (-parts.shape[1]) % 128)))


def relation_rows(rel_parts, ids, count):
    width = rel_parts.shape[1]
    places = lax.broadcasted_iota(jnp.int32, (width, ids.shape[1]), 0)
    hit = jnp.logical_and(places % count == ids, places < 3 * count)
    return dot_nn(rel_parts, jnp.where(hit, 1.0, 0.0).astype(bf16))


def make_queries(src_table, rel_parts, src_ids, rel_ids, rel_count, chunk, part, parts, before):
    dim, rows = src_table.shape
    edges = src_ids.shape[1]
    steps = edges // chunk // parts
    dtypes = (f32, bf16, f32)

    def body(table, parts_ref, src, rel, *refs):
        query, query_b, rows_out, high, low = refs[len(before) :]

        @pl.when(pl.program_id(0) == 0)
        def _():
            high[...], low[...] = split2(table[...])

        pick = select_rows(src[...], rows)
        src_rows = dot_nn(high[...], pick) + dot_nn(low[...], pick)
        rows_out[...] = src_rows
        value = product(src_rows, relation_rows(parts_ref[...], rel[...], rel_count))
        query[...] = value
        query_b[...] = value.astype(bf16)

    def columns(height):
        return pl.BlockSpec((height, chunk), lambda i: (0, i + part * steps))

    return pl.pallas_call(
        body,
        name="make_queries",
        grid=(steps,),
        in_specs=[whole((dim, rows)), whole(rel_parts.shape), columns(1), columns(1)]
        + [pl.BlockSpec(memory_space=pl.ANY)] * len(before),
        out_specs=[columns(dim)] * 3,
        out_shape=[pltpu.HBM((dim, edges), dtype) for dtype in dtypes],
        input_output_aliases={4 + i: i for i in range(len(before))},
        scratch_shapes=[pltpu.VMEM((dim, rows), bf16)] * 2,
        compiler_params=params(32),
        cost_estimate=cost(4 * dim * rows * edges // parts, 10 * dim * edges // parts),
    )(in_hbm(src_table), rel_parts, in_hbm(src_ids), in_hbm(rel_ids), *map(in_hbm, before))


def positives(part_high, query, dst_ids, chunk):
    dim, rows = part_high.shape
    edges = dst_ids.shape[1]

    def body(table, query_in, dst, coefs, dst_grad):
        @pl.when(pl.program_id(0) == 0)
        def _():
            dst_grad[...] = jnp.zeros_like(dst_grad)

        pick = select_rows(dst[...], rows)
        dst_rows = dot_nn(table[...], pick)
        value = query_in[...]
        positive = jnp.sum(value * dst_rows, axis=0, keepdims=True)
        coef = -jax.nn.sigmoid(-positive)
        coefs[...] = coef
        dst_grad[...] += dot_nt((coef * value).astype(bf16), pick)

    return pl.pallas_call(
        body,
        name="positives",
        grid=(edges // chunk,),
        in_specs=[whole((dim, rows)), lanes(dim, chunk), lanes(1, chunk)],
        out_specs=[lanes(1, chunk), whole((dim, rows))],
        out_shape=[pltpu.HBM((1, edges), f32), jax.ShapeDtypeStruct((dim, rows), f32)],
        compiler_params=params(32),
        cost_estimate=cost(6 * dim * rows * edges, 8 * dim * edges),
    )(part_high, in_hbm(query), in_hbm(dst_ids))


def negative_wave(tables, chip, quota, neg_ids, query_b, lane, chunk):
    count = len(tables)
    dim, rows = tables[0].shape
    edges = query_b.shape[1]
    slots = QMAX * count
    half_weight = 0.5 / math.sqrt(NNEG)

    def body(chip_ref, lane_ref, quota_ref, *refs):
        table_refs = refs[:count]
        ids, query_ref, neg, coef_out = refs[count : count + 4]
        grad_refs = refs[count + 4 : 2 * count + 4]
        neg_t, neg_grad = refs[2 * count + 4 :]

        live, at, base = [], [], [jnp.int32(0)]
        for s in range(count):
            spot = CORES * chip_ref[0] + (lane_ref[0] + s) % CORES
            at.append(spot)
            live.append(quota_ref[0, spot])
            base.append(base[-1] + live[-1])
        total = base[-1]

        step = pl.program_id(0)

        def picks(s, wide):
            parts = [select_rows(ids[at[s], b : b + 1, :], rows) for b in range(wide)]
            return jnp.concatenate(parts, axis=1) if wide > 1 else parts[0]

        def when_live(s, wide):
            return pl.when(jnp.logical_and(live[s] == wide, step == 0))

        def when_done(s, wide):
            return pl.when(jnp.logical_and(live[s] == wide, step == pl.num_programs(0) - 1))

        for s in range(count):
            for wide in range(1, QMAX + 1):

                @when_live(s, wide)
                def _(s=s, wide=wide):
                    value = dot_nn(table_refs[s][...], picks(s, wide))
                    for b in range(wide):
                        part = value[:, b * BLOCK : (b + 1) * BLOCK]
                        neg[base[s] + b] = part.astype(bf16)
                        neg_t[base[s] + b] = part.T.astype(bf16)
                        neg_grad[base[s] + b] = jnp.zeros((dim, BLOCK), f32)

        @pl.when(jnp.logical_and(total % 2 == 1, step == 0))
        def _():
            neg[total] = jnp.zeros((dim, BLOCK), bf16)
            neg_t[total] = jnp.zeros((BLOCK, dim), bf16)
            neg_grad[total] = jnp.zeros((dim, BLOCK), f32)

        for pairs in range(1, slots // 2 + 1):

            @pl.when((total + 1) // 2 == pairs)
            def _(blocks=2 * pairs):
                query = query_ref[...]
                rows_t = jnp.concatenate([neg_t[j] for j in range(blocks)], axis=0)
                scores = dot_nn(rows_t, query)
                coef = (half_weight * jnp.tanh(0.5 * scores) + half_weight).astype(bf16)
                coef_out[: blocks * BLOCK] = coef
                added = dot_nt(query, coef)
                for j in range(blocks):
                    neg_grad[j] += added[:, j * BLOCK : (j + 1) * BLOCK]

        for p in range(slots // 2):

            @pl.when(p >= (total + 1) // 2)
            def _(p=p):
                coef_out[2 * p * BLOCK : 2 * (p + 1) * BLOCK] = jnp.zeros((2 * BLOCK, chunk), bf16)
                neg[2 * p] = jnp.zeros((dim, BLOCK), bf16)
                neg[2 * p + 1] = jnp.zeros((dim, BLOCK), bf16)

        for s in range(count):

            @when_done(s, 0)
            def _(s=s):
                grad_refs[s][...] = jnp.zeros((dim, rows), bf16)

            for wide in range(1, QMAX + 1):

                @when_done(s, wide)
                def _(s=s, wide=wide):
                    parts = [neg_grad[base[s] + b] for b in range(wide)]
                    value = jnp.concatenate(parts, axis=1) if wide > 1 else parts[0]
                    grad_refs[s][...] = dot_nt(value.astype(bf16), picks(s, wide)).astype(bf16)

    smem = pl.BlockSpec(memory_space=pltpu.SMEM)
    shard = jax.ShapeDtypeStruct((dim, rows), bf16)
    return pl.pallas_call(
        body,
        grid=(edges // chunk,),
        in_specs=[smem, smem, smem]
        + [whole((dim, rows))] * count
        + [whole(neg_ids.shape), lanes(dim, chunk)],
        out_specs=[whole((slots, dim, BLOCK)), lanes(slots * BLOCK, chunk)]
        + [whole((dim, rows))] * count,
        scratch_shapes=[
            pltpu.VMEM((slots, BLOCK, dim), bf16),
            pltpu.VMEM((slots, dim, BLOCK), f32),
        ],
        out_shape=[
            jax.ShapeDtypeStruct((slots, dim, BLOCK), bf16),
            pltpu.HBM((slots * BLOCK, edges), bf16),
        ]
        + [shard] * count,
        compiler_params=params(32),
        cost_estimate=cost(6 * dim * 1.5 * count * BLOCK * edges, 10 * dim * edges),
    )(chip, lane, quota, *tables, neg_ids, in_hbm(query_b))


def combine(
    src_rows, rel_ids, part_high, dst_ids, pos_coef, negatives, coefs, rel_count, chunk
):
    dim, edges = src_rows.shape
    rows = part_high.shape[1]
    count = len(negatives)
    slots = negatives[0].shape[0]
    sub = min(SUB, chunk)

    def body(rows_in, rel, table, dst, pos, *refs):
        neg_refs, coef_refs = refs[:count], refs[count : 2 * count]
        grad_out, rel_out, all_neg = refs[2 * count :]

        @pl.when(pl.program_id(0) == 0)
        def _():
            rel_out[...] = jnp.zeros_like(rel_out)
            for k in range(count):
                for j in range(slots):
                    all_neg[k, :, j * BLOCK : (j + 1) * BLOCK] = neg_refs[k][j]

        found = None
        for h in range(chunk // sub):
            part = slice(h * sub, (h + 1) * sub)
            grad = pos[:, part] * dot_nn(table[...], select_rows(dst[:, part], rows))
            for k in range(count):
                grad = grad + dot_nn(all_neg[k], coef_refs[k][:, part])
            grad_out[:, part] = grad
            kinds = select_rows(rel[:, part], rel_count)
            upper, lower = split2(back(grad, rows_in[:, part]))
            more = dot_nt(kinds, upper) + dot_nt(kinds, lower)
            found = more if found is None else found + more
        rel_out[...] += found

    return pl.pallas_call(
        body,
        name="combine",
        grid=(edges // chunk,),
        in_specs=[lanes(dim, chunk), lanes(1, chunk)]
        + [whole((dim, rows)), lanes(1, chunk), lanes(1, chunk)]
        + [whole(negatives[0].shape)] * count
        + [lanes(slots * BLOCK, chunk)] * count,
        out_specs=[lanes(dim, chunk), whole((rel_count, dim))],
        out_shape=[
            pltpu.HBM((dim, edges), f32),
            jax.ShapeDtypeStruct((rel_count, dim), f32),
        ],
        scratch_shapes=[pltpu.VMEM((count, dim, slots * BLOCK), bf16)],
        compiler_params=params(48),
        cost_estimate=cost(2 * dim * NNEG * edges, 12 * dim * edges + 2 * NNEG * edges),
    )(
        in_hbm(src_rows),
        in_hbm(rel_ids),
        part_high,
        in_hbm(dst_ids),
        in_hbm(pos_coef),
        *negatives,
        *map(in_hbm, coefs),
    )


def source_side(src_table, src_state, rel_parts, src_ids, rel_ids, query_grad, rel_count, chunk):
    dim, rows = src_table.shape
    edges = src_ids.shape[1]
    sub = min(SUB, chunk)

    def body(table, state, parts, src, rel, grad_in, out, state_out, acc):
        step = pl.program_id(0)

        @pl.when(step == 0)
        def _():
            acc[...] = jnp.zeros_like(acc)

        found = None
        for h in range(chunk // sub):
            part = slice(h * sub, (h + 1) * sub)
            pick = select_rows(src[:, part], rows)
            rel_rows = relation_rows(parts[...], rel[:, part], rel_count)
            term = back(grad_in[:, part], rel_rows).astype(bf16)
            more = dot_nt(term, pick)
            found = more if found is None else found + more
        acc[...] += found

        @pl.when(step == pl.num_programs(0) - 1)
        def _():
            total = acc[...]
            new_state = state[...] + jnp.sum(total * total, axis=0, keepdims=True) / dim
            state_out[...] = new_state
            out[...] = table[...] - LEARN_RATE * total / jnp.sqrt(new_state)

    return pl.pallas_call(
        body,
        name="source_side",
        grid=(edges // chunk,),
        in_specs=[
            whole((dim, rows)),
            whole((1, rows)),
            whole(rel_parts.shape),
            lanes(1, chunk),
            lanes(1, chunk),
            lanes(dim, chunk),
        ],
        out_specs=[whole((dim, rows)), whole((1, rows))],
        out_shape=[
            jax.ShapeDtypeStruct((dim, rows), f32),
            jax.ShapeDtypeStruct((1, rows), f32),
        ],
        scratch_shapes=[pltpu.VMEM((dim, rows), f32)],
        compiler_params=params(24),
        cost_estimate=cost(4 * dim * rows * edges, 4 * dim * edges),
    )(
        in_hbm(src_table),
        in_hbm(src_state),
        rel_parts,
        in_hbm(src_ids),
        in_hbm(rel_ids),
        in_hbm(query_grad),
    )


def destination_side(high, low_options, low_order, matching, place, own_grad, grads):
    dim, rows = own_grad.shape
    count = len(grads)
    options = len(low_options)
    (n1, stride1), (n2, stride2) = low_order

    def body(match_ref, here_ref, *refs):
        high_ref, own_ref = refs[:2]
        low_refs = refs[2 : 2 + options]
        out, state_out, low_ref = refs[2 + options + count :]
        source = match_ref[here_ref[0]]
        near = behind(here_ref[0], source, n1, stride1)
        far = behind(here_ref[0], source, n2, stride2)
        index = jnp.where(far == 0, near, n1 - 1 + far)
        copy_chosen(index, low_refs, low_ref, slice(None))
        total = own_ref[...]
        for ref in refs[2 + options : 2 + options + count]:
            total = total + ref[...].astype(f32)
        packed = low_ref[...].astype(f32)
        state = packed[dim : dim + 1] + packed[dim + 1 : dim + 2] + packed[dim + 2 : dim + 3]
        new_state = state + jnp.sum(total * total, axis=0, keepdims=True) / dim
        state_out[...] = new_state
        table = high_ref[...].astype(f32) + packed[:dim]
        out[...] = table - LEARN_RATE * total / jnp.sqrt(new_state)

    width = min(rows, 128)

    operands = [high, own_grad, *low_options, *grads]
    smem = pl.BlockSpec(memory_space=pltpu.SMEM)
    return pl.pallas_call(
        body,
        name="destination_side",
        grid=(rows // width,),
        in_specs=[smem, smem] + [lanes(array.shape[0], width) for array in operands],
        out_specs=[lanes(dim, width), lanes(1, width)],
        scratch_shapes=[pltpu.VMEM((low_options[0].shape[0], width), bf16)],
        out_shape=[
            jax.ShapeDtypeStruct((dim, rows), f32),
            jax.ShapeDtypeStruct((1, rows), f32),
        ],
        compiler_params=params(16),
        cost_estimate=cost(8 * dim * rows, (12 + 2 * count) * dim * rows),
    )(matching, place, *operands)


def split_table(table, state):
    dim, rows = table.shape
    half = rows // 2
    tail = 16

    def body(table_ref, state_ref, left, right, rest):
        value = table_ref[...]
        high, low = split2(value)
        left[...] = high[:, :half]
        right[...] = high[:, half:]
        rest[:dim] = low
        first, _ = split2(state_ref[...])
        left_over = state_ref[...] - first.astype(f32)
        second, third = split2(left_over)
        parts = [first.astype(f32), second.astype(f32), third.astype(f32)]
        parts.append(jnp.zeros((tail - 3, rows), f32))
        rest[dim:] = jnp.concatenate(parts, axis=0).astype(bf16)

    return pl.pallas_call(
        body,
        name="split_table",
        grid=(1,),
        in_specs=[whole((dim, rows)), whole((1, rows))],
        out_specs=[whole((dim, half)), whole((dim, rows - half)), whole((dim + tail, rows))],
        out_shape=[
            jax.ShapeDtypeStruct((dim, half), bf16),
            jax.ShapeDtypeStruct((dim, rows - half), bf16),
            jax.ShapeDtypeStruct((dim + tail, rows), bf16),
        ],
        compiler_params=params(16),
        cost_estimate=cost(4 * dim * rows, 8 * dim * rows),
    )(in_hbm(table), in_hbm(state))


def grid_of(count):
    across = math.isqrt(count)
    while count % across:
        across -= 1
    return count // across, across


def moved(device, n, stride, shift):
    place = (device // stride) % n
    return device + ((place + shift) % n - place) * stride


def shifted(array, n, stride, shift):
    count = lax.axis_size("dom")
    return lax.ppermute(array, "dom", [(d, moved(d, n, stride, shift)) for d in range(count)])


def behind(place, source, n, stride):
    return ((place // stride) % n - (source // stride) % n + n) % n


def copy_chosen(index, options, out, columns):
    for k in range(len(options)):

        @pl.when(index == k)
        def _(k=k):
            out[:, columns] = options[k][...]


def route(values, matching, here, join=True):
    down, across = grid_of(lax.axis_size("dom"))
    axes = [(across, 1), (down, across)]
    orders = [axes, axes[::-1]][: len(values)]
    rows = values[0].shape[0]
    widths = [value.shape[1] for value in values]
    starts = [sum(widths[:i]) for i in range(len(widths))]
    vmem = pl.BlockSpec(memory_space=pltpu.VMEM)
    smem = pl.BlockSpec(memory_space=pltpu.SMEM)

    held = []
    for i, ((n1, stride1), _) in enumerate(orders):
        held.append([values[i]] + [shifted(values[i], n1, stride1, k) for k in range(1, n1)])
    flat = [array for group in held for array in group]

    def grouped(refs, groups):
        result, used = [], 0
        for group in groups:
            result.append(refs[used : used + len(group)])
            used += len(group)
        return result, refs[used:]

    def pass_on(match_ref, here_ref, *refs):
        place = here_ref[0]
        held_refs, outs = grouped(refs, held)
        used = 0
        for i, ((n1, stride1), (n2, stride2)) in enumerate(orders):
            for m in range(1, n2):
                source = match_ref[moved(place, n2, stride2, m)]
                picked = behind(place, source, n1, stride1)
                copy_chosen(picked, held_refs[i], outs[used], slice(None))
                used += 1

    hops = [(i, m) for i in range(len(orders)) for m in range(1, orders[i][1][0])]
    passed = pl.pallas_call(
        pass_on,
        in_specs=[smem, smem] + [vmem] * len(flat),
        out_specs=[vmem] * len(hops),
        out_shape=[jax.ShapeDtypeStruct((rows, widths[i]), bf16) for i, _ in hops],
        compiler_params=pltpu.CompilerParams(vmem_limit_bytes=16 * MIB),
        cost_estimate=cost(0, 4 * rows * sum(widths)),
    )(matching, here, *flat)
    found = [[] for _ in orders]
    for (i, m), array in zip(hops, passed):
        found[i].append(shifted(array, *orders[i][1], m))
    flat_found = [array for group in found for array in group]

    if not join:
        return [*held[0], *found[0]], orders[0]

    def merge(match_ref, here_ref, *refs):
        place = here_ref[0]
        held_refs, rest = grouped(refs, held)
        found_refs, (out,) = grouped(rest, found)
        source = match_ref[place]
        for i, ((n1, stride1), (n2, stride2)) in enumerate(orders):
            columns = slice(starts[i], starts[i] + widths[i])
            near = behind(place, source, n1, stride1)
            far = behind(place, source, n2, stride2)
            index = jnp.where(far == 0, near, n1 - 1 + far)
            copy_chosen(index, list(held_refs[i]) + list(found_refs[i]), out, columns)

    return pl.pallas_call(
        merge,
        in_specs=[smem, smem] + [vmem] * (len(flat) + len(flat_found)),
        out_specs=vmem,
        out_shape=jax.ShapeDtypeStruct((rows, sum(widths)), bf16),
        compiler_params=pltpu.CompilerParams(vmem_limit_bytes=24 * MIB),
        cost_estimate=cost(0, 4 * rows * sum(widths)),
    )(matching, here, *flat, *flat_found)


def total_of_peers(value, axis, stride, n):
    count = lax.axis_size(axis)

    def peer(i, k):
        digit = (i // stride) % n
        return i + ((digit ^ k) - digit) * stride

    terms = [value]
    for k in range(1, n):
        terms.append(lax.ppermute(value, axis, [(i, peer(i, k)) for i in range(count)]))
    while len(terms) > 1:
        terms = [terms[i] + terms[i + 1] for i in range(0, len(terms), 2)]
    return terms[0]


def total_over_mesh(value):
    down, across = grid_of(lax.axis_size("dom"))
    value = total_of_peers(value, "edge", 1, CORES)
    value = total_of_peers(value, "edge", CORES, lax.axis_size("edge") // CORES)
    if down * across <= 4:
        return total_of_peers(value, "dom", 1, down * across)
    value = total_of_peers(value, "dom", 1, across)
    return total_of_peers(value, "dom", across, down)


def shards(
    src_table,
    src_state,
    dst_table,
    dst_state,
    relation,
    edge_src,
    edge_dst,
    edge_rel,
    matching,
    neg_rows,
    quotas,
):
    edge_count = lax.axis_size("edge")
    chips = edge_count // CORES
    _, row_count = src_table.shape
    rel_count = relation.shape[1]
    edges = edge_src.shape[0]
    chunk = min(edges, 1024)
    wave_chunk = min(edges, 2048)
    here = lax.axis_index("edge").reshape(1).astype(jnp.int32)
    place = lax.axis_index("dom").reshape(1).astype(jnp.int32)

    src_ids = edge_src.reshape(1, edges)
    dst_ids = edge_dst.reshape(1, edges)
    rel_ids = edge_rel.reshape(1, edges)
    neg_ids = neg_rows.reshape(edge_count, QMAX, BLOCK)
    rel_parts = split_relation(relation)

    left, right, rest = split_table(dst_table, dst_state.reshape(1, row_count))
    part_high = route([left, right], matching, place)
    rest, part_high = lax.optimization_barrier((rest, part_high))
    low_options, low_order = route([rest], matching, place, join=False)

    made = []
    for part in range(2):
        made = make_queries(
            src_table, rel_parts, src_ids, rel_ids, rel_count, min(chunk, edges // 2), part, 2, made
        )
    query, query_b, src_rows = made
    pos_coef, own_grad = positives(part_high, query, dst_ids, chunk)

    swap = [(i, i ^ 1) for i in range(edge_count)]

    def swapped(array):
        return lax.ppermute(array, "edge", swap)

    chip = here // CORES
    lane = here % CORES
    arrived, negatives, coefs = [], [], []
    done, brought = [own_grad], {}
    for k in range(chips):
        pairs = [(i, i ^ (CORES * k)) for i in range(edge_count)]
        near = k & -k
        table = brought.get(k - near, part_high)
        if k:
            if k == near >= 2:
                table, _ = lax.optimization_barrier((table, done[k // 2 - 1]))
            hop = [(i, i ^ (CORES * near)) for i in range(edge_count)]
            table = lax.ppermute(table, "edge", hop)
        brought[k] = table
        live, coef, mine, theirs = negative_wave(
            [table, swapped(table)], chip ^ k, quotas, neg_ids, query_b, lane, wave_chunk
        )
        total = mine.astype(f32) + swapped(theirs).astype(f32)
        if k:
            total = lax.ppermute(total.astype(bf16), "edge", pairs)
        arrived.append(total)
        done.append(mine)
        negatives.append(live)
        coefs.append(coef)

    query_grad, rel_grad = combine(
        src_rows,
        rel_ids,
        part_high,
        dst_ids,
        pos_coef,
        negatives,
        coefs,
        rel_count,
        chunk,
    )
    src_out, src_state_out = source_side(
        src_table,
        src_state.reshape(1, row_count),
        rel_parts,
        src_ids,
        rel_ids,
        query_grad,
        rel_count,
        chunk,
    )
    relation_out = relation - REL_RATE * total_over_mesh(rel_grad).T
    dst_out, dst_state_out = destination_side(
        part_high, low_options, low_order, matching, place, own_grad, arrived
    )
    return (
        src_out,
        src_state_out.reshape(row_count),
        dst_out,
        dst_state_out.reshape(row_count),
        relation_out,
    )


def solution(mesh):
    in_specs = (
        P(None, ("dom", "edge")),
        P(("dom", "edge")),
        P(None, ("dom", "edge")),
        P(("dom", "edge")),
        P(),
        P(("dom", "edge")),
        P(("dom", "edge")),
        P(("dom", "edge")),
        P(),
        P(("dom", "edge"), None, None),
        P(("dom", "edge"), None),
    )
    out_specs = (
        P(None, ("dom", "edge")),
        P(("dom", "edge")),
        P(None, ("dom", "edge")),
        P(("dom", "edge")),
        P(),
    )

    return jax.shard_map(shards, mesh=mesh, in_specs=in_specs, out_specs=out_specs, check_vma=False)
```

```python
import math

import jax
import jax.numpy as jnp
from jax import lax
from jax.experimental import pallas as pl
from jax.experimental.pallas import tpu as pltpu
from jax.sharding import PartitionSpec as P

BLOCK = 128
QMAX = 2
QTOTAL = 12
NNEG = QTOTAL * BLOCK
CORES = 2
LEARN_RATE = 0.1
REL_RATE = 0.02
SUB = 1024


bf16 = jnp.bfloat16
f32 = jnp.float32
MIB = 2**20


def dot_nn(lhs, rhs):
    return lax.dot_general(lhs, rhs, (((1,), (0,)), ((), ())), preferred_element_type=f32)


def dot_nt(lhs, rhs):
    return lax.dot_general(lhs, rhs, (((1,), (1,)), ((), ())), preferred_element_type=f32)


def split2(value):
    high = value.astype(bf16)
    return high, (value - high.astype(f32)).astype(bf16)


def select_rows(ids, rows):
    places = lax.broadcasted_iota(jnp.int32, (rows, ids.shape[1]), 0)
    return jnp.where(places == ids, 1.0, 0.0).astype(bf16)


def product(one, other):
    half = one.shape[0] // 2
    a, b, c, d = one[:half], one[half:], other[:half], other[half:]
    return jnp.concatenate([a * c - b * d, a * d + b * c], axis=0)


def back(grad, value):
    half = grad.shape[0] // 2
    a, b, c, d = grad[:half], grad[half:], value[:half], value[half:]
    return jnp.concatenate([a * c + b * d, b * c - a * d], axis=0)


def whole(shape):
    return pl.BlockSpec(shape, lambda *_: (0,) * len(shape))


def lanes(rows, width):
    return pl.BlockSpec((rows, width), lambda i, *_: (0, i))


def params(mib):
    return pltpu.CompilerParams(
        vmem_limit_bytes=mib * MIB, dimension_semantics=("arbitrary",)
    )


def in_hbm(array):
    return pltpu.with_memory_space_constraint(array, pltpu.HBM)


def cost(flops, moved):
    return pl.CostEstimate(flops=int(flops), bytes_accessed=int(moved), transcendentals=0)


def split_relation(relation):
    high = lax.reduce_precision(relation, 8, 7)
    rest = relation - high
    mid = lax.reduce_precision(rest, 8, 7)
    low = rest - mid
    parts = jnp.concatenate([high, mid, low], axis=1).astype(bf16)
    return jnp.pad(parts, ((0, 0), (0, (-parts.shape[1]) % 128)))


def relation_rows(rel_parts, ids, count):
    width = rel_parts.shape[1]
    places = lax.broadcasted_iota(jnp.int32, (width, ids.shape[1]), 0)
    hit = jnp.logical_and(places % count == ids, places < 3 * count)
    return dot_nn(rel_parts, jnp.where(hit, 1.0, 0.0).astype(bf16))


def make_queries(src_table, rel_parts, src_ids, rel_ids, rel_count, chunk, part, parts, before):
    dim, rows = src_table.shape
    edges = src_ids.shape[1]
    steps = edges // chunk // parts
    dtypes = (f32, bf16, f32)

    def body(table, parts_ref, src, rel, *refs):
        query, query_b, rows_out, high, low = refs[len(before) :]

        @pl.when(pl.program_id(0) == 0)
        def _():
            high[...], low[...] = split2(table[...])

        pick = select_rows(src[...], rows)
        src_rows = dot_nn(high[...], pick) + dot_nn(low[...], pick)
        rows_out[...] = src_rows
        value = product(src_rows, relation_rows(parts_ref[...], rel[...], rel_count))
        query[...] = value
        query_b[...] = value.astype(bf16)

    def columns(height):
        return pl.BlockSpec((height, chunk), lambda i: (0, i + part * steps))

    return pl.pallas_call(
        body,
        name="make_queries",
        grid=(steps,),
        in_specs=[whole((dim, rows)), whole(rel_parts.shape), columns(1), columns(1)]
        + [pl.BlockSpec(memory_space=pl.ANY)] * len(before),
        out_specs=[columns(dim)] * 3,
        out_shape=[pltpu.HBM((dim, edges), dtype) for dtype in dtypes],
        input_output_aliases={4 + i: i for i in range(len(before))},
        scratch_shapes=[pltpu.VMEM((dim, rows), bf16)] * 2,
        compiler_params=params(32),
        cost_estimate=cost(4 * dim * rows * edges // parts, 10 * dim * edges // parts),
    )(in_hbm(src_table), rel_parts, in_hbm(src_ids), in_hbm(rel_ids), *map(in_hbm, before))


def positives(part_high, query, dst_ids, chunk):
    dim, rows = part_high.shape
    edges = dst_ids.shape[1]

    def body(table, query_in, dst, coefs, dst_grad):
        @pl.when(pl.program_id(0) == 0)
        def _():
            dst_grad[...] = jnp.zeros_like(dst_grad)

        pick = select_rows(dst[...], rows)
        dst_rows = dot_nn(table[...], pick)
        value = query_in[...]
        positive = jnp.sum(value * dst_rows, axis=0, keepdims=True)
        coef = -jax.nn.sigmoid(-positive)
        coefs[...] = coef
        dst_grad[...] += dot_nt((coef * value).astype(bf16), pick)

    return pl.pallas_call(
        body,
        name="positives",
        grid=(edges // chunk,),
        in_specs=[whole((dim, rows)), lanes(dim, chunk), lanes(1, chunk)],
        out_specs=[lanes(1, chunk), whole((dim, rows))],
        out_shape=[pltpu.HBM((1, edges), f32), jax.ShapeDtypeStruct((dim, rows), f32)],
        compiler_params=params(32),
        cost_estimate=cost(6 * dim * rows * edges, 8 * dim * edges),
    )(part_high, in_hbm(query), in_hbm(dst_ids))


def negative_wave(tables, chip, quota, neg_ids, query_b, lane, chunk):
    count = len(tables)
    dim, rows = tables[0].shape
    edges = query_b.shape[1]
    slots = QMAX * count
    half_weight = 0.5 / math.sqrt(NNEG)

    def body(chip_ref, lane_ref, quota_ref, *refs):
        table_refs = refs[:count]
        ids, query_ref, neg, coef_out = refs[count : count + 4]
        grad_refs = refs[count + 4 : 2 * count + 4]
        neg_t, neg_grad = refs[2 * count + 4 :]

        live, at, base = [], [], [jnp.int32(0)]
        for s in range(count):
            spot = CORES * chip_ref[0] + (lane_ref[0] + s) % CORES
            at.append(spot)
            live.append(quota_ref[0, spot])
            base.append(base[-1] + live[-1])
        total = base[-1]

        step = pl.program_id(0)

        def picks(s, wide):
            parts = [select_rows(ids[at[s], b : b + 1, :], rows) for b in range(wide)]
            return jnp.concatenate(parts, axis=1) if wide > 1 else parts[0]

        def when_live(s, wide):
            return pl.when(jnp.logical_and(live[s] == wide, step == 0))

        def when_done(s, wide):
            return pl.when(jnp.logical_and(live[s] == wide, step == pl.num_programs(0) - 1))

        for s in range(count):
            for wide in range(1, QMAX + 1):

                @when_live(s, wide)
                def _(s=s, wide=wide):
                    value = dot_nn(table_refs[s][...], picks(s, wide))
                    for b in range(wide):
                        part = value[:, b * BLOCK : (b + 1) * BLOCK]
                        neg[base[s] + b] = part.astype(bf16)
                        neg_t[base[s] + b] = part.T.astype(bf16)
                        neg_grad[base[s] + b] = jnp.zeros((dim, BLOCK), f32)

        @pl.when(jnp.logical_and(total % 2 == 1, step == 0))
        def _():
            neg[total] = jnp.zeros((dim, BLOCK), bf16)
            neg_t[total] = jnp.zeros((BLOCK, dim), bf16)
            neg_grad[total] = jnp.zeros((dim, BLOCK), f32)

        for pairs in range(1, slots // 2 + 1):

            @pl.when((total + 1) // 2 == pairs)
            def _(blocks=2 * pairs):
                query = query_ref[...]
                rows_t = jnp.concatenate([neg_t[j] for j in range(blocks)], axis=0)
                scores = dot_nn(rows_t, query)
                coef = (half_weight * jnp.tanh(0.5 * scores) + half_weight).astype(bf16)
                coef_out[: blocks * BLOCK] = coef
                added = dot_nt(query, coef)
                for j in range(blocks):
                    neg_grad[j] += added[:, j * BLOCK : (j + 1) * BLOCK]

        for p in range(slots // 2):

            @pl.when(p >= (total + 1) // 2)
            def _(p=p):
                coef_out[2 * p * BLOCK : 2 * (p + 1) * BLOCK] = jnp.zeros((2 * BLOCK, chunk), bf16)
                neg[2 * p] = jnp.zeros((dim, BLOCK), bf16)
                neg[2 * p + 1] = jnp.zeros((dim, BLOCK), bf16)

        for s in range(count):

            @when_done(s, 0)
            def _(s=s):
                grad_refs[s][...] = jnp.zeros((dim, rows), bf16)

            for wide in range(1, QMAX + 1):

                @when_done(s, wide)
                def _(s=s, wide=wide):
                    parts = [neg_grad[base[s] + b] for b in range(wide)]
                    value = jnp.concatenate(parts, axis=1) if wide > 1 else parts[0]
                    grad_refs[s][...] = dot_nt(value.astype(bf16), picks(s, wide)).astype(bf16)

    smem = pl.BlockSpec(memory_space=pltpu.SMEM)
    shard = jax.ShapeDtypeStruct((dim, rows), bf16)
    return pl.pallas_call(
        body,
        grid=(edges // chunk,),
        in_specs=[smem, smem, smem]
        + [whole((dim, rows))] * count
        + [whole(neg_ids.shape), lanes(dim, chunk)],
        out_specs=[whole((slots, dim, BLOCK)), lanes(slots * BLOCK, chunk)]
        + [whole((dim, rows))] * count,
        scratch_shapes=[
            pltpu.VMEM((slots, BLOCK, dim), bf16),
            pltpu.VMEM((slots, dim, BLOCK), f32),
        ],
        out_shape=[
            jax.ShapeDtypeStruct((slots, dim, BLOCK), bf16),
            pltpu.HBM((slots * BLOCK, edges), bf16),
        ]
        + [shard] * count,
        compiler_params=params(32),
        cost_estimate=cost(6 * dim * 1.5 * count * BLOCK * edges, 10 * dim * edges),
    )(chip, lane, quota, *tables, neg_ids, in_hbm(query_b))


def combine(
    src_rows, rel_ids, part_high, dst_ids, pos_coef, negatives, coefs, rel_count, chunk
):
    dim, edges = src_rows.shape
    rows = part_high.shape[1]
    count = len(negatives)
    slots = negatives[0].shape[0]
    sub = min(SUB, chunk)

    def body(rows_in, rel, table, dst, pos, *refs):
        neg_refs, coef_refs = refs[:count], refs[count : 2 * count]
        grad_out, rel_out, all_neg = refs[2 * count :]

        @pl.when(pl.program_id(0) == 0)
        def _():
            rel_out[...] = jnp.zeros_like(rel_out)
            for k in range(count):
                for j in range(slots):
                    all_neg[k, :, j * BLOCK : (j + 1) * BLOCK] = neg_refs[k][j]

        found = None
        for h in range(chunk // sub):
            part = slice(h * sub, (h + 1) * sub)
            grad = pos[:, part] * dot_nn(table[...], select_rows(dst[:, part], rows))
            for k in range(count):
                grad = grad + dot_nn(all_neg[k], coef_refs[k][:, part])
            grad_out[:, part] = grad.astype(bf16)
            kinds = select_rows(rel[:, part], rel_count)
            upper, lower = split2(back(grad, rows_in[:, part]))
            more = dot_nt(kinds, upper) + dot_nt(kinds, lower)
            found = more if found is None else found + more
        rel_out[...] += found

    return pl.pallas_call(
        body,
        name="combine",
        grid=(edges // chunk,),
        in_specs=[lanes(dim, chunk), lanes(1, chunk)]
        + [whole((dim, rows)), lanes(1, chunk), lanes(1, chunk)]
        + [whole(negatives[0].shape)] * count
        + [lanes(slots * BLOCK, chunk)] * count,
        out_specs=[lanes(dim, chunk), whole((rel_count, dim))],
        out_shape=[
            pltpu.HBM((dim, edges), bf16),
            jax.ShapeDtypeStruct((rel_count, dim), f32),
        ],
        scratch_shapes=[pltpu.VMEM((count, dim, slots * BLOCK), bf16)],
        compiler_params=params(48),
        cost_estimate=cost(2 * dim * NNEG * edges, 12 * dim * edges + 2 * NNEG * edges),
    )(
        in_hbm(src_rows),
        in_hbm(rel_ids),
        part_high,
        in_hbm(dst_ids),
        in_hbm(pos_coef),
        *negatives,
        *map(in_hbm, coefs),
    )


def source_side(src_table, src_state, rel_parts, src_ids, rel_ids, query_grad, rel_count, chunk):
    dim, rows = src_table.shape
    edges = src_ids.shape[1]
    sub = min(SUB, chunk)

    def body(table, state, parts, src, rel, grad_in, out, state_out, acc):
        step = pl.program_id(0)

        @pl.when(step == 0)
        def _():
            acc[...] = jnp.zeros_like(acc)

        found = None
        for h in range(chunk // sub):
            part = slice(h * sub, (h + 1) * sub)
            pick = select_rows(src[:, part], rows)
            rel_rows = relation_rows(parts[...], rel[:, part], rel_count)
            term = back(grad_in[:, part].astype(f32), rel_rows).astype(bf16)
            more = dot_nt(term, pick)
            found = more if found is None else found + more
        acc[...] += found

        @pl.when(step == pl.num_programs(0) - 1)
        def _():
            total = acc[...]
            new_state = state[...] + jnp.sum(total * total, axis=0, keepdims=True) / dim
            state_out[...] = new_state
            out[...] = table[...] - LEARN_RATE * total / jnp.sqrt(new_state)

    return pl.pallas_call(
        body,
        name="source_side",
        grid=(edges // chunk,),
        in_specs=[
            whole((dim, rows)),
            whole((1, rows)),
            whole(rel_parts.shape),
            lanes(1, chunk),
            lanes(1, chunk),
            lanes(dim, chunk),
        ],
        out_specs=[whole((dim, rows)), whole((1, rows))],
        out_shape=[
            jax.ShapeDtypeStruct((dim, rows), f32),
            jax.ShapeDtypeStruct((1, rows), f32),
        ],
        scratch_shapes=[pltpu.VMEM((dim, rows), f32)],
        compiler_params=params(24),
        cost_estimate=cost(4 * dim * rows * edges, 4 * dim * edges),
    )(
        in_hbm(src_table),
        in_hbm(src_state),
        rel_parts,
        in_hbm(src_ids),
        in_hbm(rel_ids),
        in_hbm(query_grad),
    )


def destination_side(high, low_state, own_grad, grads):
    dim, rows = own_grad.shape
    count = len(grads)

    def body(*refs):
        high_ref, low_ref, own_ref = refs[:3]
        out, state_out = refs[3 + count :]
        total = own_ref[...]
        for ref in refs[3 : 3 + count]:
            total = total + ref[...].astype(f32)
        packed = low_ref[...].astype(f32)
        state = packed[dim : dim + 1] + packed[dim + 1 : dim + 2] + packed[dim + 2 : dim + 3]
        new_state = state + jnp.sum(total * total, axis=0, keepdims=True) / dim
        state_out[...] = new_state
        table = high_ref[...].astype(f32) + packed[:dim]
        out[...] = table - LEARN_RATE * total / jnp.sqrt(new_state)

    width = min(rows, 128)

    operands = [high, low_state, own_grad, *grads]
    return pl.pallas_call(
        body,
        name="destination_side",
        grid=(rows // width,),
        in_specs=[lanes(array.shape[0], width) for array in operands],
        out_specs=[lanes(dim, width), lanes(1, width)],
        out_shape=[
            jax.ShapeDtypeStruct((dim, rows), f32),
            jax.ShapeDtypeStruct((1, rows), f32),
        ],
        compiler_params=params(16),
        cost_estimate=cost(8 * dim * rows, (12 + 2 * count) * dim * rows),
    )(*operands)


def split_table(table, state):
    dim, rows = table.shape
    half = rows // 2
    tail = 16

    def body(table_ref, state_ref, left, right, rest):
        value = table_ref[...]
        high, low = split2(value)
        left[...] = high[:, :half]
        right[...] = high[:, half:]
        rest[:dim] = low
        first, _ = split2(state_ref[...])
        left_over = state_ref[...] - first.astype(f32)
        second, third = split2(left_over)
        parts = [first.astype(f32), second.astype(f32), third.astype(f32)]
        parts.append(jnp.zeros((tail - 3, rows), f32))
        rest[dim:] = jnp.concatenate(parts, axis=0).astype(bf16)

    return pl.pallas_call(
        body,
        name="split_table",
        grid=(1,),
        in_specs=[whole((dim, rows)), whole((1, rows))],
        out_specs=[whole((dim, half)), whole((dim, rows - half)), whole((dim + tail, rows))],
        out_shape=[
            jax.ShapeDtypeStruct((dim, half), bf16),
            jax.ShapeDtypeStruct((dim, rows - half), bf16),
            jax.ShapeDtypeStruct((dim + tail, rows), bf16),
        ],
        compiler_params=params(16),
        cost_estimate=cost(4 * dim * rows, 8 * dim * rows),
    )(in_hbm(table), in_hbm(state))


def grid_of(count):
    across = math.isqrt(count)
    while count % across:
        across -= 1
    return count // across, across


def moved(device, n, stride, shift):
    place = (device // stride) % n
    return device + ((place + shift) % n - place) * stride


def shifted(array, n, stride, shift):
    count = lax.axis_size("dom")
    return lax.ppermute(array, "dom", [(d, moved(d, n, stride, shift)) for d in range(count)])


def copy_chosen(index, options, out, columns):
    for k in range(len(options)):

        @pl.when(index == k)
        def _(k=k):
            out[:, columns] = options[k][...]


def route(values, matching, here):
    down, across = grid_of(lax.axis_size("dom"))
    axes = [(across, 1), (down, across)]
    orders = [axes, axes[::-1]][: len(values)]
    rows = values[0].shape[0]
    widths = [value.shape[1] for value in values]
    starts = [sum(widths[:i]) for i in range(len(widths))]
    vmem = pl.BlockSpec(memory_space=pltpu.VMEM)
    smem = pl.BlockSpec(memory_space=pltpu.SMEM)

    held = []
    for i, ((n1, stride1), _) in enumerate(orders):
        held.append([values[i]] + [shifted(values[i], n1, stride1, k) for k in range(1, n1)])
    flat = [array for group in held for array in group]

    def grouped(refs, groups):
        result, used = [], 0
        for group in groups:
            result.append(refs[used : used + len(group)])
            used += len(group)
        return result, refs[used:]

    def behind(place, source, n, stride):
        return ((place // stride) % n - (source // stride) % n + n) % n

    def pass_on(match_ref, here_ref, *refs):
        place = here_ref[0]
        held_refs, outs = grouped(refs, held)
        used = 0
        for i, ((n1, stride1), (n2, stride2)) in enumerate(orders):
            for m in range(1, n2):
                source = match_ref[moved(place, n2, stride2, m)]
                picked = behind(place, source, n1, stride1)
                copy_chosen(picked, held_refs[i], outs[used], slice(None))
                used += 1

    hops = [(i, m) for i in range(len(orders)) for m in range(1, orders[i][1][0])]
    passed = pl.pallas_call(
        pass_on,
        in_specs=[smem, smem] + [vmem] * len(flat),
        out_specs=[vmem] * len(hops),
        out_shape=[jax.ShapeDtypeStruct((rows, widths[i]), bf16) for i, _ in hops],
        compiler_params=pltpu.CompilerParams(vmem_limit_bytes=16 * MIB),
        cost_estimate=cost(0, 4 * rows * sum(widths)),
    )(matching, here, *flat)
    found = [[] for _ in orders]
    for (i, m), array in zip(hops, passed):
        found[i].append(shifted(array, *orders[i][1], m))
    flat_found = [array for group in found for array in group]

    def merge(match_ref, here_ref, *refs):
        place = here_ref[0]
        held_refs, rest = grouped(refs, held)
        found_refs, (out,) = grouped(rest, found)
        source = match_ref[place]
        for i, ((n1, stride1), (n2, stride2)) in enumerate(orders):
            columns = slice(starts[i], starts[i] + widths[i])
            near = behind(place, source, n1, stride1)
            far = behind(place, source, n2, stride2)
            index = jnp.where(far == 0, near, n1 - 1 + far)
            copy_chosen(index, list(held_refs[i]) + list(found_refs[i]), out, columns)

    return pl.pallas_call(
        merge,
        in_specs=[smem, smem] + [vmem] * (len(flat) + len(flat_found)),
        out_specs=vmem,
        out_shape=jax.ShapeDtypeStruct((rows, sum(widths)), bf16),
        compiler_params=pltpu.CompilerParams(vmem_limit_bytes=24 * MIB),
        cost_estimate=cost(0, 4 * rows * sum(widths)),
    )(matching, here, *flat, *flat_found)


def total_of_peers(value, axis, stride, n):
    count = lax.axis_size(axis)

    def peer(i, k):
        digit = (i // stride) % n
        return i + ((digit ^ k) - digit) * stride

    terms = [value]
    for k in range(1, n):
        terms.append(lax.ppermute(value, axis, [(i, peer(i, k)) for i in range(count)]))
    while len(terms) > 1:
        terms = [terms[i] + terms[i + 1] for i in range(0, len(terms), 2)]
    return terms[0]


def total_over_mesh(value):
    down, across = grid_of(lax.axis_size("dom"))
    value = total_of_peers(value, "edge", 1, CORES)
    value = total_of_peers(value, "edge", CORES, lax.axis_size("edge") // CORES)
    if down * across <= 4:
        return total_of_peers(value, "dom", 1, down * across)
    value = total_of_peers(value, "dom", 1, across)
    return total_of_peers(value, "dom", across, down)


def shards(
    src_table,
    src_state,
    dst_table,
    dst_state,
    relation,
    edge_src,
    edge_dst,
    edge_rel,
    matching,
    neg_rows,
    quotas,
):
    edge_count = lax.axis_size("edge")
    chips = edge_count // CORES
    _, row_count = src_table.shape
    rel_count = relation.shape[1]
    edges = edge_src.shape[0]
    chunk = min(edges, 1024)
    wave_chunk = min(edges, 2048)
    here = lax.axis_index("edge").reshape(1).astype(jnp.int32)
    place = lax.axis_index("dom").reshape(1).astype(jnp.int32)

    src_ids = edge_src.reshape(1, edges)
    dst_ids = edge_dst.reshape(1, edges)
    rel_ids = edge_rel.reshape(1, edges)
    neg_ids = neg_rows.reshape(edge_count, QMAX, BLOCK)
    rel_parts = split_relation(relation)

    left, right, rest = split_table(dst_table, dst_state.reshape(1, row_count))
    part_high = route([left, right], matching, place)
    rest, part_high = lax.optimization_barrier((rest, part_high))
    low_state = route([rest], matching, place)

    made = []
    for part in range(2):
        made = make_queries(
            src_table, rel_parts, src_ids, rel_ids, rel_count, min(chunk, edges // 2), part, 2, made
        )
    query, query_b, src_rows = made
    pos_coef, own_grad = positives(part_high, query, dst_ids, chunk)

    swap = [(i, i ^ 1) for i in range(edge_count)]

    def swapped(array):
        return lax.ppermute(array, "edge", swap)

    chip = here // CORES
    lane = here % CORES
    arrived, negatives, coefs = [], [], []
    done, brought = [own_grad], {}
    for k in range(chips):
        pairs = [(i, i ^ (CORES * k)) for i in range(edge_count)]
        near = k & -k
        table = brought.get(k - near, part_high)
        if k:
            if k == near >= 2:
                table, _ = lax.optimization_barrier((table, done[k // 2 - 1]))
            hop = [(i, i ^ (CORES * near)) for i in range(edge_count)]
            table = lax.ppermute(table, "edge", hop)
        brought[k] = table
        live, coef, mine, theirs = negative_wave(
            [table, swapped(table)], chip ^ k, quotas, neg_ids, query_b, lane, wave_chunk
        )
        total = mine.astype(f32) + swapped(theirs).astype(f32)
        if k:
            total = lax.ppermute(total.astype(bf16), "edge", pairs)
        arrived.append(total)
        done.append(mine)
        negatives.append(live)
        coefs.append(coef)

    query_grad, rel_grad = combine(
        src_rows,
        rel_ids,
        part_high,
        dst_ids,
        pos_coef,
        negatives,
        coefs,
        rel_count,
        chunk,
    )
    src_out, src_state_out = source_side(
        src_table,
        src_state.reshape(1, row_count),
        rel_parts,
        src_ids,
        rel_ids,
        query_grad,
        rel_count,
        chunk,
    )
    relation_out = relation - REL_RATE * total_over_mesh(rel_grad).T
    dst_out, dst_state_out = destination_side(part_high, low_state, own_grad, arrived)
    return (
        src_out,
        src_state_out.reshape(row_count),
        dst_out,
        dst_state_out.reshape(row_count),
        relation_out,
    )


def solution(mesh):
    in_specs = (
        P(None, ("dom", "edge")),
        P(("dom", "edge")),
        P(None, ("dom", "edge")),
        P(("dom", "edge")),
        P(),
        P(("dom", "edge")),
        P(("dom", "edge")),
        P(("dom", "edge")),
        P(),
        P(("dom", "edge"), None, None),
        P(("dom", "edge"), None),
    )
    out_specs = (
        P(None, ("dom", "edge")),
        P(("dom", "edge")),
        P(None, ("dom", "edge")),
        P(("dom", "edge")),
        P(),
    )

    return jax.shard_map(shards, mesh=mesh, in_specs=in_specs, out_specs=out_specs, check_vma=False)
```
